128 devices in a mesh: gx: 64 (over x, y, z), gy: 2 (over core).
Axes of the slice: x: 4, y: 4, z: 4, core: 2. Of those that a mesh axis runs over, the one named last changes fastest.
Arguments:
- operator: float32 [243, 131072], P(None, ('gx', 'gy')), may hold values from -0.6 to 10.6
- basis_u: float32 [144, 131072], P(None, ('gx', 'gy')), may hold values from -6 to 6
- basis_c: float32 [144, 131072], P(None, ('gx', 'gy')), may hold values from -6 to 6
- right_side: float32 [3, 131072], P(None, ('gx', 'gy')), may hold values from -16 to 16
- new_rows: int32 [131072], P(('gx', 'gy')), may hold values from 0 to 131071, as said below
Outputs:
- solution: float32 [3, 131072], P(None, ('gx', 'gy'))
- residual: float32 [3, 131072], P(None, ('gx', 'gy'))
The draws below stay inside these ranges and needn't reach their ends.
Inputs may be any that keep to these rules, and one draw needn't show every extreme that they name: `new_rows`: each block row gets one new index (a permutation). Each device sends 0 to 16 of its old rows to each device, and each device both sends exactly 16 rows to some peer and receives exactly 16 rows from some peer.
All inputs are finite; a program needn't handle non-finite values.
Results may differ from the reference program's by a relative error of at most 0.0003.
Values sent between devices are 32-bit elements; how exact they have to be, the bound alone decides.
No kernel may reach another device: no remote copies, remote signals or barrier semaphores. Data moves between devices by JAX's collectives and lax.ppermute only.
A program may use at most 64 MiB of HBM per device.

```python
import jax
import jax.numpy as jnp
from jax import lax

CX = 1
CY = 8
CZ = 128
K = 48
ROWS_DEV = 1024
PEERS = 128
ROWS = 131072
N_GX = 64
N_GY = 2


def c_values(key):
    values = jnp.clip(jax.random.normal(jax.random.fold_in(key, 11), (3 * K, ROWS), jnp.float32), -6.0, 6.0)
    return values


def draw_basis_c(key, part):
    return c_values(key)


def draw_right_side(key, part):
    values = c_values(key).reshape(3, K, ROWS)
    weights = jax.random.normal(jax.random.fold_in(key, 13), (K,), jnp.float32) / jnp.sqrt(1.0 * K)
    along = jnp.einsum('amp,m->ap', values, weights)
    owner = (draw_new_rows(key, part) // ROWS_DEV).astype(jnp.float32)
    place = owner / (1.0 * (PEERS - 1))
    noise = jax.random.normal(jax.random.fold_in(key, 12), (3, ROWS), jnp.float32)
    rising = 1.0 + 4.0 * place
    return jnp.clip(noise * rising[None, :] + along, -16.0, 16.0)


def draw_operator(key, part):
    off = jnp.clip(0.1 * jax.random.normal(jax.random.fold_in(key, 21), (27, 3, 3, ROWS), jnp.float32), -0.6, 0.6)
    diag = 6.0 + 4.0 * jax.random.uniform(jax.random.fold_in(key, 22), (3, ROWS), jnp.float32)
    eye = jnp.eye(3, dtype=jnp.float32)
    off = off.at[13].add(eye[:, :, None] * diag[:, None, :])
    return off.reshape(243, ROWS)


def draw_new_rows(key, part):
    peers = PEERS
    rows = ROWS_DEV
    base = rows // peers
    half = jax.random.randint(jax.random.fold_in(key, 31), (peers // 2,), -base, base + 1)
    half = half.at[0].set(base)
    sizes = base + jnp.concatenate([half, -half])
    sigma = jax.random.permutation(jax.random.fold_in(key, 32), peers)
    tau = jax.random.permutation(jax.random.fold_in(key, 33), peers)
    counts = sizes[(sigma[:, None] + tau[None, :]) % peers]
    offsets = jnp.cumsum(counts, 0) - counts
    ends = jnp.cumsum(counts, 1)
    starts = ends - counts
    keys = jax.random.split(jax.random.fold_in(key, 34), peers)
    orders = jax.vmap(lambda k: jax.random.permutation(k, rows))(keys)
    places = jnp.arange(rows, dtype=jnp.int32)

    def one_source(order, end_row, start_row, offset_row):
        target = jnp.searchsorted(end_row, places, side='right').astype(jnp.int32)
        newer = target * rows + offset_row[target] + places - start_row[target]
        return jnp.zeros((rows,), jnp.int32).at[order].set(newer.astype(jnp.int32))
    table = jax.vmap(one_source)(orders, ends, starts, offsets)
    return table.reshape(peers * rows).astype(jnp.int32)


def level_of(key, extent, shards, smallest, high):
    loudness = 1.0
    for dim, blocks in shards:
        draws = jax.random.uniform(jax.random.fold_in(jax.random.fold_in(key, 6), dim), (blocks,), jnp.float32, smallest / len(shards), high / len(shards))
        loudness = loudness * jnp.repeat(jnp.exp(draws), extent[dim] // blocks).reshape((-1,) + (1,) * (len(extent) - 1 - dim))
    return loudness


def gaussian(key, shape, scale, reach, cuts=(), kind=jnp.bfloat16):
    result = jax.random.normal(key, shape, jnp.float32) * scale
    if len(cuts) > 0:
        result = level_of(key, shape, cuts, -0.22, 0.18) * result
    return jnp.clip(result, min=-reach, max=reach).astype(kind)


def setup_inputs(seed: int = 0) -> dict:
    key_of = jax.random.split(jax.random.key(seed), 6)
    return {
        "operator": draw_operator(jax.random.fold_in(key_of[5], 71), 0),
        "basis_u": gaussian(key_of[1], (3 * K, ROWS), 1.0, 6.0, ((1, 128),), jnp.float32),
        "basis_c": draw_basis_c(jax.random.fold_in(key_of[5], 71), 0),
        "right_side": draw_right_side(jax.random.fold_in(key_of[5], 71), 0),
        "new_rows": draw_new_rows(jax.random.fold_in(key_of[5], 71), 0),
    }


def to_grid(values):
    width = values.shape[0]
    shaped = values.reshape(width, N_GX, N_GY, CX, CY, CZ).transpose(0, 1, 3, 2, 4, 5)
    return shaped.reshape(width, N_GX * CX, N_GY * CY, CZ)

def to_rows(grid):
    width = grid.shape[0]
    shaped = grid.reshape(width, N_GX, CX, N_GY, CY, CZ).transpose(0, 1, 3, 2, 4, 5)
    return shaped.reshape(width, ROWS)

def stencil(coef, padded):
    size_x = padded.shape[1] - 2
    size_y = padded.shape[2] - 2
    size_z = padded.shape[3] - 2
    total = jnp.zeros((3, size_x, size_y, size_z), jnp.float32)
    for k in range(27):
        dx, dy, dz = (k // 9, k // 3 % 3, k % 3)
        moved = padded[:, dx:dx + size_x, dy:dy + size_y, dz:dz + size_z]
        total = total + lax.optimization_barrier(jnp.sum(coef[k] * moved[None], axis=1))
    return total

def apply_op(coef, vector):
    padded = jnp.pad(to_grid(vector), ((0, 0), (1, 1), (1, 1), (1, 1)))
    return to_rows(stencil(coef, padded))

def project(basis, vector):
    return jnp.einsum('amp,ap->m', basis, vector, precision=lax.Precision.HIGHEST)

def combine(basis, coeffs):
    return jnp.einsum('amp,m->ap', basis, coeffs, precision=lax.Precision.HIGHEST)

def reference(operator, basis_u, basis_c, right_side, new_rows):
    payload = jnp.concatenate([operator, basis_u, basis_c, right_side], 0)
    moved = jnp.zeros_like(payload).at[:, new_rows].set(payload)
    coef = to_grid(moved[:243]).reshape(27, 3, 3, N_GX * CX, N_GY * CY, CZ)
    u = moved[243:243 + 3 * K].reshape(3, K, ROWS)
    c = moved[243 + 3 * K:243 + 6 * K].reshape(3, K, ROWS)
    b = moved[243 + 6 * K:]
    gram = jnp.einsum('amp,anp->mn', c, c, precision=lax.Precision.HIGHEST)
    lower = jnp.linalg.cholesky(gram)
    lower_inv = jax.scipy.linalg.solve_triangular(lower, jnp.eye(K, dtype=jnp.float32), lower=True)
    cq = jnp.einsum('mn,anp->amp', lower_inv, c, precision=lax.Precision.HIGHEST)
    uq = jnp.einsum('mn,anp->amp', lower_inv, u, precision=lax.Precision.HIGHEST)
    start = project(cq, b)
    first_x = combine(uq, start)
    first_r = b - combine(cq, start)
    beta = jnp.sqrt(jnp.sum(first_r * first_r))
    vec_one = first_r / beta
    image = apply_op(coef, vec_one)
    proj_one = project(cq, image)
    h11 = jnp.sum(vec_one * image)
    rest = image - combine(cq, proj_one) - h11 * vec_one
    h21 = jnp.sqrt(jnp.sum(rest * rest))
    vec_two = rest / h21
    image = apply_op(coef, vec_two)
    proj_two = project(cq, image)
    h12 = jnp.sum(vec_one * image)
    h22 = jnp.sum(vec_two * image)
    rest = image - combine(cq, proj_two) - h12 * vec_one - h22 * vec_two
    h32 = jnp.sqrt(jnp.sum(rest * rest))
    m11 = h11 * h11 + h21 * h21
    m12 = h11 * h12 + h21 * h22
    m22 = h12 * h12 + h22 * h22 + h32 * h32
    g_one = beta * h11
    g_two = beta * h12
    determ = m11 * m22 - m12 * m12
    y_one = (m22 * g_one - m12 * g_two) / determ
    y_two = (m11 * g_two - m12 * g_one) / determ
    solution = first_x + y_one * vec_one + y_two * vec_two - combine(uq, y_one * proj_one + y_two * proj_two)
    residual = b - apply_op(coef, solution)
    return (solution, residual)
```

```python
import functools

import jax
import jax.numpy as jnp
from jax import lax
from jax.experimental import pallas as pl
from jax.experimental.pallas import tpu as pltpu
from jax.sharding import Mesh
from jax.sharding import PartitionSpec as P

CY = 8
CZ = 128
K = 48
SLOTS = 16
PEERS = 128
ROWS = 1024
N_GX = 64
GX_GY = ("gx_0", "gx_1", "gx_2", "gy")
GX = ("gx_0", "gx_1", "gx_2")
F32 = jnp.float32
BF16 = jnp.bfloat16
HIGHEST = lax.Precision.HIGHEST
WIRE = 50
NT = (((1,), (1,)), ((), ()))
TN = (((0,), (0,)), ((), ()))
MAIN = 3 * 128


def split(x):
    high = x.astype(BF16)
    return high, (x - high.astype(F32)).astype(BF16)


def exact_dot(x, y, dims=(((1,), (0,)), ((), ()))):
    return lax.dot_general(x, y, dims, precision=HIGHEST, preferred_element_type=F32)


def half_sum(x):
    return x[:, :128] + x[:, 128:]


def pack_kernel(op_ref, c_ref, b_ref, rows_ref, wire_ref, info_ref, s_ref, p_ref, a_ref):
    new_rows = rows_ref[...]
    target = new_rows // ROWS
    local = new_rows % ROWS
    onehot = lax.broadcasted_iota(jnp.int32, (PEERS, ROWS), 0) == target
    onehot_f = jnp.where(onehot, 1.0, 0.0).astype(F32)
    onehot_b = onehot_f.astype(BF16)
    before = lax.broadcasted_iota(jnp.int32, (128, 128), 0) < lax.broadcasted_iota(jnp.int32, (128, 128), 1)
    before = jnp.where(before, 1.0, 0.0).astype(BF16)
    ones = jnp.ones((128, 128), BF16)
    seen = jnp.zeros((PEERS, 128), F32)
    ranks = []
    for block in range(ROWS // 128):
        part = onehot_b[:, block * 128 : (block + 1) * 128]
        count = jnp.dot(part, before, preferred_element_type=F32) + seen
        ranks.append(jnp.sum(onehot_f[:, block * 128 : (block + 1) * 128] * count, axis=0, keepdims=True))
        seen = seen + jnp.dot(part, ones, preferred_element_type=F32)
    rank = jnp.concatenate(ranks, axis=1)
    rank_at = jnp.where(onehot, rank, -1.0)
    for k in range(SLOTS):
        s_ref[k * PEERS : (k + 1) * PEERS, :] = jnp.where(rank_at == k, 1.0, 0.0).astype(BF16)
    info_ref[0:1, :] = target
    info_ref[1:2, :] = rank.astype(jnp.int32)
    info_ref[2:3, :] = local
    info_ref[3:8, :] = jnp.zeros((5, ROWS), jnp.int32)

    def put(tile, start, x):
        high, low = split(x)
        p_ref[tile * 256 + start : tile * 256 + start + x.shape[0], :] = high
        p_ref[tile * 256 + 128 + start : tile * 256 + 128 + start + x.shape[0], :] = low

    put(0, 0, c_ref[0:128, :])
    put(1, 0, c_ref[128:144, :])
    put(1, 16, op_ref[0:112, :])
    put(2, 0, op_ref[112:240, :])
    for tile in range(3):
        moved = lax.dot_general(
            s_ref[...], p_ref[tile * 256 : (tile + 1) * 256, :], NT, preferred_element_type=F32
        )
        for k in range(SLOTS):
            wire_ref[pl.ds(tile * SLOTS + k, PEERS, stride=WIRE), :] = half_sum(moved[k * PEERS : (k + 1) * PEERS])

    at_rank = lax.broadcasted_iota(jnp.int32, (SLOTS, ROWS), 0).astype(F32) == rank
    rest = [op_ref[240 + i : 241 + i, :] for i in range(3)] + [b_ref[i : i + 1, :] for i in range(3)]
    rest = [jnp.where(at_rank, row, 0.0) for row in rest + [local.astype(F32)]]
    rest = jnp.concatenate(rest + [jnp.zeros((SLOTS, ROWS), F32)], axis=0)
    rest = jnp.concatenate(split(rest), axis=0)
    wire_ref[pl.ds(48, PEERS, stride=WIRE), :] = half_sum(
        lax.dot_general(onehot_b, rest, NT, preferred_element_type=F32)
    )

    gram = jnp.zeros((64, 128), F32)
    a_ref[48:128, :] = jnp.zeros((80, ROWS), F32)
    for a in range(3):
        a_ref[0:48, :] = c_ref[a * K : (a + 1) * K, :]
        a_ref[48:49, :] = b_ref[a : a + 1, :]
        gram = gram + exact_dot(a_ref[0:64, :], a_ref[...], NT)
    wire_ref[pl.ds(49, PEERS, stride=WIRE), :] = jnp.concatenate([gram, jnp.zeros((64, 128), F32)], axis=0)


def two_level(values, labels, left_ref, right_ref):
    count = len(values)
    eight = lax.broadcasted_iota(jnp.int32, (CY, 128), 0)
    lanes = lax.broadcasted_iota(jnp.int32, (128, 128), 0)
    for k in range(SLOTS):
        label = labels[k].astype(jnp.int32)
        y, z = label // CZ, label % CZ
        cols = slice(k * 128, (k + 1) * 128)
        right_ref[:, cols] = jnp.where(lanes == z, 1.0, 0.0).astype(BF16)
        here = eight == y
        for c in range(count):
            left_ref[c * CY : (c + 1) * CY, cols] = jnp.where(here, values[c][k], 0.0)
    high, low = split(left_ref[0 : count * CY, :])
    right = right_ref[...]
    return lax.dot_general(high, right, NT, preferred_element_type=F32) + lax.dot_general(
        low, right, NT, preferred_element_type=F32
    )


def unpack_kernel(wire_ref, main_ref, ext_ref, t_ref, r_ref, left_ref, right_ref):
    rest = wire_ref[pl.ds(48, PEERS, stride=WIRE), :].T
    labels = [rest[6 * SLOTS + k : 6 * SLOTS + k + 1, :] for k in range(SLOTS)]
    node = lax.broadcasted_iota(jnp.int32, (ROWS, 128), 0).astype(F32)
    for k in range(SLOTS):
        t_ref[:, k * 128 : (k + 1) * 128] = jnp.where(node == labels[k], 1.0, 0.0).astype(BF16)
    for tile in range(3):
        for k in range(SLOTS):
            high, low = split(wire_ref[pl.ds(tile * SLOTS + k, PEERS, stride=WIRE), :])
            r_ref[k * 128 : (k + 1) * 128, 0:128] = high
            r_ref[k * 128 : (k + 1) * 128, 128:256] = low
        moved = jnp.dot(t_ref[...], r_ref[...], preferred_element_type=F32)
        for y in range(CY):
            block = half_sum(moved[y * CZ : (y + 1) * CZ])
            main_ref[pl.ds(tile * 128 * CY + y, 128, stride=CY), :] = block.T
    values = [[rest[f * SLOTS + k : f * SLOTS + k + 1, :] for k in range(SLOTS)] for f in range(6)]
    ext_ref[...] = two_level(values, labels, left_ref, right_ref)


def minus_combined(start, main_ref, weights):
    result = []
    for a in range(3):
        total = start[a]
        for m in range(K):
            row = (a * K + m) * CY
            total = total - main_ref[row : row + CY, :] * weights[m : m + 1, :]
        result.append(total)
    return result


def put_vector(vector, side_ref, v_ref, line_ref):
    lower = side_ref[0] == 0
    line_ref[...] = jnp.zeros((8, 128), F32)
    for a in range(3):
        v_ref[a * CY : (a + 1) * CY, :] = vector[a]
        line_ref[a : a + 1, :] = jnp.where(lower, vector[a][7:8, :], vector[a][0:1, :])


def first_kernel(side_ref, gram_ref, main_ref, ext_ref, v_ref, line_ref, inv_ref, start_ref, beta_ref):
    rows = gram_ref[0:48, :]
    row_id = lax.broadcasted_iota(jnp.int32, (K, 128), 0)
    lane = lax.broadcasted_iota(jnp.int32, (K, 128), 1)
    work = jnp.where(lane < K + 1, rows, jnp.where(lane - 64 == row_id, 1.0, 0.0))
    for j in range(K - 1):
        pivot = work[j : j + 1, :]
        scale = jnp.where(row_id > j, work[:, j : j + 1], 0.0) * (1.0 / work[j : j + 1, j : j + 1])
        work = work - scale * pivot
    diagonal = jnp.sum(jnp.where(lane == row_id, work, 0.0), axis=1, keepdims=True)
    work = work * (1.0 / jnp.sqrt(diagonal))
    start = jnp.broadcast_to(work[:, K : K + 1], (K, 128))
    inverse = jnp.where(lane < K, pltpu.roll(work, 64, 1), 0.0)
    inv_ref[...] = inverse
    start_ref[...] = start
    weights = exact_dot(inverse, start, TN)
    load_sq = jnp.broadcast_to(gram_ref[48:49, 48:49], (1, 128))
    beta = jnp.sqrt(load_sq - jnp.sum(start * start, axis=0, keepdims=True))
    beta_ref[...] = jnp.broadcast_to(beta, (8, 128))
    load = [ext_ref[24 + a * CY : 24 + (a + 1) * CY, :] for a in range(3)]
    vector = minus_combined(load, main_ref, weights)
    put_vector([v / beta for v in vector], side_ref, v_ref, line_ref)


def put_plane(pad_ref, dx, plane, line, side):
    for a in range(3):
        base = (dx * 3 + a) * 24
        edge = line[a : a + 1, :]
        pad_ref[base + 7 : base + 8, :] = jnp.where(side == 1, edge, 0.0)
        pad_ref[base + 8 : base + 16, :] = plane[a * CY : (a + 1) * CY, :]
        pad_ref[base + 16 : base + 17, :] = jnp.where(side == 0, edge, 0.0)


def stencil(main_ref, ext_ref, pad_ref):
    lane = lax.broadcasted_iota(jnp.int32, (CY, 128), 1)
    total = [jnp.zeros((CY, 128), F32) for _ in range(3)]
    for dx in range(3):
        for dy in range(3):
            for b in range(3):
                start = (dx * 3 + b) * 24 + 7 + dy
                here = pad_ref[start : start + CY, :]
                left = jnp.where(lane == 0, 0.0, pltpu.roll(here, 1, 1))
                right = jnp.where(lane == 127, 0.0, pltpu.roll(here, 127, 1))
                for dz, moved in enumerate((left, here, right)):
                    for a in range(3):
                        q = ((dx * 9 + dy * 3 + dz) * 3 + a) * 3 + b
                        if q < 240:
                            row = (3 * K + q) * CY
                            total[a] = total[a] + main_ref[row : row + CY, :] * moved
                        else:
                            row = (q - 240) * CY
                            total[a] = total[a] + ext_ref[row : row + CY, :] * moved
    return total


def image_kernel(count, side_ref, main_ref, ext_ref, line_ref, up_ref, down_ref, *refs):
    vectors, (image_ref, send_ref, pad_ref, part_ref) = refs[:count], refs[count:]
    side = side_ref[0]
    put_plane(pad_ref, 0, up_ref[0:24, :], up_ref[24:32, :], side)
    put_plane(pad_ref, 1, vectors[-1][...], line_ref[...], side)
    put_plane(pad_ref, 2, down_ref[0:24, :], down_ref[24:32, :], side)
    image = stencil(main_ref, ext_ref, pad_ref)
    for a in range(3):
        image_ref[a * CY : (a + 1) * CY, :] = image[a]
    for m in range(K):
        rows = [(a * K + m) * CY for a in range(3)]
        part_ref[m * CY : (m + 1) * CY, :] = sum(
            main_ref[row : row + CY, :] * image[a] for a, row in enumerate(rows)
        )
    others = [image] + [[ref[a * CY : (a + 1) * CY, :] for a in range(3)] for ref in vectors]
    for i in range(8):
        m = K + i
        if i < len(others):
            part_ref[m * CY : (m + 1) * CY, :] = sum(o * w for o, w in zip(others[i], image))
        else:
            part_ref[m * CY : (m + 1) * CY, :] = jnp.zeros((CY, 128), F32)
    part = sum(part_ref[pl.ds(y, K + 8, stride=CY), :] for y in range(CY))
    part = jnp.concatenate([part, jnp.zeros((128 - K - 8, 128), F32)], axis=0)
    send_ref[...] = exact_dot(jnp.ones((PEERS, 128), F32), part, NT)


def totals(got_ref):
    return exact_dot(got_ref[...], jnp.ones((PEERS, 128), F32), TN)


def next_kernel(side_ref, got_ref, main_ref, image_ref, one_ref, inv_ref, v_ref, line_ref, proj_ref, h_ref):
    sums = totals(got_ref)
    inverse = inv_ref[...]
    projection = exact_dot(inverse, sums)
    h11 = sums[K + 1 : K + 2, :]
    h21 = jnp.sqrt(sums[K : K + 1, :] - jnp.sum(projection * projection, axis=0, keepdims=True) - h11 * h11)
    weights = exact_dot(inverse, projection, TN)
    begin = [
        image_ref[a * CY : (a + 1) * CY, :] - h11 * one_ref[a * CY : (a + 1) * CY, :] for a in range(3)
    ]
    vector = minus_combined(begin, main_ref, weights)
    put_vector([v / h21 for v in vector], side_ref, v_ref, line_ref)
    proj_ref[...] = projection
    h_ref[...] = jnp.zeros((8, 128), F32)
    h_ref[0:1, :] = h11
    h_ref[1:2, :] = h21


def send_kernel(got_ref, inv_ref, start_ref, proj_ref, h_ref, beta_ref, u_ref, info_ref, wire_ref, y_ref):
    sums = totals(got_ref)
    inverse = inv_ref[...]
    proj_two = exact_dot(inverse, sums)
    h11, h21 = h_ref[0:1, :], h_ref[1:2, :]
    h12, h22 = sums[K + 1 : K + 2, :], sums[K + 2 : K + 3, :]
    h32_sq = sums[K : K + 1, :] - jnp.sum(proj_two * proj_two, axis=0, keepdims=True) - h12 * h12 - h22 * h22
    h32 = jnp.sqrt(h32_sq)
    beta = beta_ref[0:1, :]
    m11 = h11 * h11 + h21 * h21
    m12 = h11 * h12 + h21 * h22
    m22 = h12 * h12 + h22 * h22 + h32 * h32
    g_one = beta * h11
    g_two = beta * h12
    determ = m11 * m22 - m12 * m12
    y_one = (m22 * g_one - m12 * g_two) / determ
    y_two = (m11 * g_two - m12 * g_one) / determ
    y_ref[...] = jnp.zeros((8, 128), F32)
    y_ref[0:1, :] = y_one
    y_ref[1:2, :] = y_two
    mixing = start_ref[...] - y_one * proj_ref[...] - y_two * proj_two
    weights = exact_dot(inverse, mixing, TN)[0:K]
    wide = jnp.concatenate([weights] * (ROWS // 128), axis=1)
    target, rank, local = (info_ref[i : i + 1, :] for i in range(3))
    at_rank = lax.broadcasted_iota(jnp.int32, (SLOTS, ROWS), 0) == rank
    rows = [jnp.sum(u_ref[a * K : (a + 1) * K, :] * wide, axis=0, keepdims=True) for a in range(3)]
    rows = jnp.concatenate([jnp.where(at_rank, r, 0.0) for r in rows + [local.astype(F32)]], axis=0)
    rows = jnp.concatenate(split(rows), axis=0)
    onehot = lax.broadcasted_iota(jnp.int32, (PEERS, ROWS), 0) == target
    onehot = jnp.where(onehot, 1.0, 0.0).astype(BF16)
    mine = lax.dot_general(onehot, rows, NT, preferred_element_type=F32)
    mine = mine + pltpu.roll(mine, 64, 1)
    peer = lax.broadcasted_iota(jnp.int32, (PEERS, 128), 0)
    lane = lax.broadcasted_iota(jnp.int32, (PEERS, 128), 1)
    other = jnp.where(peer % 2 == 0, pltpu.roll(mine, PEERS - 1, 0), pltpu.roll(mine, 1, 0))
    pair = jnp.where(lane < 64, mine, other)
    wire_ref[pl.ds(0, PEERS, stride=3), :] = jnp.where(peer < 2, 0.0, pltpu.roll(pair, 2, 0))
    wire_ref[pl.ds(1, PEERS, stride=3), :] = pair
    wire_ref[pl.ds(2, PEERS, stride=3), :] = jnp.where(peer >= PEERS - 2, 0.0, pltpu.roll(pair, PEERS - 2, 0))


def last_kernel(
    side_ref, got_ref, main_ref, ext_ref, y_ref, one_ref, two_ref, im_one_ref, im_two_ref,
    sol_ref, res_ref, left_ref, right_ref, pad_ref,
):
    side = side_ref[0]
    for dx in range(3):
        got = got_ref[pl.ds(dx, PEERS, stride=3), :].T
        planes = []
        for base in (0, 64):
            values = [
                [got[base + a * SLOTS + k : base + a * SLOTS + k + 1, :] for k in range(SLOTS)] for a in range(3)
            ]
            labels = [got[base + 48 + k : base + 49 + k, :] for k in range(SLOTS)]
            planes.append(two_level(values, labels, left_ref, right_ref))
        own, other = planes
        lines = [
            jnp.where(side == 0, other[a * CY : a * CY + 1, :], other[a * CY + 7 : a * CY + 8, :]) for a in range(3)
        ]
        put_plane(pad_ref, dx, own, jnp.concatenate(lines, axis=0), side)
        if dx == 1:
            term = own
    image = stencil(main_ref, ext_ref, pad_ref)
    y_one, y_two = y_ref[0:1, :], y_ref[1:2, :]
    solution = term + y_one * one_ref[...] + y_two * two_ref[...]
    for a in range(3):
        rows = slice(a * CY, (a + 1) * CY)
        residual = ext_ref[24 + a * CY : 24 + (a + 1) * CY, :] - image[a]
        residual = residual - y_one * im_one_ref[rows, :] - y_two * im_two_ref[rows, :]
        for y in range(CY):
            cols = slice(y * CZ, (y + 1) * CZ)
            sol_ref[a : a + 1, cols] = solution[a * CY + y : a * CY + y + 1, :]
            res_ref[a : a + 1, cols] = residual[y : y + 1, :]


def shape(*dims, dtype=F32):
    return jax.ShapeDtypeStruct(dims, dtype)


def call(kernel, outs, scratch=(), scalars=0, inputs=0, limit=40, cost=None):
    smem = [pl.BlockSpec(memory_space=pltpu.SMEM)] * scalars
    vmem = [pl.BlockSpec(memory_space=pltpu.VMEM)] * (inputs - scalars)
    return pl.pallas_call(
        kernel,
        out_shape=outs,
        in_specs=smem + vmem,
        out_specs=tuple(pl.BlockSpec(memory_space=pltpu.VMEM) for _ in outs),
        scratch_shapes=list(scratch),
        compiler_params=pltpu.CompilerParams(vmem_limit_bytes=limit * 2**20),
        cost_estimate=cost,
    )


def exchange(rows):
    count = rows.shape[0] // PEERS
    shaped = rows.reshape(PEERS, count, 1, 128)
    got = lax.all_to_all(shaped, GX_GY, split_axis=0, concat_axis=0, tiled=True)
    return got.reshape(PEERS * count, 128)


def halo(vector, line):
    other = lax.ppermute(line, "gy", [(0, 1), (1, 0)])
    plane = jnp.concatenate([vector, other], axis=0)
    up = lax.ppermute(plane, GX, [(i, i + 1) for i in range(N_GX - 1)])
    down = lax.ppermute(plane, GX, [(i + 1, i) for i in range(N_GX - 1)])
    return other, up, down


def body(operator, basis_u, basis_c, right_side, new_rows):
    side = lax.axis_index("gy").astype(jnp.int32).reshape(1)
    wire, info = call(
        pack_kernel,
        (shape(PEERS * WIRE, 128), shape(8, ROWS, dtype=jnp.int32)),
        [
            pltpu.VMEM((PEERS * SLOTS, ROWS), BF16),
            pltpu.VMEM((2 * MAIN, ROWS), BF16),
            pltpu.VMEM((128, ROWS), F32),
        ],
        inputs=4,
    )(operator, basis_c, right_side, new_rows.reshape(1, ROWS))
    got = exchange(wire)
    gram_row = jnp.sum(got.reshape(PEERS, WIRE, 128)[:, WIRE - 1], axis=0, keepdims=True)
    gram = exchange(jnp.broadcast_to(gram_row, (PEERS, 128)))
    two_level_scratch = [pltpu.VMEM((48, SLOTS * PEERS), F32), pltpu.VMEM((128, SLOTS * PEERS), BF16)]
    main, ext = call(
        unpack_kernel,
        (shape(MAIN * CY, 128), shape(48, 128)),
        [pltpu.VMEM((ROWS, SLOTS * PEERS), BF16), pltpu.VMEM((SLOTS * PEERS, 256), BF16), *two_level_scratch],
        inputs=1,
        cost=pl.CostEstimate(flops=4 * 10**9, bytes_accessed=5 * 10**6, transcendentals=0),
    )(got)
    vector_outs = (shape(3 * CY, 128), shape(8, 128))
    one, line, inverse, start, beta = call(
        first_kernel, (*vector_outs, shape(K, 128), shape(K, 128), shape(8, 128)), scalars=1, inputs=4
    )(side, gram, main, ext)
    pad = pltpu.VMEM((9 * 24, 128), F32)
    image_scratch = [pad, pltpu.VMEM(((K + 8) * CY, 128), F32)]
    image_outs = (shape(3 * CY, 128), shape(PEERS, 128))
    image_one, send = call(functools.partial(image_kernel, 1), image_outs, image_scratch, scalars=1, inputs=7)(
        side, main, ext, *halo(one, line), one
    )
    sums = exchange(send)
    two, line, proj_one, h_one = call(
        next_kernel, (*vector_outs, shape(K, 128), shape(8, 128)), scalars=1, inputs=6
    )(side, sums, main, image_one, one, inverse)
    image_two, send = call(functools.partial(image_kernel, 2), image_outs, image_scratch, scalars=1, inputs=8)(
        side, main, ext, *halo(two, line), one, two
    )
    sums = exchange(send)
    wire, y = call(send_kernel, (shape(PEERS * 3, 128), shape(8, 128)), inputs=8)(
        sums, inverse, start, proj_one, h_one, beta, basis_u, info
    )
    got = exchange(wire)
    return call(
        last_kernel, (shape(3, ROWS), shape(3, ROWS)), [*two_level_scratch, pad], scalars=1, inputs=9
    )(side, got, main, ext, y, one, two, image_one, image_two)


def solution(mesh):
    torus = Mesh(mesh.devices.reshape(4, 4, 4, mesh.shape["gy"]), ("gx_0", "gx_1", "gx_2", "gy"))
    placed = (P(None, GX_GY), P(None, GX_GY), P(None, GX_GY), P(None, GX_GY), P(GX_GY))
    return jax.shard_map(
        body,
        mesh=torus,
        in_specs=placed,
        out_specs=(P(None, GX_GY), P(None, GX_GY)),
        check_vma=False,
    )
```

```python
import functools

import jax
import jax.numpy as jnp
from jax import lax
from jax.experimental import pallas as pl
from jax.experimental.pallas import tpu as pltpu
from jax.sharding import Mesh
from jax.sharding import PartitionSpec as P

CY = 8
CZ = 128
K = 48
SLOTS = 16
PEERS = 128
ROWS = 1024
N_GX = 64
GX_GY = ("gx_0", "gx_1", "gx_2", "gy")
GX = ("gx_0", "gx_1", "gx_2")
F32 = jnp.float32
BF16 = jnp.bfloat16
HIGHEST = lax.Precision.HIGHEST
SIDE = K + 1
BANDS = 25
GRAM = 10
WIRE = 49 + GRAM
CHUNKS = 4
NT = (((1,), (1,)), ((), ()))
TN = (((0,), (0,)), ((), ()))
MAIN = 3 * 128


def split(x):
    high = x.astype(BF16)
    return high, (x - high.astype(F32)).astype(BF16)


def exact_dot(x, y, dims=(((1,), (0,)), ((), ()))):
    return lax.dot_general(x, y, dims, precision=HIGHEST, preferred_element_type=F32)


def half_sum(x):
    return x[:, :128] + x[:, 128:]


def folded(rows, start_ref):
    twice = rows + pltpu.roll(rows, SIDE, 1)
    sub = lax.broadcasted_iota(jnp.int32, (8, 128), 0)
    for tile in range(7):
        here = twice[tile * 8 : (tile + 1) * 8]
        total = jnp.zeros((8, 128), F32)
        for r in range(8):
            i = tile * 8 + r
            if i < SIDE:
                moved = pltpu.roll(here, (128 - i + BANDS * (i // GRAM)) % 128, 1)
                total = jnp.where(sub == r, moved, total)
        start_ref[tile * 8 : (tile + 1) * 8, :] = total
    lane = lax.broadcasted_iota(jnp.int32, (GRAM, 128), 1)
    return sum(
        jnp.where(lane // BANDS == g, start_ref[g * GRAM : (g + 1) * GRAM, :], 0.0) for g in range(5)
    )


def unfolded(bands, start_ref):
    sub = lax.broadcasted_iota(jnp.int32, (8, 128), 0)
    lane = lax.broadcasted_iota(jnp.int32, (GRAM, 128), 1)
    start_ref[48:56, :] = jnp.zeros((8, 128), F32)
    for g in range(5):
        start_ref[g * GRAM : (g + 1) * GRAM, :] = jnp.where(lane // BANDS == g, bands, 0.0)
    tiles = []
    for tile in range(7):
        here = start_ref[tile * 8 : (tile + 1) * 8, :]
        total = jnp.zeros((8, 128), F32)
        for r in range(8):
            i = tile * 8 + r
            if i < SIDE:
                moved = pltpu.roll(here, (128 + i - BANDS * (i // GRAM)) % 128, 1)
                total = jnp.where(sub == r, moved, total)
        tiles.append(total)
    half = jnp.concatenate(tiles + [jnp.zeros((72, 128), F32)], axis=0)
    row = lax.broadcasted_iota(jnp.int32, (128, 128), 0)
    lane = lax.broadcasted_iota(jnp.int32, (128, 128), 1)
    half = jnp.where(lane < SIDE, half + pltpu.roll(half, 128 - SIDE, 1), 0.0)
    return half + jnp.where(row == lane, 0.0, half.T)


def pack_kernel(
    op_hbm, c_hbm, b_hbm, rows_hbm, wire_hbm, info_ref,
    op_ref, c_ref, b_ref, rows_ref, p_ref, a_ref, fold_ref, wire_ref, in_sem, out_sem,
):
    copies = [
        pltpu.make_async_copy(source, target, in_sem.at[i])
        for i, (source, target) in enumerate(
            [(rows_hbm, rows_ref), (c_hbm, c_ref), (b_hbm, b_ref), (op_hbm, op_ref)]
        )
    ]
    for copy in copies:
        copy.start()
    copies[0].wait()
    new_rows = rows_ref[...]
    target = new_rows // ROWS
    local = new_rows % ROWS
    onehot = lax.broadcasted_iota(jnp.int32, (PEERS, ROWS), 0) == target
    onehot_f = jnp.where(onehot, 1.0, 0.0).astype(F32)
    onehot_b = onehot_f.astype(BF16)
    before = lax.broadcasted_iota(jnp.int32, (128, 128), 0) < lax.broadcasted_iota(jnp.int32, (128, 128), 1)
    before = jnp.where(before, 1.0, 0.0).astype(BF16)
    ones = jnp.ones((128, 128), BF16)
    seen = jnp.zeros((PEERS, 128), F32)
    ranks = []
    for block in range(ROWS // 128):
        part = onehot_b[:, block * 128 : (block + 1) * 128]
        count = jnp.dot(part, before, preferred_element_type=F32) + seen
        ranks.append(jnp.sum(onehot_f[:, block * 128 : (block + 1) * 128] * count, axis=0, keepdims=True))
        seen = seen + jnp.dot(part, ones, preferred_element_type=F32)
    rank = jnp.concatenate(ranks, axis=1)
    rank_at = jnp.where(onehot, rank, -1.0)
    info_ref[0:1, :] = target
    info_ref[1:2, :] = rank.astype(jnp.int32)
    info_ref[2:3, :] = local
    info_ref[3:8, :] = jnp.zeros((5, ROWS), jnp.int32)

    def put(tile, start, x):
        high, low = split(x)
        p_ref[tile * 256 + start : tile * 256 + start + x.shape[0], :] = high
        p_ref[tile * 256 + 128 + start : tile * 256 + 128 + start + x.shape[0], :] = low

    copies[1].wait()
    copies[2].wait()
    gram = jnp.zeros((64, 128), F32)
    a_ref[48:128, :] = jnp.zeros((80, ROWS), F32)
    for a in range(3):
        a_ref[0:48, :] = c_ref[a * K : (a + 1) * K, :]
        a_ref[48:49, :] = b_ref[a : a + 1, :]
        gram = gram + exact_dot(a_ref[0:64, :], a_ref[...], NT)
    bands = folded(gram, fold_ref)
    for i in range(GRAM):
        wire_ref[pl.ds(49 + i, PEERS, stride=WIRE), :] = jnp.broadcast_to(bands[i : i + 1, :], (PEERS, 128))
    put(0, 0, c_ref[0:128, :])
    put(1, 0, c_ref[128:144, :])
    copies[3].wait()
    put(1, 16, op_ref[0:112, :])
    put(2, 0, op_ref[112:240, :])

    at_rank = lax.broadcasted_iota(jnp.int32, (SLOTS, ROWS), 0).astype(F32) == rank
    rest = [op_ref[240 + i : 241 + i, :] for i in range(3)] + [b_ref[i : i + 1, :] for i in range(3)]
    rest = [jnp.where(at_rank, row, 0.0) for row in rest + [local.astype(F32)]]
    rest = jnp.concatenate(rest + [jnp.zeros((SLOTS, ROWS), F32)], axis=0)
    rest = jnp.concatenate(split(rest), axis=0)
    wire_ref[pl.ds(48, PEERS, stride=WIRE), :] = half_sum(
        lax.dot_general(onehot_b, rest, NT, preferred_element_type=F32)
    )
    sent = []
    count = PEERS // CHUNKS
    for chunk in range(CHUNKS):
        mine = rank_at[chunk * count : (chunk + 1) * count]
        choice = [jnp.where(mine == k, 1.0, 0.0).astype(BF16) for k in range(SLOTS)]
        moved = lax.dot_general(jnp.concatenate(choice, axis=0), p_ref[...], NT, preferred_element_type=F32)
        for tile in range(3):
            both = half_sum(moved[:, tile * 256 : (tile + 1) * 256])
            for k in range(SLOTS):
                wire_ref[pl.ds(chunk * count * WIRE + tile * SLOTS + k, count, stride=WIRE), :] = both[
                    k * count : (k + 1) * count
                ]
        rows = pl.ds(chunk * count * WIRE, count * WIRE)
        sent.append(pltpu.make_async_copy(wire_ref.at[rows], wire_hbm.at[rows], out_sem.at[chunk]))
        sent[-1].start()
    for copy in sent:
        copy.wait()


def two_level(groups, left_ref, right_ref):
    eight = lax.broadcasted_iota(jnp.int32, (CY, 128), 0)
    deep = lax.broadcasted_iota(jnp.int32, (128, 128), 0)
    count = groups[0][0].shape[0] // SLOTS
    for g, (values, labels) in enumerate(groups):
        labels = labels.astype(jnp.int32)
        y, z = labels // CZ, labels % CZ
        for k in range(SLOTS):
            cols = slice(k * 128, (k + 1) * 128)
            right_ref[g * 128 : (g + 1) * 128, cols] = jnp.where(deep == z[k : k + 1], 1.0, 0.0).astype(BF16)
            here = eight == y[k : k + 1]
            for c in range(count):
                row = (g * count + c) * CY
                value = values[c * SLOTS + k : c * SLOTS + k + 1]
                left_ref[row : row + CY, cols] = jnp.where(here, value, 0.0)
    rows = len(groups) * count * CY
    left = jnp.concatenate(split(left_ref[...]), axis=0)
    moved = lax.dot_general(left, right_ref[...], NT, preferred_element_type=F32)
    moved = moved[0:rows] + moved[rows:]
    size = count * CY
    return [moved[g * size : (g + 1) * size, g * 128 : (g + 1) * 128] for g in range(len(groups))]


def minus_combined(start, main_ref, weights):
    result = []
    for a in range(3):
        total = start[a]
        for m in range(K):
            row = (a * K + m) * CY
            total = total - main_ref[row : row + CY, :] * weights[m : m + 1, :]
        result.append(total)
    return result


def put_vector(vector, place_ref, v_ref, line_ref):
    lower = place_ref[0] == 0
    line_ref[...] = jnp.zeros((8, 128), F32)
    v_ref[24:32, :] = jnp.zeros((8, 128), F32)
    for a in range(3):
        v_ref[a * CY : (a + 1) * CY, :] = vector[a]
        line_ref[a : a + 1, :] = jnp.where(lower, vector[a][7:8, :], vector[a][0:1, :])


def swept(work, begin, count):
    row_id = lax.broadcasted_iota(jnp.int32, (K, 128), 0)
    columns = [jnp.broadcast_to(work[:, j : j + 1], (K, 128)) for j in range(begin, begin + count)]
    for s in range(count):
        j = begin + s
        column = columns[s]
        inverse = 1.0 / column[j : j + 1, :]
        here = row_id == j

        def step(x):
            pivot = x[j : j + 1, :] * inverse
            return jnp.where(here, pivot, x - column * pivot)

        work = step(work)
        columns = columns[: s + 1] + [step(c) for c in columns[s + 1 :]]
    return work


def unpack_kernel(
    place_ref, wire_ref, main_ref, ext_ref, v_ref, line_ref, inv_ref, start_ref, beta_ref,
    t_ref, r_ref, left_ref, right_ref, fold_ref,
):
    bands = [
        jnp.sum(wire_ref[pl.ds(49 + i, PEERS, stride=WIRE), :], axis=0, keepdims=True) for i in range(GRAM)
    ]
    gram = unfolded(jnp.concatenate(bands, axis=0), fold_ref)
    load_sq = jnp.broadcast_to(gram[48:49, 48:49], (1, 128))
    row_id = lax.broadcasted_iota(jnp.int32, (K, 128), 0)
    lane = lax.broadcasted_iota(jnp.int32, (K, 128), 1)
    raw = jnp.broadcast_to(gram[0:K, K : K + 1], (K, 128))
    work = jnp.where(lane < K + 1, gram[0:K], jnp.where(lane - 64 == row_id, 1.0, 0.0))

    rest = wire_ref[pl.ds(48, PEERS, stride=WIRE), :].T
    labels = rest[6 * SLOTS : 7 * SLOTS]
    node = lax.broadcasted_iota(jnp.int32, (ROWS, 128), 0).astype(F32)
    for k in range(SLOTS):
        t_ref[:, k * 128 : (k + 1) * 128] = jnp.where(node == labels[k : k + 1], 1.0, 0.0).astype(BF16)
    for tile in range(3):
        work = swept(work, tile * 16, 4)
        work = swept(work, tile * 16 + 4, 4)
        for k in range(SLOTS):
            high, low = split(wire_ref[pl.ds(tile * SLOTS + k, PEERS, stride=WIRE), :])
            r_ref[k * 128 : (k + 1) * 128, 0:128] = high
            r_ref[k * 128 : (k + 1) * 128, 128:256] = low
        work = swept(work, tile * 16 + 8, 4)
        moved = jnp.dot(t_ref[...], r_ref[...], preferred_element_type=F32)
        work = swept(work, tile * 16 + 12, 4)
        for y in range(CY):
            block = half_sum(moved[y * CZ : (y + 1) * CZ])
            main_ref[pl.ds(tile * 128 * CY + y, 128, stride=CY), :] = block.T
    [ext] = two_level([(rest[0 : 6 * SLOTS], labels)], left_ref, right_ref)
    ext_ref[...] = ext

    inverse = jnp.where(lane < K, pltpu.roll(work, 64, 1), 0.0)
    weights = jnp.broadcast_to(work[:, K : K + 1], (K, 128))
    inv_ref[...] = inverse
    start_ref[...] = weights
    beta = jnp.sqrt(load_sq - jnp.sum(raw * weights, axis=0, keepdims=True))
    beta_ref[...] = jnp.broadcast_to(beta, (8, 128))
    load = [ext[24 + a * CY : 24 + (a + 1) * CY, :] for a in range(3)]
    vector = minus_combined(load, main_ref, weights)
    put_vector([v / beta for v in vector], place_ref, v_ref, line_ref)


def put_plane(pad_ref, dx, plane, line, side):
    for a in range(3):
        base = (dx * 3 + a) * 24
        edge = line[a : a + 1, :]
        pad_ref[base + 7 : base + 8, :] = jnp.where(side == 1, edge, 0.0)
        pad_ref[base + 8 : base + 16, :] = plane[a * CY : (a + 1) * CY, :]
        pad_ref[base + 16 : base + 17, :] = jnp.where(side == 0, edge, 0.0)


def stencil(main_ref, ext_ref, pad_ref):
    lane = lax.broadcasted_iota(jnp.int32, (CY, 128), 1)
    total = [jnp.zeros((CY, 128), F32) for _ in range(3)]
    for dx in range(3):
        for dy in range(3):
            for b in range(3):
                start = (dx * 3 + b) * 24 + 7 + dy
                here = pad_ref[start : start + CY, :]
                left = jnp.where(lane == 0, 0.0, pltpu.roll(here, 1, 1))
                right = jnp.where(lane == 127, 0.0, pltpu.roll(here, 127, 1))
                for dz, moved in enumerate((left, here, right)):
                    for a in range(3):
                        q = ((dx * 9 + dy * 3 + dz) * 3 + a) * 3 + b
                        if q < 240:
                            row = (3 * K + q) * CY
                            total[a] = total[a] + main_ref[row : row + CY, :] * moved
                        else:
                            row = (q - 240) * CY
                            total[a] = total[a] + ext_ref[row : row + CY, :] * moved
    return total


def image_kernel(count, place_ref, main_ref, ext_ref, line_ref, first_ref, second_ref, *refs):
    vectors, (image_ref, send_ref, pad_ref, part_ref) = refs[:count], refs[count:]
    side = place_ref[0]
    even = place_ref[1] == 0
    first, second = first_ref[...], second_ref[...]
    up, down = jnp.where(even, second, first), jnp.where(even, first, second)
    put_plane(pad_ref, 0, up[0:24], up[24:32], side)
    put_plane(pad_ref, 1, vectors[-1][0:24, :], line_ref[...], side)
    put_plane(pad_ref, 2, down[0:24], down[24:32], side)
    image = stencil(main_ref, ext_ref, pad_ref)
    for a in range(3):
        image_ref[a * CY : (a + 1) * CY, :] = image[a]
    for m in range(K):
        rows = [(a * K + m) * CY for a in range(3)]
        part_ref[m * CY : (m + 1) * CY, :] = sum(
            main_ref[row : row + CY, :] * image[a] for a, row in enumerate(rows)
        )
    others = [image] + [[ref[a * CY : (a + 1) * CY, :] for a in range(3)] for ref in vectors]
    for i in range(8):
        m = K + i
        if i < len(others):
            part_ref[m * CY : (m + 1) * CY, :] = sum(o * w for o, w in zip(others[i], image))
        else:
            part_ref[m * CY : (m + 1) * CY, :] = jnp.zeros((CY, 128), F32)
    part = sum(part_ref[pl.ds(y, K + 8, stride=CY), :] for y in range(CY))
    part = jnp.concatenate([part, jnp.zeros((128 - K - 8, 128), F32)], axis=0)
    send_ref[...] = exact_dot(jnp.ones((PEERS, 128), F32), part, NT)


def totals(got_ref):
    return exact_dot(got_ref[...], jnp.ones((PEERS, 128), F32), TN)


def next_kernel(place_ref, got_ref, main_ref, image_ref, one_ref, inv_ref, v_ref, line_ref, weights_ref, h_ref):
    sums = totals(got_ref)
    weights = exact_dot(inv_ref[...], sums)
    h11 = sums[K + 1 : K + 2, :]
    along = jnp.sum(sums[0:K] * weights, axis=0, keepdims=True)
    h21 = jnp.sqrt(sums[K : K + 1, :] - along - h11 * h11)
    begin = [
        image_ref[a * CY : (a + 1) * CY, :] - h11 * one_ref[a * CY : (a + 1) * CY, :] for a in range(3)
    ]
    vector = minus_combined(begin, main_ref, weights)
    put_vector([v / h21 for v in vector], place_ref, v_ref, line_ref)
    weights_ref[...] = weights
    h_ref[...] = jnp.zeros((8, 128), F32)
    h_ref[0:1, :] = h11
    h_ref[1:2, :] = h21


def send_kernel(got_ref, inv_ref, start_ref, first_ref, h_ref, beta_ref, u_ref, info_ref, wire_ref, y_ref):
    sums = totals(got_ref)
    weights = exact_dot(inv_ref[...], sums)
    h11, h21 = h_ref[0:1, :], h_ref[1:2, :]
    h12, h22 = sums[K + 1 : K + 2, :], sums[K + 2 : K + 3, :]
    along = jnp.sum(sums[0:K] * weights, axis=0, keepdims=True)
    h32 = jnp.sqrt(sums[K : K + 1, :] - along - h12 * h12 - h22 * h22)
    beta = beta_ref[0:1, :]
    m11 = h11 * h11 + h21 * h21
    m12 = h11 * h12 + h21 * h22
    m22 = h12 * h12 + h22 * h22 + h32 * h32
    g_one = beta * h11
    g_two = beta * h12
    determ = m11 * m22 - m12 * m12
    y_one = (m22 * g_one - m12 * g_two) / determ
    y_two = (m11 * g_two - m12 * g_one) / determ
    y_ref[...] = jnp.zeros((8, 128), F32)
    y_ref[0:1, :] = y_one
    y_ref[1:2, :] = y_two
    weights = start_ref[...] - y_one * first_ref[...] - y_two * weights
    wide = jnp.concatenate([weights] * (ROWS // 128), axis=1)
    target, rank, local = (info_ref[i : i + 1, :] for i in range(3))
    at_rank = lax.broadcasted_iota(jnp.int32, (SLOTS, ROWS), 0) == rank
    rows = [jnp.sum(u_ref[a * K : (a + 1) * K, :] * wide, axis=0, keepdims=True) for a in range(3)]
    rows = jnp.concatenate([jnp.where(at_rank, r, 0.0) for r in rows + [local.astype(F32)]], axis=0)
    rows = jnp.concatenate(split(rows), axis=0)
    onehot = lax.broadcasted_iota(jnp.int32, (PEERS, ROWS), 0) == target
    onehot = jnp.where(onehot, 1.0, 0.0).astype(BF16)
    mine = lax.dot_general(onehot, rows, NT, preferred_element_type=F32)
    mine = mine + pltpu.roll(mine, 64, 1)
    peer = lax.broadcasted_iota(jnp.int32, (PEERS, 128), 0)
    lane = lax.broadcasted_iota(jnp.int32, (PEERS, 128), 1)
    other = jnp.where(peer % 2 == 0, pltpu.roll(mine, PEERS - 1, 0), pltpu.roll(mine, 1, 0))
    pair = jnp.where(lane < 64, mine, other)
    wire_ref[pl.ds(0, PEERS, stride=3), :] = jnp.where(peer < 2, 0.0, pltpu.roll(pair, 2, 0))
    wire_ref[pl.ds(1, PEERS, stride=3), :] = pair
    wire_ref[pl.ds(2, PEERS, stride=3), :] = jnp.where(peer >= PEERS - 2, 0.0, pltpu.roll(pair, PEERS - 2, 0))


def last_kernel(
    place_ref, got_ref, main_ref, ext_ref, y_ref, one_ref, two_ref, im_one_ref, im_two_ref,
    sol_ref, res_ref, left_ref, right_ref, pad_ref,
):
    side = place_ref[0]
    for dx in range(3):
        got = got_ref[pl.ds(dx, PEERS, stride=3), :].T
        own, other = two_level(
            [(got[base : base + 48], got[base + 48 : base + 64]) for base in (0, 64)], left_ref, right_ref
        )
        lines = [
            jnp.where(side == 0, other[a * CY : a * CY + 1, :], other[a * CY + 7 : a * CY + 8, :]) for a in range(3)
        ]
        put_plane(pad_ref, dx, own, jnp.concatenate(lines, axis=0), side)
        if dx == 1:
            term = own
    image = stencil(main_ref, ext_ref, pad_ref)
    y_one, y_two = y_ref[0:1, :], y_ref[1:2, :]
    solution = term + y_one * one_ref[0:24, :] + y_two * two_ref[0:24, :]
    for a in range(3):
        rows = slice(a * CY, (a + 1) * CY)
        residual = ext_ref[24 + a * CY : 24 + (a + 1) * CY, :] - image[a]
        residual = residual - y_one * im_one_ref[rows, :] - y_two * im_two_ref[rows, :]
        for y in range(CY):
            cols = slice(y * CZ, (y + 1) * CZ)
            sol_ref[a : a + 1, cols] = solution[a * CY + y : a * CY + y + 1, :]
            res_ref[a : a + 1, cols] = residual[y : y + 1, :]


def shape(*dims, dtype=F32):
    return jax.ShapeDtypeStruct(dims, dtype)


def specs(*spaces):
    return tuple(pl.BlockSpec(memory_space=space) for space in spaces)


def call(kernel, outs, scratch=(), scalars=0, inputs=0, in_specs=None, out_specs=None, limit=40):
    vmem = pltpu.VMEM
    return pl.pallas_call(
        kernel,
        out_shape=outs,
        in_specs=in_specs or specs(*[pltpu.SMEM] * scalars, *[vmem] * (inputs - scalars)),
        out_specs=out_specs or specs(*[vmem] * len(outs)),
        scratch_shapes=list(scratch),
        compiler_params=pltpu.CompilerParams(vmem_limit_bytes=limit * 2**20),
    )


def exchange(rows):
    count = rows.shape[0] // PEERS
    shaped = rows.reshape(PEERS, count, 1, 128)
    got = lax.all_to_all(shaped, GX_GY, split_axis=0, concat_axis=0, tiled=True)
    return got.reshape(PEERS * count, 128)


def swap(plane, first):
    pairs = [(i, i + 1) for i in range(first, N_GX - 1, 2)]
    return lax.ppermute(plane, GX, pairs + [(j, i) for i, j in pairs])


def halo(vector, line):
    other = lax.ppermute(line, "gy", [(0, 1), (1, 0)])
    plane = lax.dynamic_update_slice(vector, other, (24, 0))
    return other, swap(plane, 0), swap(plane, 1)


def body(operator, basis_u, basis_c, right_side, new_rows):
    place = jnp.stack([lax.axis_index("gy"), lax.axis_index(GX) % 2]).astype(jnp.int32)
    vmem, hbm = pltpu.VMEM, pltpu.HBM
    wire, info = call(
        pack_kernel,
        (shape(PEERS * WIRE, 128), shape(8, ROWS, dtype=jnp.int32)),
        [
            vmem((243, ROWS), F32),
            vmem((144, ROWS), F32),
            vmem((3, ROWS), F32),
            vmem((1, ROWS), jnp.int32),
            vmem((2 * MAIN, ROWS), BF16),
            vmem((128, ROWS), F32),
            vmem((56, 128), F32),
            vmem((PEERS * WIRE, 128), F32),
            pltpu.SemaphoreType.DMA((4,)),
            pltpu.SemaphoreType.DMA((CHUNKS,)),
        ],
        in_specs=specs(hbm, hbm, hbm, hbm),
        out_specs=specs(hbm, vmem),
    )(operator, basis_c, right_side, new_rows.reshape(1, ROWS))
    got = exchange(wire)
    vector_outs = (shape(32, 128), shape(8, 128))
    main, ext, one, line, inverse, start, beta = call(
        unpack_kernel,
        (shape(MAIN * CY, 128), shape(48, 128), *vector_outs, shape(K, 128), shape(K, 128), shape(8, 128)),
        [
            vmem((ROWS, SLOTS * PEERS), BF16),
            vmem((SLOTS * PEERS, 256), BF16),
            vmem((48, SLOTS * PEERS), F32),
            vmem((128, SLOTS * PEERS), BF16),
            vmem((56, 128), F32),
        ],
        scalars=1,
        inputs=2,
    )(place, got)
    pad = vmem((9 * 24, 128), F32)
    image_scratch = [pad, vmem(((K + 8) * CY, 128), F32)]
    image_outs = (shape(3 * CY, 128), shape(PEERS, 128))
    image_one, send = call(functools.partial(image_kernel, 1), image_outs, image_scratch, scalars=1, inputs=7)(
        place, main, ext, *halo(one, line), one
    )
    sums = exchange(send)
    two, line, weights, h_one = call(
        next_kernel, (*vector_outs, shape(K, 128), shape(8, 128)), scalars=1, inputs=6
    )(place, sums, main, image_one, one, inverse)
    image_two, send = call(functools.partial(image_kernel, 2), image_outs, image_scratch, scalars=1, inputs=8)(
        place, main, ext, *halo(two, line), one, two
    )
    sums = exchange(send)
    wire, y = call(send_kernel, (shape(PEERS * 3, 128), shape(8, 128)), inputs=8)(
        sums, inverse, start, weights, h_one, beta, basis_u, info
    )
    got = exchange(wire)
    return call(
        last_kernel,
        (shape(3, ROWS), shape(3, ROWS)),
        [vmem((48, SLOTS * PEERS), F32), vmem((256, SLOTS * PEERS), BF16), pad],
        scalars=1,
        inputs=9,
    )(place, got, main, ext, y, one, two, image_one, image_two)


def solution(mesh):
    torus = Mesh(mesh.devices.reshape(4, 4, 4, mesh.shape["gy"]), ("gx_0", "gx_1", "gx_2", "gy"))
    placed = (P(None, GX_GY), P(None, GX_GY), P(None, GX_GY), P(None, GX_GY), P(GX_GY))
    return jax.shard_map(
        body,
        mesh=torus,
        in_specs=placed,
        out_specs=(P(None, GX_GY), P(None, GX_GY)),
        check_vma=False,
    )
```

```python
import functools

import jax
import jax.numpy as jnp
from jax import lax
from jax.experimental import pallas as pl
from jax.experimental.pallas import tpu as pltpu
from jax.sharding import Mesh
from jax.sharding import PartitionSpec as P

CY = 8
CZ = 128
K = 48
SLOTS = 16
PEERS = 128
ROWS = 1024
N_GX = 64
GX_GY = ("gx_0", "gx_1", "gx_2", "gy")
GX = ("gx_0", "gx_1", "gx_2")
F32 = jnp.float32
BF16 = jnp.bfloat16
HIGHEST = lax.Precision.HIGHEST
SIDE = K + 1
BANDS = 25
GRAM = 10
WIRE = 49 + GRAM
CHUNKS = 8
NT = (((1,), (1,)), ((), ()))
TN = (((0,), (0,)), ((), ()))
MAIN = 3 * 128


def split(x):
    high = x.astype(BF16)
    return high, (x - high.astype(F32)).astype(BF16)


def exact_dot(x, y, dims=(((1,), (0,)), ((), ()))):
    return lax.dot_general(x, y, dims, precision=HIGHEST, preferred_element_type=F32)


def half_sum(x):
    return x[:, :128] + x[:, 128:]


def folded(rows, start_ref):
    twice = rows + pltpu.roll(rows, SIDE, 1)
    sub = lax.broadcasted_iota(jnp.int32, (8, 128), 0)
    for tile in range(7):
        here = twice[tile * 8 : (tile + 1) * 8]
        total = jnp.zeros((8, 128), F32)
        for r in range(8):
            i = tile * 8 + r
            if i < SIDE:
                moved = pltpu.roll(here, (128 - i + BANDS * (i // GRAM)) % 128, 1)
                total = jnp.where(sub == r, moved, total)
        start_ref[tile * 8 : (tile + 1) * 8, :] = total
    lane = lax.broadcasted_iota(jnp.int32, (GRAM, 128), 1)
    return sum(
        jnp.where(lane // BANDS == g, start_ref[g * GRAM : (g + 1) * GRAM, :], 0.0) for g in range(5)
    )


def unfolded(bands, start_ref):
    sub = lax.broadcasted_iota(jnp.int32, (8, 128), 0)
    lane = lax.broadcasted_iota(jnp.int32, (GRAM, 128), 1)
    start_ref[48:56, :] = jnp.zeros((8, 128), F32)
    for g in range(5):
        start_ref[g * GRAM : (g + 1) * GRAM, :] = jnp.where(lane // BANDS == g, bands, 0.0)
    tiles = []
    for tile in range(7):
        here = start_ref[tile * 8 : (tile + 1) * 8, :]
        total = jnp.zeros((8, 128), F32)
        for r in range(8):
            i = tile * 8 + r
            if i < SIDE:
                moved = pltpu.roll(here, (128 + i - BANDS * (i // GRAM)) % 128, 1)
                total = jnp.where(sub == r, moved, total)
        tiles.append(total)
    half = jnp.concatenate(tiles + [jnp.zeros((72, 128), F32)], axis=0)
    row = lax.broadcasted_iota(jnp.int32, (128, 128), 0)
    lane = lax.broadcasted_iota(jnp.int32, (128, 128), 1)
    half = jnp.where(lane < SIDE, half + pltpu.roll(half, 128 - SIDE, 1), 0.0)
    return half + jnp.where(row == lane, 0.0, half.T)


def pack_kernel(
    op_hbm, c_hbm, b_hbm, rows_hbm, wire_hbm, info_ref,
    op_ref, c_ref, b_ref, rows_ref, p_ref, a_ref, fold_ref, wire_ref, in_sem, out_sem,
):
    copies = [
        pltpu.make_async_copy(source, target, in_sem.at[i])
        for i, (source, target) in enumerate(
            [(rows_hbm, rows_ref), (c_hbm, c_ref), (b_hbm, b_ref), (op_hbm, op_ref)]
        )
    ]
    for copy in copies:
        copy.start()
    copies[0].wait()
    new_rows = rows_ref[...]
    target = new_rows // ROWS
    local = new_rows % ROWS
    onehot = lax.broadcasted_iota(jnp.int32, (PEERS, ROWS), 0) == target
    onehot_f = jnp.where(onehot, 1.0, 0.0).astype(F32)
    onehot_b = onehot_f.astype(BF16)
    before = lax.broadcasted_iota(jnp.int32, (128, 128), 0) < lax.broadcasted_iota(jnp.int32, (128, 128), 1)
    before = jnp.where(before, 1.0, 0.0).astype(BF16)
    ones = jnp.ones((128, 128), BF16)
    seen = jnp.zeros((PEERS, 128), F32)
    ranks = []
    for block in range(ROWS // 128):
        part = onehot_b[:, block * 128 : (block + 1) * 128]
        count = jnp.dot(part, before, preferred_element_type=F32) + seen
        ranks.append(jnp.sum(onehot_f[:, block * 128 : (block + 1) * 128] * count, axis=0, keepdims=True))
        seen = seen + jnp.dot(part, ones, preferred_element_type=F32)
    rank = jnp.concatenate(ranks, axis=1)
    rank_at = jnp.where(onehot, rank, -1.0)
    info_ref[0:1, :] = target
    info_ref[1:2, :] = rank.astype(jnp.int32)
    info_ref[2:3, :] = local
    info_ref[3:8, :] = jnp.zeros((5, ROWS), jnp.int32)
    for copy in copies[1:]:
        copy.wait()
    middle = jnp.concatenate([c_ref[128:144, :], op_ref[0:112, :]], axis=0)
    for tile, x in enumerate((c_ref[0:128, :], middle, op_ref[112:240, :])):
        p_ref[:, tile * 256 : tile * 256 + 128], p_ref[:, tile * 256 + 128 : (tile + 1) * 256] = split(x.T)
    gram = jnp.zeros((64, 128), F32)
    a_ref[48:128, :] = jnp.zeros((80, ROWS), F32)
    for a in range(3):
        a_ref[0:48, :] = c_ref[a * K : (a + 1) * K, :]
        a_ref[48:49, :] = b_ref[a : a + 1, :]
        gram = gram + exact_dot(a_ref[0:64, :], a_ref[...], NT)
    bands = folded(gram, fold_ref)
    for i in range(GRAM):
        wire_ref[pl.ds(49 + i, PEERS, stride=WIRE), :] = jnp.broadcast_to(bands[i : i + 1, :], (PEERS, 128))

    at_rank = lax.broadcasted_iota(jnp.int32, (SLOTS, ROWS), 0).astype(F32) == rank
    rest = [op_ref[240 + i : 241 + i, :] for i in range(3)] + [b_ref[i : i + 1, :] for i in range(3)]
    rest = [jnp.where(at_rank, row, 0.0) for row in rest + [local.astype(F32)]]
    rest = jnp.concatenate(rest + [jnp.zeros((SLOTS, ROWS), F32)], axis=0)
    rest = jnp.concatenate(split(rest), axis=0)
    wire_ref[pl.ds(48, PEERS, stride=WIRE), :] = half_sum(
        lax.dot_general(onehot_b, rest, NT, preferred_element_type=F32)
    )
    sent = []
    count = PEERS // CHUNKS
    for chunk in range(CHUNKS):
        mine = rank_at[chunk * count : (chunk + 1) * count]
        choice = [jnp.where(mine == k, 1.0, 0.0).astype(BF16) for k in range(SLOTS)]
        moved = jnp.dot(jnp.concatenate(choice, axis=0), p_ref[...], preferred_element_type=F32)
        for tile in range(3):
            both = half_sum(moved[:, tile * 256 : (tile + 1) * 256])
            for k in range(SLOTS):
                wire_ref[pl.ds(chunk * count * WIRE + tile * SLOTS + k, count, stride=WIRE), :] = both[
                    k * count : (k + 1) * count
                ]
        rows = pl.ds(chunk * count * WIRE, count * WIRE)
        sent.append(pltpu.make_async_copy(wire_ref.at[rows], wire_hbm.at[rows], out_sem.at[chunk]))
        sent[-1].start()
    for copy in sent:
        copy.wait()


def two_level(groups, left_ref, right_ref):
    eight = lax.broadcasted_iota(jnp.int32, (CY, 128), 0)
    deep = lax.broadcasted_iota(jnp.int32, (128, 128), 0)
    count = groups[0][0].shape[0] // SLOTS
    for g, (values, labels) in enumerate(groups):
        labels = labels.astype(jnp.int32)
        y, z = labels // CZ, labels % CZ
        for k in range(SLOTS):
            cols = slice(k * 128, (k + 1) * 128)
            right_ref[g * 128 : (g + 1) * 128, cols] = jnp.where(deep == z[k : k + 1], 1.0, 0.0).astype(BF16)
            here = eight == y[k : k + 1]
            for c in range(count):
                row = (g * count + c) * CY
                value = values[c * SLOTS + k : c * SLOTS + k + 1]
                left_ref[row : row + CY, cols] = jnp.where(here, value, 0.0)
    rows = len(groups) * count * CY
    left = jnp.concatenate(split(left_ref[...]), axis=0)
    moved = lax.dot_general(left, right_ref[...], NT, preferred_element_type=F32)
    moved = moved[0:rows] + moved[rows:]
    size = count * CY
    return [moved[g * size : (g + 1) * size, g * 128 : (g + 1) * 128] for g in range(len(groups))]


def minus_combined(start, main_ref, weights):
    result = []
    for a in range(3):
        total = start[a]
        for m in range(K):
            row = (a * K + m) * CY
            total = total - main_ref[row : row + CY, :] * weights[m : m + 1, :]
        result.append(total)
    return result


def put_vector(vector, place_ref, v_ref, line_ref):
    lower = place_ref[0:1, :] == 0
    line_ref[...] = jnp.zeros((8, 128), F32)
    v_ref[24:32, :] = jnp.zeros((8, 128), F32)
    for a in range(3):
        v_ref[a * CY : (a + 1) * CY, :] = vector[a]
        line_ref[a : a + 1, :] = jnp.where(lower, vector[a][7:8, :], vector[a][0:1, :])


def swept(work, begin, count):
    row_id = lax.broadcasted_iota(jnp.int32, (K, 128), 0)
    columns = [jnp.broadcast_to(work[:, j : j + 1], (K, 128)) for j in range(begin, begin + count)]
    for s in range(count):
        j = begin + s
        column = columns[s]
        inverse = 1.0 / column[j : j + 1, :]
        here = row_id == j

        def step(x):
            pivot = x[j : j + 1, :] * inverse
            return jnp.where(here, pivot, x - column * pivot)

        work = step(work)
        columns = columns[: s + 1] + [step(c) for c in columns[s + 1 :]]
    return work


def unpack_kernel(
    place_ref, wire_hbm, main_ref, ext_ref, v_ref, line_ref, inv_ref, start_ref, beta_ref,
    wire_ref, t_ref, r_ref, part_ref, left_ref, right_ref, fold_ref, in_sem,
):
    half = PEERS // 2
    copies = []
    for part in range(2):
        rows = pl.ds(part * half * WIRE, half * WIRE)
        copies.append(pltpu.make_async_copy(wire_hbm.at[rows], wire_ref.at[rows], in_sem.at[part]))
        copies[-1].start()
    node = lax.broadcasted_iota(jnp.int32, (ROWS, 128), 0).astype(F32)
    for part in range(2):
        copies[part].wait()
        if part == 1:
            bands = [
                jnp.sum(wire_ref[pl.ds(49 + i, PEERS, stride=WIRE), :], axis=0, keepdims=True) for i in range(GRAM)
            ]
            gram = unfolded(jnp.concatenate(bands, axis=0), fold_ref)
            load_sq = jnp.broadcast_to(gram[48:49, 48:49], (1, 128))
            row_id = lax.broadcasted_iota(jnp.int32, (K, 128), 0)
            lane = lax.broadcasted_iota(jnp.int32, (K, 128), 1)
            raw = jnp.broadcast_to(gram[0:K, K : K + 1], (K, 128))
            work = jnp.where(lane < K + 1, gram[0:K], jnp.where(lane - 64 == row_id, 1.0, 0.0))
            for begin in range(0, K, 4):
                work = swept(work, begin, 4)
        first = part * half * WIRE
        labels = wire_ref[pl.ds(first + 48, half, stride=WIRE), :].T[6 * SLOTS : 7 * SLOTS]
        labels = jnp.concatenate([labels[0:8], labels[8:16]], axis=1)
        for i in range(8):
            t_ref[part, :, i * 128 : (i + 1) * 128] = jnp.where(node == labels[i : i + 1], 1.0, 0.0).astype(BF16)
        for tile in range(3):
            for k in range(SLOTS):
                high, low = split(wire_ref[pl.ds(first + tile * SLOTS + k, half, stride=WIRE), :])
                row = k % 8 * 128 + k // 8 * half
                r_ref[part, tile, row : row + half, 0:128] = high
                r_ref[part, tile, row : row + half, 128:256] = low
            moved = half_sum(jnp.dot(t_ref[part], r_ref[part, tile], preferred_element_type=F32))
            if part == 0:
                part_ref[tile] = moved
                continue
            moved = moved + part_ref[tile]
            for y in range(CY):
                main_ref[pl.ds(tile * 128 * CY + y, 128, stride=CY), :] = moved[y * CZ : (y + 1) * CZ].T
    rest = wire_ref[pl.ds(48, PEERS, stride=WIRE), :].T
    labels = rest[6 * SLOTS : 7 * SLOTS]
    [ext] = two_level([(rest[0 : 6 * SLOTS], labels)], left_ref, right_ref)
    ext_ref[...] = ext

    inverse = jnp.where(lane < K, pltpu.roll(work, 64, 1), 0.0)
    weights = jnp.broadcast_to(work[:, K : K + 1], (K, 128))
    inv_ref[...] = inverse
    start_ref[...] = weights
    beta = jnp.sqrt(load_sq - jnp.sum(raw * weights, axis=0, keepdims=True))
    beta_ref[...] = jnp.broadcast_to(beta, (8, 128))
    load = [ext[24 + a * CY : 24 + (a + 1) * CY, :] for a in range(3)]
    vector = minus_combined(load, main_ref, weights)
    put_vector([v / beta for v in vector], place_ref, v_ref, line_ref)


def put_plane(pad_ref, dx, plane, line, side):
    for a in range(3):
        base = (dx * 3 + a) * 24
        edge = line[a : a + 1, :]
        pad_ref[base + 7 : base + 8, :] = jnp.where(side == 1, edge, 0.0)
        pad_ref[base + 8 : base + 16, :] = plane[a * CY : (a + 1) * CY, :]
        pad_ref[base + 16 : base + 17, :] = jnp.where(side == 0, edge, 0.0)


def stencil(main_ref, ext_ref, pad_ref):
    lane = lax.broadcasted_iota(jnp.int32, (CY, 128), 1)
    total = [jnp.zeros((CY, 128), F32) for _ in range(3)]
    for dx in range(3):
        for dy in range(3):
            for b in range(3):
                start = (dx * 3 + b) * 24 + 7 + dy
                here = pad_ref[start : start + CY, :]
                left = jnp.where(lane == 0, 0.0, pltpu.roll(here, 1, 1))
                right = jnp.where(lane == 127, 0.0, pltpu.roll(here, 127, 1))
                for dz, moved in enumerate((left, here, right)):
                    for a in range(3):
                        q = ((dx * 9 + dy * 3 + dz) * 3 + a) * 3 + b
                        if q < 240:
                            row = (3 * K + q) * CY
                            total[a] = total[a] + main_ref[row : row + CY, :] * moved
                        else:
                            row = (q - 240) * CY
                            total[a] = total[a] + ext_ref[row : row + CY, :] * moved
    return total


def image_kernel(count, place_ref, main_ref, ext_ref, line_ref, first_ref, second_ref, *refs):
    vectors, (image_ref, send_ref, pad_ref, part_ref) = refs[:count], refs[count:]
    side = place_ref[0:1, :]
    even = place_ref[1:2, :] == 0
    first, second = first_ref[...], second_ref[...]
    up, down = jnp.where(even, second, first), jnp.where(even, first, second)
    put_plane(pad_ref, 0, up[0:24], up[24:32], side)
    put_plane(pad_ref, 1, vectors[-1][0:24, :], line_ref[...], side)
    put_plane(pad_ref, 2, down[0:24], down[24:32], side)
    image = stencil(main_ref, ext_ref, pad_ref)
    for a in range(3):
        image_ref[a * CY : (a + 1) * CY, :] = image[a]
    for m in range(K):
        rows = [(a * K + m) * CY for a in range(3)]
        part_ref[m * CY : (m + 1) * CY, :] = sum(
            main_ref[row : row + CY, :] * image[a] for a, row in enumerate(rows)
        )
    others = [image] + [[ref[a * CY : (a + 1) * CY, :] for a in range(3)] for ref in vectors]
    for i in range(8):
        m = K + i
        if i < len(others):
            part_ref[m * CY : (m + 1) * CY, :] = sum(o * w for o, w in zip(others[i], image))
        else:
            part_ref[m * CY : (m + 1) * CY, :] = jnp.zeros((CY, 128), F32)
    part = sum(part_ref[pl.ds(y, K + 8, stride=CY), :] for y in range(CY))
    part = jnp.concatenate([part, jnp.zeros((128 - K - 8, 128), F32)], axis=0)
    send_ref[...] = exact_dot(jnp.ones((PEERS, 128), F32), part, NT)


def totals(got_ref):
    return exact_dot(got_ref[...], jnp.ones((PEERS, 128), F32), TN)


def next_kernel(place_ref, got_ref, main_ref, image_ref, one_ref, inv_ref, v_ref, line_ref, weights_ref, h_ref):
    sums = totals(got_ref)
    weights = exact_dot(inv_ref[...], sums)
    h11 = sums[K + 1 : K + 2, :]
    along = jnp.sum(sums[0:K] * weights, axis=0, keepdims=True)
    h21 = jnp.sqrt(sums[K : K + 1, :] - along - h11 * h11)
    begin = [
        image_ref[a * CY : (a + 1) * CY, :] - h11 * one_ref[a * CY : (a + 1) * CY, :] for a in range(3)
    ]
    vector = minus_combined(begin, main_ref, weights)
    put_vector([v / h21 for v in vector], place_ref, v_ref, line_ref)
    weights_ref[...] = weights
    h_ref[...] = jnp.zeros((8, 128), F32)
    h_ref[0:1, :] = h11
    h_ref[1:2, :] = h21


def send_kernel(got_ref, inv_ref, start_ref, first_ref, h_ref, beta_ref, u_ref, info_ref, wire_ref, y_ref):
    sums = totals(got_ref)
    weights = exact_dot(inv_ref[...], sums)
    h11, h21 = h_ref[0:1, :], h_ref[1:2, :]
    h12, h22 = sums[K + 1 : K + 2, :], sums[K + 2 : K + 3, :]
    along = jnp.sum(sums[0:K] * weights, axis=0, keepdims=True)
    h32 = jnp.sqrt(sums[K : K + 1, :] - along - h12 * h12 - h22 * h22)
    beta = beta_ref[0:1, :]
    m11 = h11 * h11 + h21 * h21
    m12 = h11 * h12 + h21 * h22
    m22 = h12 * h12 + h22 * h22 + h32 * h32
    g_one = beta * h11
    g_two = beta * h12
    determ = m11 * m22 - m12 * m12
    y_one = (m22 * g_one - m12 * g_two) / determ
    y_two = (m11 * g_two - m12 * g_one) / determ
    y_ref[...] = jnp.zeros((8, 128), F32)
    y_ref[0:1, :] = y_one
    y_ref[1:2, :] = y_two
    weights = start_ref[...] - y_one * first_ref[...] - y_two * weights
    wide = jnp.concatenate([weights] * (ROWS // 128), axis=1)
    target, rank, local = (info_ref[i : i + 1, :] for i in range(3))
    at_rank = lax.broadcasted_iota(jnp.int32, (SLOTS, ROWS), 0) == rank
    rows = [jnp.sum(u_ref[a * K : (a + 1) * K, :] * wide, axis=0, keepdims=True) for a in range(3)]
    rows = jnp.concatenate([jnp.where(at_rank, r, 0.0) for r in rows + [local.astype(F32)]], axis=0)
    rows = jnp.concatenate(split(rows), axis=0)
    onehot = lax.broadcasted_iota(jnp.int32, (PEERS, ROWS), 0) == target
    onehot = jnp.where(onehot, 1.0, 0.0).astype(BF16)
    mine = lax.dot_general(onehot, rows, NT, preferred_element_type=F32)
    mine = mine + pltpu.roll(mine, 64, 1)
    peer = lax.broadcasted_iota(jnp.int32, (PEERS, 128), 0)
    lane = lax.broadcasted_iota(jnp.int32, (PEERS, 128), 1)
    other = jnp.where(peer % 2 == 0, pltpu.roll(mine, PEERS - 1, 0), pltpu.roll(mine, 1, 0))
    pair = jnp.where(lane < 64, mine, other)
    wire_ref[pl.ds(0, PEERS, stride=3), :] = jnp.where(peer < 2, 0.0, pltpu.roll(pair, 2, 0))
    wire_ref[pl.ds(1, PEERS, stride=3), :] = pair
    wire_ref[pl.ds(2, PEERS, stride=3), :] = jnp.where(peer >= PEERS - 2, 0.0, pltpu.roll(pair, PEERS - 2, 0))


def last_kernel(
    place_ref, got_ref, main_ref, ext_ref, y_ref, one_ref, two_ref, im_one_ref, im_two_ref,
    sol_ref, res_ref, left_ref, right_ref, pad_ref,
):
    side = place_ref[0:1, :]
    for dx in range(3):
        got = got_ref[pl.ds(dx, PEERS, stride=3), :].T
        own, other = two_level(
            [(got[base : base + 48], got[base + 48 : base + 64]) for base in (0, 64)],
            left_ref.at[dx],
            right_ref.at[dx],
        )
        lines = [
            jnp.where(side == 0, other[a * CY : a * CY + 1, :], other[a * CY + 7 : a * CY + 8, :]) for a in range(3)
        ]
        put_plane(pad_ref, dx, own, jnp.concatenate(lines, axis=0), side)
        if dx == 1:
            term = own
    image = stencil(main_ref, ext_ref, pad_ref)
    y_one, y_two = y_ref[0:1, :], y_ref[1:2, :]
    solution = term + y_one * one_ref[0:24, :] + y_two * two_ref[0:24, :]
    for a in range(3):
        rows = slice(a * CY, (a + 1) * CY)
        residual = ext_ref[24 + a * CY : 24 + (a + 1) * CY, :] - image[a]
        residual = residual - y_one * im_one_ref[rows, :] - y_two * im_two_ref[rows, :]
        for y in range(CY):
            cols = slice(y * CZ, (y + 1) * CZ)
            sol_ref[a : a + 1, cols] = solution[a * CY + y : a * CY + y + 1, :]
            res_ref[a : a + 1, cols] = residual[y : y + 1, :]


def shape(*dims, dtype=F32):
    return jax.ShapeDtypeStruct(dims, dtype)


def specs(*spaces):
    return tuple(pl.BlockSpec(memory_space=space) for space in spaces)


def call(kernel, outs, scratch=(), inputs=0, in_specs=None, out_specs=None, limit=40):
    vmem = pltpu.VMEM
    return pl.pallas_call(
        kernel,
        out_shape=outs,
        in_specs=in_specs or specs(*[vmem] * inputs),
        out_specs=out_specs or specs(*[vmem] * len(outs)),
        scratch_shapes=list(scratch),
        compiler_params=pltpu.CompilerParams(vmem_limit_bytes=limit * 2**20),
    )


def exchange(rows):
    count = rows.shape[0] // PEERS
    shaped = rows.reshape(PEERS, count, 1, 128)
    got = lax.all_to_all(shaped, GX_GY, split_axis=0, concat_axis=0, tiled=True)
    return got.reshape(PEERS * count, 128)


def swap(plane, first):
    pairs = [(i, i + 1) for i in range(first, N_GX - 1, 2)]
    return lax.ppermute(plane, GX, pairs + [(j, i) for i, j in pairs])


def halo(vector, line):
    other = lax.ppermute(line, "gy", [(0, 1), (1, 0)])
    plane = lax.dynamic_update_slice(vector, other, (24, 0))
    return other, swap(plane, 0), swap(plane, 1)


def body(operator, basis_u, basis_c, right_side, new_rows):
    row = lax.broadcasted_iota(jnp.int32, (8, 128), 0)
    place = jnp.where(row == 0, lax.axis_index("gy"), lax.axis_index(GX) % 2).astype(jnp.int32)
    vmem, hbm = pltpu.VMEM, pltpu.HBM
    wire, info = call(
        pack_kernel,
        (shape(PEERS * WIRE, 128), shape(8, ROWS, dtype=jnp.int32)),
        [
            vmem((243, ROWS), F32),
            vmem((144, ROWS), F32),
            vmem((3, ROWS), F32),
            vmem((1, ROWS), jnp.int32),
            vmem((ROWS, 2 * MAIN), BF16),
            vmem((128, ROWS), F32),
            vmem((56, 128), F32),
            vmem((PEERS * WIRE, 128), F32),
            pltpu.SemaphoreType.DMA((4,)),
            pltpu.SemaphoreType.DMA((CHUNKS,)),
        ],
        in_specs=specs(hbm, hbm, hbm, hbm),
        out_specs=specs(hbm, vmem),
        limit=56,
    )(operator, basis_c, right_side, new_rows.reshape(1, ROWS))
    got = exchange(wire)
    vector_outs = (shape(32, 128), shape(8, 128))
    main, ext, one, line, inverse, start, beta = call(
        unpack_kernel,
        (shape(MAIN * CY, 128), shape(48, 128), *vector_outs, shape(K, 128), shape(K, 128), shape(8, 128)),
        [
            vmem((PEERS * WIRE, 128), F32),
            vmem((2, ROWS, SLOTS * PEERS // 2), BF16),
            vmem((2, 3, SLOTS * PEERS // 2, 256), BF16),
            vmem((3, ROWS, 128), F32),
            vmem((48, SLOTS * PEERS), F32),
            vmem((128, SLOTS * PEERS), BF16),
            vmem((56, 128), F32),
            pltpu.SemaphoreType.DMA((2,)),
        ],
        in_specs=specs(vmem, hbm),
        limit=40,
    )(place, got)
    pad = vmem((9 * 24, 128), F32)
    image_scratch = [pad, vmem(((K + 8) * CY, 128), F32)]
    image_outs = (shape(3 * CY, 128), shape(PEERS, 128))
    image_one, send = call(functools.partial(image_kernel, 1), image_outs, image_scratch, inputs=7)(
        place, main, ext, *halo(one, line), one
    )
    sums = exchange(send)
    two, line, weights, h_one = call(
        next_kernel, (*vector_outs, shape(K, 128), shape(8, 128)), inputs=6
    )(place, sums, main, image_one, one, inverse)
    image_two, send = call(functools.partial(image_kernel, 2), image_outs, image_scratch, inputs=8)(
        place, main, ext, *halo(two, line), one, two
    )
    sums = exchange(send)
    wire, y = call(send_kernel, (shape(PEERS * 3, 128), shape(8, 128)), inputs=8)(
        sums, inverse, start, weights, h_one, beta, basis_u, info
    )
    got = exchange(wire)
    return call(
        last_kernel,
        (shape(3, ROWS), shape(3, ROWS)),
        [vmem((3, 48, SLOTS * PEERS), F32), vmem((3, 256, SLOTS * PEERS), BF16), pad],
        inputs=9,
    )(place, got, main, ext, y, one, two, image_one, image_two)


def solution(mesh):
    torus = Mesh(mesh.devices.reshape(4, 4, 4, mesh.shape["gy"]), ("gx_0", "gx_1", "gx_2", "gy"))
    placed = (P(None, GX_GY), P(None, GX_GY), P(None, GX_GY), P(None, GX_GY), P(GX_GY))
    return jax.shard_map(
        body,
        mesh=torus,
        in_specs=placed,
        out_specs=(P(None, GX_GY), P(None, GX_GY)),
        check_vma=False,
    )
```

```python
import functools

import jax
import jax.numpy as jnp
from jax import lax
from jax.experimental import pallas as pl
from jax.experimental.pallas import tpu as pltpu
from jax.sharding import Mesh
from jax.sharding import PartitionSpec as P

CY = 8
CZ = 128
K = 48
SLOTS = 16
PEERS = 128
ROWS = 1024
N_GX = 64
GX_GY = ("gx_0", "gx_1", "gx_2", "gy")
GX = ("gx_0", "gx_1", "gx_2")
F32 = jnp.float32
BF16 = jnp.bfloat16
HIGHEST = lax.Precision.HIGHEST
SIDE = K + 1
BANDS = 25
GRAM = 10
WIRE = 49 + GRAM
CHUNKS = 8
NT = (((1,), (1,)), ((), ()))
TN = (((0,), (0,)), ((), ()))
MAIN = 3 * 128


def split(x):
    high = x.astype(BF16)
    return high, (x - high.astype(F32)).astype(BF16)


def exact_dot(x, y, dims=(((1,), (0,)), ((), ()))):
    return lax.dot_general(x, y, dims, precision=HIGHEST, preferred_element_type=F32)


def chosen(mask):
    return jnp.where(mask, jnp.ones(mask.shape, BF16), jnp.zeros(mask.shape, BF16))


def half_sum(x):
    return x[:, :128] + x[:, 128:]


def squared(x):
    x = jnp.concatenate([x, jnp.zeros((64, 64), F32)], axis=1)
    return jnp.concatenate([x, jnp.zeros((64, 128), F32)], axis=0)


def folded(rows, start_ref):
    twice = rows + pltpu.roll(rows, SIDE, 1)
    sub = lax.broadcasted_iota(jnp.int32, (8, 128), 0)
    for tile in range(7):
        here = twice[tile * 8 : (tile + 1) * 8]
        total = jnp.zeros((8, 128), F32)
        for r in range(8):
            i = tile * 8 + r
            if i < SIDE:
                moved = pltpu.roll(here, (128 - i + BANDS * (i // GRAM)) % 128, 1)
                total = jnp.where(sub == r, moved, total)
        start_ref[tile * 8 : (tile + 1) * 8, :] = total
    lane = lax.broadcasted_iota(jnp.int32, (GRAM, 128), 1)
    return sum(
        jnp.where(lane // BANDS == g, start_ref[g * GRAM : (g + 1) * GRAM, :], 0.0) for g in range(5)
    )


def unfolded(bands, start_ref):
    sub = lax.broadcasted_iota(jnp.int32, (8, 128), 0)
    lane = lax.broadcasted_iota(jnp.int32, (GRAM, 128), 1)
    start_ref[48:56, :] = jnp.zeros((8, 128), F32)
    for g in range(5):
        start_ref[g * GRAM : (g + 1) * GRAM, :] = jnp.where(lane // BANDS == g, bands, 0.0)
    tiles = []
    for tile in range(7):
        here = start_ref[tile * 8 : (tile + 1) * 8, :]
        total = jnp.zeros((8, 128), F32)
        for r in range(8):
            i = tile * 8 + r
            if i < SIDE:
                moved = pltpu.roll(here, (128 + i - BANDS * (i // GRAM)) % 128, 1)
                total = jnp.where(sub == r, moved, total)
        tiles.append(total)
    half = jnp.concatenate(tiles + [jnp.zeros((72, 128), F32)], axis=0)
    row = lax.broadcasted_iota(jnp.int32, (128, 128), 0)
    lane = lax.broadcasted_iota(jnp.int32, (128, 128), 1)
    half = jnp.where(lane < SIDE, half + pltpu.roll(half, 128 - SIDE, 1), 0.0)
    return half + jnp.where(row == lane, 0.0, half.T)


def pieces(source, target, size):
    count = source.shape[0]
    parts = [pl.ds(i, min(size, count - i)) for i in range(0, count, size)]
    return [(source.at[part], target.at[part]) for part in parts]


def pack_kernel(
    op_hbm, c_hbm, b_hbm, rows_hbm, wire_hbm, info_ref,
    op_ref, c_ref, b_ref, rows_ref, p_ref, a_ref, fold_ref, wire_ref, in_sem, out_sem,
):
    copies = [
        pltpu.make_async_copy(source, target, in_sem.at[i])
        for i, (source, target) in enumerate(
            [(rows_hbm, rows_ref), (b_hbm, b_ref), *pieces(c_hbm, c_ref, 72), *pieces(op_hbm, op_ref, 128)]
        )
    ]
    for copy in copies:
        copy.start()
    copies[0].wait()
    new_rows = rows_ref[...]
    target = new_rows // ROWS
    local = new_rows % ROWS
    onehot = lax.broadcasted_iota(jnp.int32, (PEERS, ROWS), 0) == target
    onehot_f = jnp.where(onehot, 1.0, 0.0).astype(F32)
    onehot_b = onehot_f.astype(BF16)
    before = lax.broadcasted_iota(jnp.int32, (128, 128), 0) < lax.broadcasted_iota(jnp.int32, (128, 128), 1)
    before = jnp.where(before, 1.0, 0.0).astype(BF16)
    ones = jnp.ones((128, 128), BF16)
    seen = jnp.zeros((PEERS, 128), F32)
    ranks = []
    for block in range(ROWS // 128):
        part = onehot_b[:, block * 128 : (block + 1) * 128]
        count = jnp.dot(part, before, preferred_element_type=F32) + seen
        ranks.append(jnp.sum(onehot_f[:, block * 128 : (block + 1) * 128] * count, axis=0, keepdims=True))
        seen = seen + jnp.dot(part, ones, preferred_element_type=F32)
    rank = jnp.concatenate(ranks, axis=1)
    rank_at = jnp.where(onehot, rank, -1.0).astype(BF16)
    info_ref[0:1, :] = target
    info_ref[1:2, :] = rank.astype(jnp.int32)
    info_ref[2:3, :] = local
    info_ref[3:8, :] = jnp.zeros((5, ROWS), jnp.int32)
    for copy in copies[1:]:
        copy.wait()
    middle = jnp.concatenate([c_ref[128:144, :], op_ref[0:112, :]], axis=0)
    for tile, x in enumerate((c_ref[0:128, :], middle, op_ref[112:240, :])):
        p_ref[:, tile * 256 : tile * 256 + 128], p_ref[:, tile * 256 + 128 : (tile + 1) * 256] = split(x.T)
    sums, low = jnp.zeros((192, 64), F32), jnp.zeros((64, 64), F32)
    for a in range(3):
        a_ref[a, 48:64, :] = jnp.zeros((16, ROWS), F32)
        a_ref[a, 0:48, :] = c_ref[a * K : (a + 1) * K, :]
        a_ref[a, 48:49, :] = b_ref[a : a + 1, :]
        one, two = split(a_ref[a])
        three = (a_ref[a] - one.astype(F32) - two.astype(F32)).astype(BF16)
        terms = jnp.concatenate([one, two, three], axis=0)
        sums = sums + lax.dot_general(terms, one, NT, preferred_element_type=F32)
        low = low + lax.dot_general(two, two, NT, preferred_element_type=F32)
    cross = squared(sums[64:128] + sums[128:192])
    gram = squared(sums[0:64] + low) + cross + cross.T
    bands = folded(gram[0:64], fold_ref)
    for i in range(GRAM):
        wire_ref[pl.ds(49 + i, PEERS, stride=WIRE), :] = jnp.broadcast_to(bands[i : i + 1, :], (PEERS, 128))

    at_rank = lax.broadcasted_iota(jnp.int32, (SLOTS, ROWS), 0).astype(F32) == rank
    rest = [op_ref[240 + i : 241 + i, :] for i in range(3)] + [b_ref[i : i + 1, :] for i in range(3)]
    rest = [jnp.where(at_rank, row, 0.0) for row in rest + [local.astype(F32)]]
    rest = jnp.concatenate(rest + [jnp.zeros((SLOTS, ROWS), F32)], axis=0)
    rest = jnp.concatenate(split(rest), axis=0)
    wire_ref[pl.ds(48, PEERS, stride=WIRE), :] = half_sum(
        lax.dot_general(onehot_b, rest, NT, preferred_element_type=F32)
    )
    sent = []
    count = PEERS // CHUNKS
    for chunk in range(CHUNKS):
        mine = rank_at[chunk * count : (chunk + 1) * count]
        choice = [chosen(mine == k) for k in range(SLOTS)]
        moved = jnp.dot(jnp.concatenate(choice, axis=0), p_ref[...], preferred_element_type=F32)
        for tile in range(3):
            both = half_sum(moved[:, tile * 256 : (tile + 1) * 256])
            for k in range(SLOTS):
                wire_ref[pl.ds(chunk * count * WIRE + tile * SLOTS + k, count, stride=WIRE), :] = both[
                    k * count : (k + 1) * count
                ]
        rows = pl.ds(chunk * count * WIRE, count * WIRE)
        sent.append(pltpu.make_async_copy(wire_ref.at[rows], wire_hbm.at[rows], out_sem.at[chunk]))
        sent[-1].start()
    for copy in sent:
        copy.wait()


def two_level(groups, left_ref, right_ref):
    eight = lax.broadcasted_iota(jnp.int32, (CY, 128), 0)
    deep = lax.broadcasted_iota(jnp.int32, (128, 128), 0).astype(F32).astype(BF16)
    count = groups[0][0].shape[0] // SLOTS
    for g, (values, labels) in enumerate(groups):
        labels = labels.astype(jnp.int32)
        y, z = labels // CZ, (labels % CZ).astype(F32)
        for k in range(SLOTS):
            cols = slice(k * 128, (k + 1) * 128)
            row = jnp.broadcast_to(z[k : k + 1], (128, 128)).astype(BF16)
            right_ref[g * 128 : (g + 1) * 128, cols] = chosen(deep == row)
            here = eight == y[k : k + 1]
            for c in range(count):
                row = (g * count + c) * CY
                value = values[c * SLOTS + k : c * SLOTS + k + 1]
                left_ref[row : row + CY, cols] = jnp.where(here, value, 0.0)
    rows = len(groups) * count * CY
    left = jnp.concatenate(split(left_ref[...]), axis=0)
    moved = lax.dot_general(left, right_ref[...], NT, preferred_element_type=F32)
    moved = moved[0:rows] + moved[rows:]
    size = count * CY
    return [moved[g * size : (g + 1) * size, g * 128 : (g + 1) * 128] for g in range(len(groups))]


def minus_combined(start, main_ref, weights):
    result = []
    for a in range(3):
        total = start[a]
        for m in range(K):
            row = (a * K + m) * CY
            total = total - main_ref[row : row + CY, :] * weights[m : m + 1, :]
        result.append(total)
    return result


def put_vector(vector, lines, v_ref):
    v_ref[24:32, :] = jnp.zeros((8, 128), F32)
    for a in range(3):
        v_ref[a * CY : (a + 1) * CY, :] = vector[a]
        v_ref[24 + a : 25 + a, :] = lines[a]


def swept(work, begin, count):
    row_id = lax.broadcasted_iota(jnp.int32, (K, 128), 0)
    columns = [jnp.broadcast_to(work[:, j : j + 1], (K, 128)) for j in range(begin, begin + count)]
    for s in range(count):
        j = begin + s
        column = columns[s]
        inverse = 1.0 / column[j : j + 1, :]
        here = row_id == j

        def step(x):
            pivot = x[j : j + 1, :] * inverse
            return jnp.where(here, pivot, x - column * pivot)

        work = step(work)
        columns = columns[: s + 1] + [step(c) for c in columns[s + 1 :]]
    return work


def unpack_kernel(
    place_ref, wire_hbm, main_ref, ext_ref, v_ref, inv_ref, start_ref, beta_ref,
    wire_ref, t_ref, r_ref, part_ref, left_ref, right_ref, fold_ref, in_sem,
):
    half = PEERS // 2
    copies = []
    for part in range(2):
        rows = pl.ds(part * half * WIRE, half * WIRE)
        copies.append(pltpu.make_async_copy(wire_hbm.at[rows], wire_ref.at[rows], in_sem.at[part]))
        copies[-1].start()
    deep = lax.broadcasted_iota(jnp.int32, (CZ, 128), 0).astype(F32).astype(BF16)
    for part in range(2):
        copies[part].wait()
        if part == 1:
            bands = [
                jnp.sum(wire_ref[pl.ds(49 + i, PEERS, stride=WIRE), :], axis=0, keepdims=True) for i in range(GRAM)
            ]
            gram = unfolded(jnp.concatenate(bands, axis=0), fold_ref)
            load_sq = jnp.broadcast_to(gram[48:49, 48:49], (1, 128))
            row_id = lax.broadcasted_iota(jnp.int32, (K, 128), 0)
            lane = lax.broadcasted_iota(jnp.int32, (K, 128), 1)
            raw = jnp.broadcast_to(gram[0:K, K : K + 1], (K, 128))
            work = jnp.where(lane < K + 1, gram[0:K], jnp.where(lane - 64 == row_id, 1.0, 0.0))
            for begin in range(0, K, 4):
                work = swept(work, begin, 4)
        first = part * half * WIRE
        labels = wire_ref[pl.ds(first + 48, half, stride=WIRE), :].T[6 * SLOTS : 7 * SLOTS]
        labels = jnp.concatenate([labels[0:8], labels[8:16]], axis=1).astype(jnp.int32)
        label_y, label_z = (labels // CZ).astype(F32), (labels % CZ).astype(F32)
        for i in range(8):
            here = deep == jnp.broadcast_to(label_z[i : i + 1], (CZ, 128)).astype(BF16)
            here = chosen(here)
            row = jnp.broadcast_to(label_y[i : i + 1], (CZ, 128)).astype(BF16)
            for y in range(CY):
                t_ref[part, y * CZ : (y + 1) * CZ, i * 128 : (i + 1) * 128] = jnp.where(
                    row == y, here, jnp.zeros((CZ, 128), BF16)
                )
        for tile in range(3):
            for k in range(SLOTS):
                high, low = split(wire_ref[pl.ds(first + tile * SLOTS + k, half, stride=WIRE), :])
                row = k % 8 * 128 + k // 8 * half
                r_ref[part, tile, row : row + half, 0:128] = high
                r_ref[part, tile, row : row + half, 128:256] = low
            moved = half_sum(jnp.dot(t_ref[part], r_ref[part, tile], preferred_element_type=F32))
            if part == 0:
                part_ref[tile] = moved
                continue
            moved = moved + part_ref[tile]
            for y in range(CY):
                main_ref[pl.ds(tile * 128 * CY + y, 128, stride=CY), :] = moved[y * CZ : (y + 1) * CZ].T
    rest = wire_ref[pl.ds(48, PEERS, stride=WIRE), :].T
    labels = rest[6 * SLOTS : 7 * SLOTS]
    [ext] = two_level([(rest[0 : 6 * SLOTS], labels)], left_ref, right_ref)
    ext_ref[...] = ext

    inverse = jnp.where(lane < K, pltpu.roll(work, 64, 1), 0.0)
    weights = jnp.broadcast_to(work[:, K : K + 1], (K, 128))
    inv_ref[...] = inverse
    start_ref[...] = weights
    beta = jnp.sqrt(load_sq - jnp.sum(raw * weights, axis=0, keepdims=True))
    beta_ref[...] = jnp.broadcast_to(beta, (8, 128))
    load = [ext[24 + a * CY : 24 + (a + 1) * CY, :] for a in range(3)]
    vector = [v / beta for v in minus_combined(load, main_ref, weights)]
    lower = place_ref[0:1, :] == 0
    put_vector(vector, [jnp.where(lower, v[CY - 1 : CY], v[0:1]) for v in vector], v_ref)


def put_plane(pad_ref, dx, plane, line, side):
    for a in range(3):
        base = (dx * 3 + a) * 24
        edge = line[a : a + 1, :]
        pad_ref[base + 7 : base + 8, :] = jnp.where(side == 1, edge, 0.0)
        pad_ref[base + 8 : base + 16, :] = plane[a * CY : (a + 1) * CY, :]
        pad_ref[base + 16 : base + 17, :] = jnp.where(side == 0, edge, 0.0)


def stencil(main_ref, ext_ref, pad_ref):
    lane = lax.broadcasted_iota(jnp.int32, (CY, 128), 1)
    total = [jnp.zeros((CY, 128), F32) for _ in range(3)]
    for dx in range(3):
        for dy in range(3):
            for b in range(3):
                start = (dx * 3 + b) * 24 + 7 + dy
                here = pad_ref[start : start + CY, :]
                left = jnp.where(lane == 0, 0.0, pltpu.roll(here, 1, 1))
                right = jnp.where(lane == 127, 0.0, pltpu.roll(here, 127, 1))
                for dz, moved in enumerate((left, here, right)):
                    for a in range(3):
                        q = ((dx * 9 + dy * 3 + dz) * 3 + a) * 3 + b
                        if q < 240:
                            row = (3 * K + q) * CY
                            total[a] = total[a] + main_ref[row : row + CY, :] * moved
                        else:
                            row = (q - 240) * CY
                            total[a] = total[a] + ext_ref[row : row + CY, :] * moved
    return total


def image_kernel(count, place_ref, main_ref, ext_ref, first_ref, second_ref, *refs):
    vectors, (image_ref, send_ref, *edges, pad_ref, part_ref) = refs[:count], refs[count:]
    side = place_ref[0:1, :]
    even = place_ref[1:2, :] == 0
    first, second = first_ref[...], second_ref[...]
    up, down = jnp.where(even, second, first), jnp.where(even, first, second)
    put_plane(pad_ref, 0, up[0:24], up[24:32], side)
    put_plane(pad_ref, 1, vectors[-1][0:24, :], vectors[-1][24:32, :], side)
    put_plane(pad_ref, 2, down[0:24], down[24:32], side)
    image = stencil(main_ref, ext_ref, pad_ref)
    for a in range(3):
        image_ref[a * CY : (a + 1) * CY, :] = image[a]
    for edge_ref in edges:
        last = main_ref[pl.ds(CY - 1, 3 * K, stride=CY), :]
        edge_ref[0 : 3 * K, :] = jnp.where(side == 0, last, main_ref[pl.ds(0, 3 * K, stride=CY), :])
        edge_ref[3 * K :, :] = jnp.zeros((8, 128), F32)
        for a in range(3):
            row = 3 * K + a
            edge_ref[row : row + 1, :] = jnp.where(side == 0, image[a][CY - 1 : CY], image[a][0:1])
    for m in range(K):
        rows = [(a * K + m) * CY for a in range(3)]
        part_ref[m * CY : (m + 1) * CY, :] = sum(
            main_ref[row : row + CY, :] * image[a] for a, row in enumerate(rows)
        )
    others = [image] + [[ref[a * CY : (a + 1) * CY, :] for a in range(3)] for ref in vectors]
    for i in range(8):
        m = K + i
        if i < len(others):
            part_ref[m * CY : (m + 1) * CY, :] = sum(o * w for o, w in zip(others[i], image))
        else:
            part_ref[m * CY : (m + 1) * CY, :] = jnp.zeros((CY, 128), F32)
    part = sum(part_ref[pl.ds(y, K + 8, stride=CY), :] for y in range(CY))
    part = jnp.concatenate([part, jnp.zeros((128 - K - 8, 128), F32)], axis=0)
    send_ref[...] = exact_dot(jnp.ones((PEERS, 128), F32), part, NT)


def totals(got_ref):
    return exact_dot(got_ref[...], jnp.ones((PEERS, 128), F32), TN)


def next_kernel(got_ref, main_ref, image_ref, one_ref, other_ref, inv_ref, v_ref, weights_ref, h_ref):
    sums = totals(got_ref)
    weights = exact_dot(inv_ref[...], sums)
    h11 = sums[K + 1 : K + 2, :]
    along = jnp.sum(sums[0:K] * weights, axis=0, keepdims=True)
    h21 = jnp.sqrt(sums[K : K + 1, :] - along - h11 * h11)
    begin = [
        image_ref[a * CY : (a + 1) * CY, :] - h11 * one_ref[a * CY : (a + 1) * CY, :] for a in range(3)
    ]
    vector = [v / h21 for v in minus_combined(begin, main_ref, weights)]
    lines = []
    for a in range(3):
        along_line = jnp.sum(other_ref[a * K : (a + 1) * K, :] * weights, axis=0, keepdims=True)
        line = other_ref[3 * K + a : 3 * K + a + 1, :] - along_line - h11 * one_ref[24 + a : 25 + a, :]
        lines.append(line / h21)
    put_vector(vector, lines, v_ref)
    weights_ref[...] = weights
    h_ref[...] = jnp.zeros((8, 128), F32)
    h_ref[0:1, :] = h11
    h_ref[1:2, :] = h21


def send_kernel(got_ref, inv_ref, start_ref, first_ref, h_ref, beta_ref, u_ref, info_ref, wire_ref, y_ref):
    sums = totals(got_ref)
    weights = exact_dot(inv_ref[...], sums)
    h11, h21 = h_ref[0:1, :], h_ref[1:2, :]
    h12, h22 = sums[K + 1 : K + 2, :], sums[K + 2 : K + 3, :]
    along = jnp.sum(sums[0:K] * weights, axis=0, keepdims=True)
    h32 = jnp.sqrt(sums[K : K + 1, :] - along - h12 * h12 - h22 * h22)
    beta = beta_ref[0:1, :]
    m11 = h11 * h11 + h21 * h21
    m12 = h11 * h12 + h21 * h22
    m22 = h12 * h12 + h22 * h22 + h32 * h32
    g_one = beta * h11
    g_two = beta * h12
    determ = m11 * m22 - m12 * m12
    y_one = (m22 * g_one - m12 * g_two) / determ
    y_two = (m11 * g_two - m12 * g_one) / determ
    y_ref[...] = jnp.zeros((8, 128), F32)
    y_ref[0:1, :] = y_one
    y_ref[1:2, :] = y_two
    weights = start_ref[...] - y_one * first_ref[...] - y_two * weights
    wide = jnp.concatenate([weights] * (ROWS // 128), axis=1)
    target, rank, local = (info_ref[i : i + 1, :] for i in range(3))
    at_rank = lax.broadcasted_iota(jnp.int32, (SLOTS, ROWS), 0) == rank
    rows = [jnp.sum(u_ref[a * K : (a + 1) * K, :] * wide, axis=0, keepdims=True) for a in range(3)]
    rows = jnp.concatenate([jnp.where(at_rank, r, 0.0) for r in rows + [local.astype(F32)]], axis=0)
    rows = jnp.concatenate(split(rows), axis=0)
    onehot = lax.broadcasted_iota(jnp.int32, (PEERS, ROWS), 0) == target
    onehot = jnp.where(onehot, 1.0, 0.0).astype(BF16)
    mine = lax.dot_general(onehot, rows, NT, preferred_element_type=F32)
    mine = mine + pltpu.roll(mine, 64, 1)
    peer = lax.broadcasted_iota(jnp.int32, (PEERS, 128), 0)
    lane = lax.broadcasted_iota(jnp.int32, (PEERS, 128), 1)
    other = jnp.where(peer % 2 == 0, pltpu.roll(mine, PEERS - 1, 0), pltpu.roll(mine, 1, 0))
    pair = jnp.where(lane < 64, mine, other)
    wire_ref[pl.ds(0, PEERS, stride=3), :] = jnp.where(peer < 2, 0.0, pltpu.roll(pair, 2, 0))
    wire_ref[pl.ds(1, PEERS, stride=3), :] = pair
    wire_ref[pl.ds(2, PEERS, stride=3), :] = jnp.where(peer >= PEERS - 2, 0.0, pltpu.roll(pair, PEERS - 2, 0))


def last_kernel(
    place_ref, got_ref, main_ref, ext_ref, y_ref, one_ref, two_ref, im_one_ref, im_two_ref,
    sol_ref, res_ref, left_ref, right_ref, pad_ref,
):
    side = place_ref[0:1, :]
    for dx in range(3):
        got = got_ref[pl.ds(dx, PEERS, stride=3), :].T
        own, other = two_level(
            [(got[base : base + 48], got[base + 48 : base + 64]) for base in (0, 64)],
            left_ref.at[dx],
            right_ref.at[dx],
        )
        lines = [
            jnp.where(side == 0, other[a * CY : a * CY + 1, :], other[a * CY + 7 : a * CY + 8, :]) for a in range(3)
        ]
        put_plane(pad_ref, dx, own, jnp.concatenate(lines, axis=0), side)
        if dx == 1:
            term = own
    image = stencil(main_ref, ext_ref, pad_ref)
    y_one, y_two = y_ref[0:1, :], y_ref[1:2, :]
    solution = term + y_one * one_ref[0:24, :] + y_two * two_ref[0:24, :]
    for a in range(3):
        rows = slice(a * CY, (a + 1) * CY)
        residual = ext_ref[24 + a * CY : 24 + (a + 1) * CY, :] - image[a]
        residual = residual - y_one * im_one_ref[rows, :] - y_two * im_two_ref[rows, :]
        for y in range(CY):
            cols = slice(y * CZ, (y + 1) * CZ)
            sol_ref[a : a + 1, cols] = solution[a * CY + y : a * CY + y + 1, :]
            res_ref[a : a + 1, cols] = residual[y : y + 1, :]


def shape(*dims, dtype=F32):
    return jax.ShapeDtypeStruct(dims, dtype)


def specs(*spaces):
    return tuple(pl.BlockSpec(memory_space=space) for space in spaces)


def call(kernel, outs, scratch=(), inputs=0, in_specs=None, out_specs=None, limit=40):
    vmem = pltpu.VMEM
    return pl.pallas_call(
        kernel,
        out_shape=outs,
        in_specs=in_specs or specs(*[vmem] * inputs),
        out_specs=out_specs or specs(*[vmem] * len(outs)),
        scratch_shapes=list(scratch),
        compiler_params=pltpu.CompilerParams(vmem_limit_bytes=limit * 2**20),
    )


def exchange(rows):
    count = rows.shape[0] // PEERS
    shaped = rows.reshape(PEERS, count, 1, 128)
    got = lax.all_to_all(shaped, GX_GY, split_axis=0, concat_axis=0, tiled=True)
    return got.reshape(PEERS * count, 128)


def swap(plane, first):
    pairs = [(i, i + 1) for i in range(first, N_GX - 1, 2)]
    return lax.ppermute(plane, GX, pairs + [(j, i) for i, j in pairs])


def other_core(x):
    return lax.ppermute(x, "gy", [(0, 1), (1, 0)])


def body(operator, basis_u, basis_c, right_side, new_rows):
    row = lax.broadcasted_iota(jnp.int32, (8, 128), 0)
    place = jnp.where(row == 0, lax.axis_index("gy"), lax.axis_index(GX) % 2).astype(jnp.int32)
    vmem, hbm = pltpu.VMEM, pltpu.HBM
    wire, info = call(
        pack_kernel,
        (shape(PEERS * WIRE, 128), shape(8, ROWS, dtype=jnp.int32)),
        [
            vmem((243, ROWS), F32),
            vmem((144, ROWS), F32),
            vmem((3, ROWS), F32),
            vmem((1, ROWS), jnp.int32),
            vmem((ROWS, 2 * MAIN), BF16),
            vmem((3, 64, ROWS), F32),
            vmem((56, 128), F32),
            vmem((PEERS * WIRE, 128), F32),
            pltpu.SemaphoreType.DMA((6,)),
            pltpu.SemaphoreType.DMA((CHUNKS,)),
        ],
        in_specs=specs(hbm, hbm, hbm, hbm),
        out_specs=specs(hbm, vmem),
        limit=56,
    )(operator, basis_c, right_side, new_rows.reshape(1, ROWS))
    got = exchange(wire)
    plane = shape(32, 128)
    main, ext, one, inverse, start, beta = call(
        unpack_kernel,
        (shape(MAIN * CY, 128), shape(48, 128), plane, shape(K, 128), shape(K, 128), shape(8, 128)),
        [
            vmem((PEERS * WIRE, 128), F32),
            vmem((2, ROWS, SLOTS * PEERS // 2), BF16),
            vmem((2, 3, SLOTS * PEERS // 2, 256), BF16),
            vmem((3, ROWS, 128), F32),
            vmem((48, SLOTS * PEERS), F32),
            vmem((128, SLOTS * PEERS), BF16),
            vmem((56, 128), F32),
            pltpu.SemaphoreType.DMA((2,)),
        ],
        in_specs=specs(vmem, hbm),
        limit=40,
    )(place, got)
    pad = vmem((9 * 24, 128), F32)
    image_scratch = [pad, vmem(((K + 8) * CY, 128), F32)]
    image_outs = (shape(3 * CY, 128), shape(PEERS, 128))
    one = lax.dynamic_update_slice(one, other_core(one[24:32]), (24, 0))
    image_one, send, edge = call(
        functools.partial(image_kernel, 1), (*image_outs, shape(3 * K + 8, 128)), image_scratch, inputs=6
    )(place, main, ext, swap(one, 0), swap(one, 1), one)
    other = other_core(edge)
    sums = exchange(send)
    two, weights, h_one = call(next_kernel, (plane, shape(K, 128), shape(8, 128)), inputs=6)(
        sums, main, image_one, one, other, inverse
    )
    image_two, send = call(functools.partial(image_kernel, 2), image_outs, image_scratch, inputs=7)(
        place, main, ext, swap(two, 0), swap(two, 1), one, two
    )
    sums = exchange(send)
    wire, y = call(send_kernel, (shape(PEERS * 3, 128), shape(8, 128)), inputs=8)(
        sums, inverse, start, weights, h_one, beta, basis_u, info
    )
    got = exchange(wire)
    return call(
        last_kernel,
        (shape(3, ROWS), shape(3, ROWS)),
        [vmem((3, 48, SLOTS * PEERS), F32), vmem((3, 256, SLOTS * PEERS), BF16), pad],
        inputs=9,
    )(place, got, main, ext, y, one, two, image_one, image_two)


def solution(mesh):
    torus = Mesh(mesh.devices.reshape(4, 4, 4, mesh.shape["gy"]), ("gx_0", "gx_1", "gx_2", "gy"))
    placed = (P(None, GX_GY), P(None, GX_GY), P(None, GX_GY), P(None, GX_GY), P(GX_GY))
    return jax.shard_map(
        body,
        mesh=torus,
        in_specs=placed,
        out_specs=(P(None, GX_GY), P(None, GX_GY)),
        check_vma=False,
    )
```

```python
import functools

import jax
import jax.numpy as jnp
from jax import lax
from jax.experimental import pallas as pl
from jax.experimental.pallas import tpu as pltpu
from jax.sharding import Mesh
from jax.sharding import PartitionSpec as P

CY = 8
CZ = 128
K = 48
SLOTS = 16
PEERS = 128
ROWS = 1024
N_GX = 64
GX_GY = ("gx_0", "gx_1", "gx_2", "gy")
GX = ("gx_0", "gx_1", "gx_2")
F32 = jnp.float32
BF16 = jnp.bfloat16
HIGHEST = lax.Precision.HIGHEST
SIDE = K + 1
BANDS = 25
GRAM = 10
WIRE = 49 + GRAM
PARTS = 1
CHUNKS = 8
NT = (((1,), (1,)), ((), ()))
TN = (((0,), (0,)), ((), ()))
MAIN = 3 * 128


def split(x):
    high = x.astype(BF16)
    return high, (x - high.astype(F32)).astype(BF16)


def exact_dot(x, y, dims=(((1,), (0,)), ((), ()))):
    return lax.dot_general(x, y, dims, precision=HIGHEST, preferred_element_type=F32)


def chosen(mask):
    return jnp.where(mask, jnp.ones(mask.shape, BF16), jnp.zeros(mask.shape, BF16))


def half_sum(x):
    return x[:, :128] + x[:, 128:]


def squared(x):
    x = jnp.concatenate([x, jnp.zeros((64, 64), F32)], axis=1)
    return jnp.concatenate([x, jnp.zeros((64, 128), F32)], axis=0)


def folded(rows, start_ref):
    twice = rows + pltpu.roll(rows, SIDE, 1)
    sub = lax.broadcasted_iota(jnp.int32, (8, 128), 0)
    for tile in range(7):
        here = twice[tile * 8 : (tile + 1) * 8]
        total = jnp.zeros((8, 128), F32)
        for r in range(8):
            i = tile * 8 + r
            if i < SIDE:
                moved = pltpu.roll(here, (128 - i + BANDS * (i // GRAM)) % 128, 1)
                total = jnp.where(sub == r, moved, total)
        start_ref[tile * 8 : (tile + 1) * 8, :] = total
    lane = lax.broadcasted_iota(jnp.int32, (GRAM, 128), 1)
    return sum(
        jnp.where(lane // BANDS == g, start_ref[g * GRAM : (g + 1) * GRAM, :], 0.0) for g in range(5)
    )


def unfolded(bands, start_ref):
    sub = lax.broadcasted_iota(jnp.int32, (8, 128), 0)
    lane = lax.broadcasted_iota(jnp.int32, (GRAM, 128), 1)
    start_ref[48:56, :] = jnp.zeros((8, 128), F32)
    for g in range(5):
        start_ref[g * GRAM : (g + 1) * GRAM, :] = jnp.where(lane // BANDS == g, bands, 0.0)
    tiles = []
    for tile in range(7):
        here = start_ref[tile * 8 : (tile + 1) * 8, :]
        total = jnp.zeros((8, 128), F32)
        for r in range(8):
            i = tile * 8 + r
            if i < SIDE:
                moved = pltpu.roll(here, (128 + i - BANDS * (i // GRAM)) % 128, 1)
                total = jnp.where(sub == r, moved, total)
        tiles.append(total)
    half = jnp.concatenate(tiles + [jnp.zeros((72, 128), F32)], axis=0)
    row = lax.broadcasted_iota(jnp.int32, (128, 128), 0)
    lane = lax.broadcasted_iota(jnp.int32, (128, 128), 1)
    half = jnp.where(lane < SIDE, half + pltpu.roll(half, 128 - SIDE, 1), 0.0)
    return half + jnp.where(row == lane, 0.0, half.T)


def pieces(source, target, size):
    count = source.shape[0]
    parts = [pl.ds(i, min(size, count - i)) for i in range(0, count, size)]
    return [(source.at[part], target.at[part]) for part in parts]


def pack_kernel(
    op_hbm, c_hbm, b_hbm, rows_hbm, wire_hbm, info_ref,
    op_ref, c_ref, b_ref, rows_ref, p_ref, a_ref, fold_ref, wire_ref, in_sem, out_sem,
):
    copies = [
        pltpu.make_async_copy(source, target, in_sem.at[i])
        for i, (source, target) in enumerate(
            [(rows_hbm, rows_ref), (b_hbm, b_ref), *pieces(c_hbm, c_ref, 72), *pieces(op_hbm, op_ref, 128)]
        )
    ]
    for copy in copies:
        copy.start()
    copies[0].wait()
    new_rows = rows_ref[...]
    target = new_rows // ROWS
    local = new_rows % ROWS
    onehot = lax.broadcasted_iota(jnp.int32, (PEERS, ROWS), 0) == target
    onehot_f = jnp.where(onehot, 1.0, 0.0).astype(F32)
    onehot_b = onehot_f.astype(BF16)
    before = lax.broadcasted_iota(jnp.int32, (128, 128), 0) < lax.broadcasted_iota(jnp.int32, (128, 128), 1)
    before = jnp.where(before, 1.0, 0.0).astype(BF16)
    ones = jnp.ones((128, 128), BF16)
    seen = jnp.zeros((PEERS, 128), F32)
    ranks = []
    for block in range(ROWS // 128):
        part = onehot_b[:, block * 128 : (block + 1) * 128]
        count = jnp.dot(part, before, preferred_element_type=F32) + seen
        ranks.append(jnp.sum(onehot_f[:, block * 128 : (block + 1) * 128] * count, axis=0, keepdims=True))
        seen = seen + jnp.dot(part, ones, preferred_element_type=F32)
    rank = jnp.concatenate(ranks, axis=1)
    rank_at = jnp.where(onehot, rank, -1.0).astype(BF16)
    info_ref[0:1, :] = target
    info_ref[1:2, :] = rank.astype(jnp.int32)
    info_ref[2:3, :] = local
    info_ref[3:8, :] = jnp.zeros((5, ROWS), jnp.int32)
    for copy in copies[1:]:
        copy.wait()
    middle = jnp.concatenate([c_ref[128:144, :], op_ref[0:112, :]], axis=0)
    for tile, x in enumerate((c_ref[0:128, :], middle, op_ref[112:240, :])):
        p_ref[:, tile * 256 : tile * 256 + 128], p_ref[:, tile * 256 + 128 : (tile + 1) * 256] = split(x.T)
    sums, low = jnp.zeros((192, 64), F32), jnp.zeros((64, 64), F32)
    for a in range(3):
        a_ref[a, 48:64, :] = jnp.zeros((16, ROWS), F32)
        a_ref[a, 0:48, :] = c_ref[a * K : (a + 1) * K, :]
        a_ref[a, 48:49, :] = b_ref[a : a + 1, :]
        one, two = split(a_ref[a])
        three = (a_ref[a] - one.astype(F32) - two.astype(F32)).astype(BF16)
        terms = jnp.concatenate([one, two, three], axis=0)
        sums = sums + lax.dot_general(terms, one, NT, preferred_element_type=F32)
        low = low + lax.dot_general(two, two, NT, preferred_element_type=F32)
    cross = squared(sums[64:128] + sums[128:192])
    gram = squared(sums[0:64] + low) + cross + cross.T
    bands = folded(gram[0:64], fold_ref)
    for i in range(GRAM):
        wire_ref[pl.ds(49 + i, PEERS, stride=WIRE), :] = jnp.broadcast_to(bands[i : i + 1, :], (PEERS, 128))

    at_rank = lax.broadcasted_iota(jnp.int32, (SLOTS, ROWS), 0).astype(F32) == rank
    rest = [op_ref[240 + i : 241 + i, :] for i in range(3)] + [b_ref[i : i + 1, :] for i in range(3)]
    rest = [jnp.where(at_rank, row, 0.0) for row in rest + [local.astype(F32)]]
    rest = jnp.concatenate(rest + [jnp.zeros((SLOTS, ROWS), F32)], axis=0)
    rest = jnp.concatenate(split(rest), axis=0)
    wire_ref[pl.ds(48, PEERS, stride=WIRE), :] = half_sum(
        lax.dot_general(onehot_b, rest, NT, preferred_element_type=F32)
    )
    sent = []
    count = PEERS // CHUNKS
    for chunk in range(CHUNKS):
        mine = rank_at[chunk * count : (chunk + 1) * count]
        choice = [chosen(mine == k) for k in range(SLOTS)]
        moved = jnp.dot(jnp.concatenate(choice, axis=0), p_ref[...], preferred_element_type=F32)
        for tile in range(3):
            both = half_sum(moved[:, tile * 256 : (tile + 1) * 256])
            for k in range(SLOTS):
                wire_ref[pl.ds(chunk * count * WIRE + tile * SLOTS + k, count, stride=WIRE), :] = both[
                    k * count : (k + 1) * count
                ]
        rows = pl.ds(chunk * count * WIRE, count * WIRE)
        sent.append(pltpu.make_async_copy(wire_ref.at[rows], wire_hbm.at[rows], out_sem.at[chunk]))
        sent[-1].start()
    for copy in sent:
        copy.wait()


def two_level(groups, left_ref, right_ref):
    eight = lax.broadcasted_iota(jnp.int32, (CY, 128), 0)
    deep = lax.broadcasted_iota(jnp.int32, (128, 128), 0).astype(F32).astype(BF16)
    count = groups[0][0].shape[0] // SLOTS
    for g, (values, labels) in enumerate(groups):
        labels = labels.astype(jnp.int32)
        y, z = labels // CZ, (labels % CZ).astype(F32)
        for k in range(SLOTS):
            cols = slice(k * 128, (k + 1) * 128)
            row = jnp.broadcast_to(z[k : k + 1], (128, 128)).astype(BF16)
            right_ref[g * 128 : (g + 1) * 128, cols] = chosen(deep == row)
            here = eight == y[k : k + 1]
            for c in range(count):
                row = (g * count + c) * CY
                value = values[c * SLOTS + k : c * SLOTS + k + 1]
                left_ref[row : row + CY, cols] = jnp.where(here, value, 0.0)
    rows = len(groups) * count * CY
    left = jnp.concatenate(split(left_ref[...]), axis=0)
    moved = lax.dot_general(left, right_ref[...], NT, preferred_element_type=F32)
    moved = moved[0:rows] + moved[rows:]
    size = count * CY
    return [moved[g * size : (g + 1) * size, g * 128 : (g + 1) * 128] for g in range(len(groups))]


def minus_combined(start, main_ref, weights):
    result = []
    for a in range(3):
        total = start[a]
        for m in range(K):
            row = (a * K + m) * CY
            total = total - main_ref[row : row + CY, :] * weights[m : m + 1, :]
        result.append(total)
    return result


def put_vector(vector, lines, v_ref):
    v_ref[24:32, :] = jnp.zeros((8, 128), F32)
    for a in range(3):
        v_ref[a * CY : (a + 1) * CY, :] = vector[a]
        v_ref[24 + a : 25 + a, :] = lines[a]


def swept(work, begin, count):
    row_id = lax.broadcasted_iota(jnp.int32, (K, 128), 0)
    columns = [jnp.broadcast_to(work[:, j : j + 1], (K, 128)) for j in range(begin, begin + count)]
    for s in range(count):
        j = begin + s
        column = columns[s]
        inverse = 1.0 / column[j : j + 1, :]
        here = row_id == j

        def step(x):
            pivot = x[j : j + 1, :] * inverse
            return jnp.where(here, pivot, x - column * pivot)

        work = step(work)
        columns = columns[: s + 1] + [step(c) for c in columns[s + 1 :]]
    return work


def unpack_kernel(
    place_ref, wire_hbm, main_ref, ext_ref, v_ref, inv_ref, start_ref, beta_ref,
    wire_ref, t_ref, r_ref, left_ref, right_ref, fold_ref, in_sem,
):
    copies = []
    for part, (source, target) in enumerate(pieces(wire_hbm, wire_ref, PEERS * WIRE // PARTS)):
        copies.append(pltpu.make_async_copy(source, target, in_sem.at[part]))
        copies[-1].start()
    deep = lax.broadcasted_iota(jnp.int32, (CZ, 128), 0).astype(F32).astype(BF16)
    for copy in copies:
        copy.wait()
    bands = [
        jnp.sum(wire_ref[pl.ds(49 + i, PEERS, stride=WIRE), :], axis=0, keepdims=True) for i in range(GRAM)
    ]
    gram = unfolded(jnp.concatenate(bands, axis=0), fold_ref)
    load_sq = jnp.broadcast_to(gram[48:49, 48:49], (1, 128))
    row_id = lax.broadcasted_iota(jnp.int32, (K, 128), 0)
    lane = lax.broadcasted_iota(jnp.int32, (K, 128), 1)
    raw = jnp.broadcast_to(gram[0:K, K : K + 1], (K, 128))
    work = jnp.where(lane < K + 1, gram[0:K], jnp.where(lane - 64 == row_id, 1.0, 0.0))
    for begin in range(0, K, 4):
        work = swept(work, begin, 4)
    rest = wire_ref[pl.ds(48, PEERS, stride=WIRE), :].T
    labels = rest[6 * SLOTS : 7 * SLOTS]
    whole = labels.astype(jnp.int32)
    label_y, label_z = (whole // CZ).astype(F32), (whole % CZ).astype(F32)
    for k in range(SLOTS):
        here = chosen(deep == jnp.broadcast_to(label_z[k : k + 1], (CZ, 128)).astype(BF16))
        row = jnp.broadcast_to(label_y[k : k + 1], (CZ, 128)).astype(BF16)
        for y in range(CY):
            t_ref[y * CZ : (y + 1) * CZ, k * 128 : (k + 1) * 128] = jnp.where(
                row == y, here, jnp.zeros((CZ, 128), BF16)
            )
    for tile in range(3):
        for k in range(SLOTS):
            high, low = split(wire_ref[pl.ds(tile * SLOTS + k, PEERS, stride=WIRE), :])
            r_ref[tile, k * 128 : (k + 1) * 128, 0:128] = high
            r_ref[tile, k * 128 : (k + 1) * 128, 128:256] = low
        moved = half_sum(jnp.dot(t_ref[...], r_ref[tile], preferred_element_type=F32))
        for y in range(CY):
            main_ref[pl.ds(tile * 128 * CY + y, 128, stride=CY), :] = moved[y * CZ : (y + 1) * CZ].T
    [ext] = two_level([(rest[0 : 6 * SLOTS], labels)], left_ref, right_ref)
    ext_ref[...] = ext

    inverse = jnp.where(lane < K, pltpu.roll(work, 64, 1), 0.0)
    weights = jnp.broadcast_to(work[:, K : K + 1], (K, 128))
    inv_ref[...] = inverse
    start_ref[...] = weights
    beta = jnp.sqrt(load_sq - jnp.sum(raw * weights, axis=0, keepdims=True))
    beta_ref[...] = jnp.broadcast_to(beta, (8, 128))
    load = [ext[24 + a * CY : 24 + (a + 1) * CY, :] for a in range(3)]
    vector = [v / beta for v in minus_combined(load, main_ref, weights)]
    lower = place_ref[0:1, :] == 0
    put_vector(vector, [jnp.where(lower, v[CY - 1 : CY], v[0:1]) for v in vector], v_ref)


def put_plane(pad_ref, dx, plane, line, side):
    for a in range(3):
        base = (dx * 3 + a) * 24
        edge = line[a : a + 1, :]
        pad_ref[base + 7 : base + 8, :] = jnp.where(side == 1, edge, 0.0)
        pad_ref[base + 8 : base + 16, :] = plane[a * CY : (a + 1) * CY, :]
        pad_ref[base + 16 : base + 17, :] = jnp.where(side == 0, edge, 0.0)


def stencil(main_ref, ext_ref, pad_ref):
    lane = lax.broadcasted_iota(jnp.int32, (CY, 128), 1)
    total = [jnp.zeros((CY, 128), F32) for _ in range(3)]
    for dx in range(3):
        for dy in range(3):
            for b in range(3):
                start = (dx * 3 + b) * 24 + 7 + dy
                here = pad_ref[start : start + CY, :]
                left = jnp.where(lane == 0, 0.0, pltpu.roll(here, 1, 1))
                right = jnp.where(lane == 127, 0.0, pltpu.roll(here, 127, 1))
                for dz, moved in enumerate((left, here, right)):
                    for a in range(3):
                        q = ((dx * 9 + dy * 3 + dz) * 3 + a) * 3 + b
                        if q < 240:
                            row = (3 * K + q) * CY
                            total[a] = total[a] + main_ref[row : row + CY, :] * moved
                        else:
                            row = (q - 240) * CY
                            total[a] = total[a] + ext_ref[row : row + CY, :] * moved
    return total


def image_kernel(count, place_ref, main_ref, ext_ref, first_ref, second_ref, *refs):
    vectors, (image_ref, send_ref, *edges, pad_ref, part_ref) = refs[:count], refs[count:]
    side = place_ref[0:1, :]
    even = place_ref[1:2, :] == 0
    first, second = first_ref[...], second_ref[...]
    up, down = jnp.where(even, second, first), jnp.where(even, first, second)
    put_plane(pad_ref, 0, up[0:24], up[24:32], side)
    put_plane(pad_ref, 1, vectors[-1][0:24, :], vectors[-1][24:32, :], side)
    put_plane(pad_ref, 2, down[0:24], down[24:32], side)
    image = stencil(main_ref, ext_ref, pad_ref)
    for a in range(3):
        image_ref[a * CY : (a + 1) * CY, :] = image[a]
    for edge_ref in edges:
        last = main_ref[pl.ds(CY - 1, 3 * K, stride=CY), :]
        edge_ref[0 : 3 * K, :] = jnp.where(side == 0, last, main_ref[pl.ds(0, 3 * K, stride=CY), :])
        edge_ref[3 * K :, :] = jnp.zeros((8, 128), F32)
        for a in range(3):
            row = 3 * K + a
            edge_ref[row : row + 1, :] = jnp.where(side == 0, image[a][CY - 1 : CY], image[a][0:1])
    for m in range(K):
        rows = [(a * K + m) * CY for a in range(3)]
        part_ref[m * CY : (m + 1) * CY, :] = sum(
            main_ref[row : row + CY, :] * image[a] for a, row in enumerate(rows)
        )
    others = [image] + [[ref[a * CY : (a + 1) * CY, :] for a in range(3)] for ref in vectors]
    for i in range(8):
        m = K + i
        if i < len(others):
            part_ref[m * CY : (m + 1) * CY, :] = sum(o * w for o, w in zip(others[i], image))
        else:
            part_ref[m * CY : (m + 1) * CY, :] = jnp.zeros((CY, 128), F32)
    part = sum(part_ref[pl.ds(y, K + 8, stride=CY), :] for y in range(CY))
    part = jnp.concatenate([part, jnp.zeros((128 - K - 8, 128), F32)], axis=0)
    send_ref[...] = exact_dot(jnp.ones((PEERS, 128), F32), part, NT)


def totals(got_ref):
    return exact_dot(got_ref[...], jnp.ones((PEERS, 128), F32), TN)


def next_kernel(got_ref, main_ref, image_ref, one_ref, other_ref, inv_ref, v_ref, weights_ref, h_ref):
    sums = totals(got_ref)
    weights = exact_dot(inv_ref[...], sums)
    h11 = sums[K + 1 : K + 2, :]
    along = jnp.sum(sums[0:K] * weights, axis=0, keepdims=True)
    h21 = jnp.sqrt(sums[K : K + 1, :] - along - h11 * h11)
    begin = [
        image_ref[a * CY : (a + 1) * CY, :] - h11 * one_ref[a * CY : (a + 1) * CY, :] for a in range(3)
    ]
    vector = [v / h21 for v in minus_combined(begin, main_ref, weights)]
    lines = []
    for a in range(3):
        along_line = jnp.sum(other_ref[a * K : (a + 1) * K, :] * weights, axis=0, keepdims=True)
        line = other_ref[3 * K + a : 3 * K + a + 1, :] - along_line - h11 * one_ref[24 + a : 25 + a, :]
        lines.append(line / h21)
    put_vector(vector, lines, v_ref)
    weights_ref[...] = weights
    h_ref[...] = jnp.zeros((8, 128), F32)
    h_ref[0:1, :] = h11
    h_ref[1:2, :] = h21


def send_kernel(got_ref, inv_ref, start_ref, first_ref, h_ref, beta_ref, u_ref, info_ref, wire_ref, y_ref):
    sums = totals(got_ref)
    weights = exact_dot(inv_ref[...], sums)
    h11, h21 = h_ref[0:1, :], h_ref[1:2, :]
    h12, h22 = sums[K + 1 : K + 2, :], sums[K + 2 : K + 3, :]
    along = jnp.sum(sums[0:K] * weights, axis=0, keepdims=True)
    h32 = jnp.sqrt(sums[K : K + 1, :] - along - h12 * h12 - h22 * h22)
    beta = beta_ref[0:1, :]
    m11 = h11 * h11 + h21 * h21
    m12 = h11 * h12 + h21 * h22
    m22 = h12 * h12 + h22 * h22 + h32 * h32
    g_one = beta * h11
    g_two = beta * h12
    determ = m11 * m22 - m12 * m12
    y_one = (m22 * g_one - m12 * g_two) / determ
    y_two = (m11 * g_two - m12 * g_one) / determ
    y_ref[...] = jnp.zeros((8, 128), F32)
    y_ref[0:1, :] = y_one
    y_ref[1:2, :] = y_two
    weights = start_ref[...] - y_one * first_ref[...] - y_two * weights
    wide = jnp.concatenate([weights] * (ROWS // 128), axis=1)
    target, rank, local = (info_ref[i : i + 1, :] for i in range(3))
    at_rank = lax.broadcasted_iota(jnp.int32, (SLOTS, ROWS), 0) == rank
    rows = [jnp.sum(u_ref[a * K : (a + 1) * K, :] * wide, axis=0, keepdims=True) for a in range(3)]
    rows = jnp.concatenate([jnp.where(at_rank, r, 0.0) for r in rows + [local.astype(F32)]], axis=0)
    rows = jnp.concatenate(split(rows), axis=0)
    onehot = lax.broadcasted_iota(jnp.int32, (PEERS, ROWS), 0) == target
    onehot = jnp.where(onehot, 1.0, 0.0).astype(BF16)
    mine = lax.dot_general(onehot, rows, NT, preferred_element_type=F32)
    mine = mine + pltpu.roll(mine, 64, 1)
    peer = lax.broadcasted_iota(jnp.int32, (PEERS, 128), 0)
    lane = lax.broadcasted_iota(jnp.int32, (PEERS, 128), 1)
    other = jnp.where(peer % 2 == 0, pltpu.roll(mine, PEERS - 1, 0), pltpu.roll(mine, 1, 0))
    pair = jnp.where(lane < 64, mine, other)
    wire_ref[pl.ds(0, PEERS, stride=3), :] = jnp.where(peer < 2, 0.0, pltpu.roll(pair, 2, 0))
    wire_ref[pl.ds(1, PEERS, stride=3), :] = pair
    wire_ref[pl.ds(2, PEERS, stride=3), :] = jnp.where(peer >= PEERS - 2, 0.0, pltpu.roll(pair, PEERS - 2, 0))


def last_kernel(
    place_ref, got_ref, main_ref, ext_ref, y_ref, one_ref, two_ref, im_one_ref, im_two_ref,
    sol_ref, res_ref, left_ref, right_ref, pad_ref,
):
    side = place_ref[0:1, :]
    for dx in range(3):
        got = got_ref[pl.ds(dx, PEERS, stride=3), :].T
        own, other = two_level(
            [(got[base : base + 48], got[base + 48 : base + 64]) for base in (0, 64)],
            left_ref.at[dx],
            right_ref.at[dx],
        )
        lines = [
            jnp.where(side == 0, other[a * CY : a * CY + 1, :], other[a * CY + 7 : a * CY + 8, :]) for a in range(3)
        ]
        put_plane(pad_ref, dx, own, jnp.concatenate(lines, axis=0), side)
        if dx == 1:
            term = own
    image = stencil(main_ref, ext_ref, pad_ref)
    y_one, y_two = y_ref[0:1, :], y_ref[1:2, :]
    solution = term + y_one * one_ref[0:24, :] + y_two * two_ref[0:24, :]
    for a in range(3):
        rows = slice(a * CY, (a + 1) * CY)
        residual = ext_ref[24 + a * CY : 24 + (a + 1) * CY, :] - image[a]
        residual = residual - y_one * im_one_ref[rows, :] - y_two * im_two_ref[rows, :]
        for y in range(CY):
            cols = slice(y * CZ, (y + 1) * CZ)
            sol_ref[a : a + 1, cols] = solution[a * CY + y : a * CY + y + 1, :]
            res_ref[a : a + 1, cols] = residual[y : y + 1, :]


def shape(*dims, dtype=F32):
    return jax.ShapeDtypeStruct(dims, dtype)


def specs(*spaces):
    return tuple(pl.BlockSpec(memory_space=space) for space in spaces)


def call(kernel, outs, scratch=(), inputs=0, in_specs=None, out_specs=None, limit=40):
    vmem = pltpu.VMEM
    return pl.pallas_call(
        kernel,
        out_shape=outs,
        in_specs=in_specs or specs(*[vmem] * inputs),
        out_specs=out_specs or specs(*[vmem] * len(outs)),
        scratch_shapes=list(scratch),
        compiler_params=pltpu.CompilerParams(vmem_limit_bytes=limit * 2**20),
    )


def exchange(rows):
    count = rows.shape[0] // PEERS
    shaped = rows.reshape(PEERS, count, 1, 128)
    got = lax.all_to_all(shaped, GX_GY, split_axis=0, concat_axis=0, tiled=True)
    return got.reshape(PEERS * count, 128)


def swap(plane, first):
    pairs = [(i, i + 1) for i in range(first, N_GX - 1, 2)]
    return lax.ppermute(plane, GX, pairs + [(j, i) for i, j in pairs])


def other_core(x):
    return lax.ppermute(x, "gy", [(0, 1), (1, 0)])


def body(operator, basis_u, basis_c, right_side, new_rows):
    row = lax.broadcasted_iota(jnp.int32, (8, 128), 0)
    place = jnp.where(row == 0, lax.axis_index("gy"), lax.axis_index(GX) % 2).astype(jnp.int32)
    vmem, hbm = pltpu.VMEM, pltpu.HBM
    wire, info = call(
        pack_kernel,
        (shape(PEERS * WIRE, 128), shape(8, ROWS, dtype=jnp.int32)),
        [
            vmem((243, ROWS), F32),
            vmem((144, ROWS), F32),
            vmem((3, ROWS), F32),
            vmem((1, ROWS), jnp.int32),
            vmem((ROWS, 2 * MAIN), BF16),
            vmem((3, 64, ROWS), F32),
            vmem((56, 128), F32),
            vmem((PEERS * WIRE, 128), F32),
            pltpu.SemaphoreType.DMA((6,)),
            pltpu.SemaphoreType.DMA((CHUNKS,)),
        ],
        in_specs=specs(hbm, hbm, hbm, hbm),
        out_specs=specs(hbm, vmem),
        limit=56,
    )(operator, basis_c, right_side, new_rows.reshape(1, ROWS))
    got = exchange(wire)
    plane = shape(32, 128)
    main, ext, one, inverse, start, beta = call(
        unpack_kernel,
        (shape(MAIN * CY, 128), shape(48, 128), plane, shape(K, 128), shape(K, 128), shape(8, 128)),
        [
            vmem((PEERS * WIRE, 128), F32),
            vmem((ROWS, SLOTS * PEERS), BF16),
            vmem((3, SLOTS * PEERS, 256), BF16),
            vmem((48, SLOTS * PEERS), F32),
            vmem((128, SLOTS * PEERS), BF16),
            vmem((56, 128), F32),
            pltpu.SemaphoreType.DMA((PARTS,)),
        ],
        in_specs=specs(vmem, hbm),
        limit=40,
    )(place, got)
    pad = vmem((9 * 24, 128), F32)
    image_scratch = [pad, vmem(((K + 8) * CY, 128), F32)]
    image_outs = (shape(3 * CY, 128), shape(PEERS, 128))
    one = lax.dynamic_update_slice(one, other_core(one[24:32]), (24, 0))
    image_one, send, edge = call(
        functools.partial(image_kernel, 1), (*image_outs, shape(3 * K + 8, 128)), image_scratch, inputs=6
    )(place, main, ext, swap(one, 0), swap(one, 1), one)
    other = other_core(edge)
    sums = exchange(send)
    two, weights, h_one = call(next_kernel, (plane, shape(K, 128), shape(8, 128)), inputs=6)(
        sums, main, image_one, one, other, inverse
    )
    image_two, send = call(functools.partial(image_kernel, 2), image_outs, image_scratch, inputs=7)(
        place, main, ext, swap(two, 0), swap(two, 1), one, two
    )
    sums = exchange(send)
    wire, y = call(send_kernel, (shape(PEERS * 3, 128), shape(8, 128)), inputs=8)(
        sums, inverse, start, weights, h_one, beta, basis_u, info
    )
    got = exchange(wire)
    return call(
        last_kernel,
        (shape(3, ROWS), shape(3, ROWS)),
        [vmem((3, 48, SLOTS * PEERS), F32), vmem((3, 256, SLOTS * PEERS), BF16), pad],
        inputs=9,
    )(place, got, main, ext, y, one, two, image_one, image_two)


def solution(mesh):
    torus = Mesh(mesh.devices.reshape(4, 4, 4, mesh.shape["gy"]), ("gx_0", "gx_1", "gx_2", "gy"))
    placed = (P(None, GX_GY), P(None, GX_GY), P(None, GX_GY), P(None, GX_GY), P(GX_GY))
    return jax.shard_map(
        body,
        mesh=torus,
        in_specs=placed,
        out_specs=(P(None, GX_GY), P(None, GX_GY)),
        check_vma=False,
    )
```

```python
import functools

import jax
import jax.numpy as jnp
from jax import lax
from jax.experimental import pallas as pl
from jax.experimental.pallas import tpu as pltpu
from jax.sharding import Mesh
from jax.sharding import PartitionSpec as P

CY = 8
CZ = 128
K = 48
SLOTS = 16
PEERS = 128
ROWS = 1024
N_GX = 64
GX_GY = ("gx_0", "gx_1", "gx_2", "gy")
GX = ("gx_0", "gx_1", "gx_2")
F32 = jnp.float32
BF16 = jnp.bfloat16
HIGHEST = lax.Precision.HIGHEST
SIDE = K + 1
BANDS = 25
GRAM = 10
HALF = GRAM // 2
WIRE = 49 + HALF
CHUNKS = 8
NT = (((1,), (1,)), ((), ()))
TN = (((0,), (0,)), ((), ()))
MAIN = 3 * 128


def split(x):
    high = x.astype(BF16)
    return high, (x - high.astype(F32)).astype(BF16)


def exact_dot(x, y, dims=(((1,), (0,)), ((), ()))):
    return lax.dot_general(x, y, dims, precision=HIGHEST, preferred_element_type=F32)


def chosen(mask):
    return jnp.where(mask, jnp.ones(mask.shape, BF16), jnp.zeros(mask.shape, BF16))


def half_sum(x):
    return x[:, :128] + x[:, 128:]


def squared(x):
    x = jnp.concatenate([x, jnp.zeros((64, 64), F32)], axis=1)
    return jnp.concatenate([x, jnp.zeros((64, 128), F32)], axis=0)


def folded(rows, start_ref):
    twice = rows + pltpu.roll(rows, SIDE, 1)
    sub = lax.broadcasted_iota(jnp.int32, (8, 128), 0)
    for tile in range(7):
        here = twice[tile * 8 : (tile + 1) * 8]
        total = jnp.zeros((8, 128), F32)
        for r in range(8):
            i = tile * 8 + r
            if i < SIDE:
                moved = pltpu.roll(here, (128 - i + BANDS * (i // GRAM)) % 128, 1)
                total = jnp.where(sub == r, moved, total)
        start_ref[tile * 8 : (tile + 1) * 8, :] = total
    lane = lax.broadcasted_iota(jnp.int32, (GRAM, 128), 1)
    return sum(
        jnp.where(lane // BANDS == g, start_ref[g * GRAM : (g + 1) * GRAM, :], 0.0) for g in range(5)
    )


def unfolded(bands, start_ref):
    sub = lax.broadcasted_iota(jnp.int32, (8, 128), 0)
    lane = lax.broadcasted_iota(jnp.int32, (GRAM, 128), 1)
    start_ref[48:56, :] = jnp.zeros((8, 128), F32)
    for g in range(5):
        start_ref[g * GRAM : (g + 1) * GRAM, :] = jnp.where(lane // BANDS == g, bands, 0.0)
    tiles = []
    for tile in range(7):
        here = start_ref[tile * 8 : (tile + 1) * 8, :]
        total = jnp.zeros((8, 128), F32)
        for r in range(8):
            i = tile * 8 + r
            if i < SIDE:
                moved = pltpu.roll(here, (128 + i - BANDS * (i // GRAM)) % 128, 1)
                total = jnp.where(sub == r, moved, total)
        tiles.append(total)
    half = jnp.concatenate(tiles + [jnp.zeros((72, 128), F32)], axis=0)
    row = lax.broadcasted_iota(jnp.int32, (128, 128), 0)
    lane = lax.broadcasted_iota(jnp.int32, (128, 128), 1)
    half = jnp.where(lane < SIDE, half + pltpu.roll(half, 128 - SIDE, 1), 0.0)
    return half + jnp.where(row == lane, 0.0, half.T)


def pieces(source, target, size):
    count = source.shape[0]
    parts = [pl.ds(i, min(size, count - i)) for i in range(0, count, size)]
    return [(source.at[part], target.at[part]) for part in parts]


def pack_kernel(
    op_hbm, c_hbm, b_hbm, rows_hbm, wire_hbm, info_ref,
    op_ref, c_ref, b_ref, rows_ref, p_ref, a_ref, fold_ref, wire_ref, in_sem, out_sem,
):
    copies = [
        pltpu.make_async_copy(source, target, in_sem.at[i])
        for i, (source, target) in enumerate(
            [(rows_hbm, rows_ref), (b_hbm, b_ref), *pieces(c_hbm, c_ref, 72), *pieces(op_hbm, op_ref, 128)]
        )
    ]
    for copy in copies:
        copy.start()
    copies[0].wait()
    new_rows = rows_ref[...]
    target = new_rows // ROWS
    local = new_rows % ROWS
    onehot = lax.broadcasted_iota(jnp.int32, (PEERS, ROWS), 0) == target
    onehot_f = jnp.where(onehot, 1.0, 0.0).astype(F32)
    onehot_b = onehot_f.astype(BF16)
    before = lax.broadcasted_iota(jnp.int32, (128, 128), 0) < lax.broadcasted_iota(jnp.int32, (128, 128), 1)
    before = jnp.where(before, 1.0, 0.0).astype(BF16)
    ones = jnp.ones((128, 128), BF16)
    seen = jnp.zeros((PEERS, 128), F32)
    ranks = []
    for block in range(ROWS // 128):
        part = onehot_b[:, block * 128 : (block + 1) * 128]
        count = jnp.dot(part, before, preferred_element_type=F32) + seen
        ranks.append(jnp.sum(onehot_f[:, block * 128 : (block + 1) * 128] * count, axis=0, keepdims=True))
        seen = seen + jnp.dot(part, ones, preferred_element_type=F32)
    rank = jnp.concatenate(ranks, axis=1)
    rank_at = jnp.where(onehot, rank, -1.0).astype(BF16)
    info_ref[0:1, :] = target
    info_ref[1:2, :] = rank.astype(jnp.int32)
    info_ref[2:3, :] = local
    info_ref[3:8, :] = jnp.zeros((5, ROWS), jnp.int32)
    for copy in copies[1:4]:
        copy.wait()

    def put(tile, x):
        p_ref[:, tile * 256 : tile * 256 + 128], p_ref[:, tile * 256 + 128 : (tile + 1) * 256] = split(x.T)

    put(0, c_ref[0:128, :])
    sums, low = jnp.zeros((192, 64), F32), jnp.zeros((64, 64), F32)
    for a in range(3):
        a_ref[a, 48:64, :] = jnp.zeros((16, ROWS), F32)
        a_ref[a, 0:48, :] = c_ref[a * K : (a + 1) * K, :]
        a_ref[a, 48:49, :] = b_ref[a : a + 1, :]
        one, two = split(a_ref[a])
        three = (a_ref[a] - one.astype(F32) - two.astype(F32)).astype(BF16)
        terms = jnp.concatenate([one, two, three], axis=0)
        sums = sums + lax.dot_general(terms, one, NT, preferred_element_type=F32)
        low = low + lax.dot_general(two, two, NT, preferred_element_type=F32)
    cross = squared(sums[64:128] + sums[128:192])
    gram = squared(sums[0:64] + low) + cross + cross.T
    bands = folded(gram[0:64], fold_ref)
    second = lax.broadcasted_iota(jnp.int32, (PEERS, 128), 0) % 2 == 1
    for i in range(HALF):
        wire_ref[pl.ds(49 + i, PEERS, stride=WIRE), :] = jnp.where(
            second, bands[HALF + i : HALF + i + 1, :], bands[i : i + 1, :]
        )
    for copy in copies[4:]:
        copy.wait()
    put(1, jnp.concatenate([c_ref[128:144, :], op_ref[0:112, :]], axis=0))
    put(2, op_ref[112:240, :])
    at_rank = lax.broadcasted_iota(jnp.int32, (SLOTS, ROWS), 0).astype(F32) == rank
    rest = [op_ref[240 + i : 241 + i, :] for i in range(3)] + [b_ref[i : i + 1, :] for i in range(3)]
    rest = [jnp.where(at_rank, row, 0.0) for row in rest + [local.astype(F32)]]
    rest = jnp.concatenate(rest + [jnp.zeros((SLOTS, ROWS), F32)], axis=0)
    rest = jnp.concatenate(split(rest), axis=0)
    wire_ref[pl.ds(48, PEERS, stride=WIRE), :] = half_sum(
        lax.dot_general(onehot_b, rest, NT, preferred_element_type=F32)
    )
    sent = []
    count = PEERS // CHUNKS
    for chunk in range(CHUNKS):
        mine = rank_at[chunk * count : (chunk + 1) * count]
        choice = [chosen(mine == k) for k in range(SLOTS)]
        moved = jnp.dot(jnp.concatenate(choice, axis=0), p_ref[...], preferred_element_type=F32)
        for tile in range(3):
            both = half_sum(moved[:, tile * 256 : (tile + 1) * 256])
            for k in range(SLOTS):
                wire_ref[pl.ds(chunk * count * WIRE + tile * SLOTS + k, count, stride=WIRE), :] = both[
                    k * count : (k + 1) * count
                ]
        rows = pl.ds(chunk * count * WIRE, count * WIRE)
        sent.append(pltpu.make_async_copy(wire_ref.at[rows], wire_hbm.at[rows], out_sem.at[chunk]))
        sent[-1].start()
    for copy in sent:
        copy.wait()


def two_level(groups, left_ref, right_ref):
    eight = lax.broadcasted_iota(jnp.int32, (CY, 128), 0)
    deep = lax.broadcasted_iota(jnp.int32, (128, 128), 0).astype(F32).astype(BF16)
    count = groups[0][0].shape[0] // SLOTS
    for g, (values, labels) in enumerate(groups):
        labels = labels.astype(jnp.int32)
        y, z = labels // CZ, (labels % CZ).astype(F32)
        for k in range(SLOTS):
            cols = slice(k * 128, (k + 1) * 128)
            row = jnp.broadcast_to(z[k : k + 1], (128, 128)).astype(BF16)
            right_ref[g * 128 : (g + 1) * 128, cols] = chosen(deep == row)
            here = eight == y[k : k + 1]
            for c in range(count):
                row = (g * count + c) * CY
                value = values[c * SLOTS + k : c * SLOTS + k + 1]
                left_ref[row : row + CY, cols] = jnp.where(here, value, 0.0)
    rows = len(groups) * count * CY
    left = jnp.concatenate(split(left_ref[...]), axis=0)
    moved = lax.dot_general(left, right_ref[...], NT, preferred_element_type=F32)
    moved = moved[0:rows] + moved[rows:]
    size = count * CY
    return [moved[g * size : (g + 1) * size, g * 128 : (g + 1) * 128] for g in range(len(groups))]


def minus_combined(start, main_ref, weights):
    result = []
    for a in range(3):
        total = start[a]
        for m in range(K):
            row = (a * K + m) * CY
            total = total - main_ref[row : row + CY, :] * weights[m : m + 1, :]
        result.append(total)
    return result


def put_vector(vector, lines, v_ref):
    v_ref[24:32, :] = jnp.zeros((8, 128), F32)
    for a in range(3):
        v_ref[a * CY : (a + 1) * CY, :] = vector[a]
        v_ref[24 + a : 25 + a, :] = lines[a]


def swept(work, begin, count):
    row_id = lax.broadcasted_iota(jnp.int32, (K, 128), 0)
    columns = [jnp.broadcast_to(work[:, j : j + 1], (K, 128)) for j in range(begin, begin + count)]
    for s in range(count):
        j = begin + s
        column = columns[s]
        inverse = 1.0 / column[j : j + 1, :]
        here = row_id == j

        def step(x):
            pivot = x[j : j + 1, :] * inverse
            return jnp.where(here, pivot, x - column * pivot)

        work = step(work)
        columns = columns[: s + 1] + [step(c) for c in columns[s + 1 :]]
    return work


def unpack_kernel(
    place_ref, wire_ref, mine_ref, other_ref, main_ref, ext_ref, v_ref, inv_ref, start_ref, beta_ref,
    t_ref, r_ref, left_ref, right_ref, fold_ref,
):
    deep = lax.broadcasted_iota(jnp.int32, (CZ, 128), 0).astype(F32).astype(BF16)
    lower = place_ref[0:1, :] == 0
    mine, other = mine_ref[0:HALF, :], other_ref[0:HALF, :]
    bands = jnp.concatenate([jnp.where(lower, mine, other), jnp.where(lower, other, mine)], axis=0)
    gram = unfolded(bands, fold_ref)
    load_sq = jnp.broadcast_to(gram[48:49, 48:49], (1, 128))
    row_id = lax.broadcasted_iota(jnp.int32, (K, 128), 0)
    lane = lax.broadcasted_iota(jnp.int32, (K, 128), 1)
    raw = jnp.broadcast_to(gram[0:K, K : K + 1], (K, 128))
    work = jnp.where(lane < K + 1, gram[0:K], jnp.where(lane - 64 == row_id, 1.0, 0.0))
    for begin in range(0, K, 4):
        work = swept(work, begin, 4)
    rest = wire_ref[pl.ds(48, PEERS, stride=WIRE), :].T
    labels = rest[6 * SLOTS : 7 * SLOTS]
    whole = labels.astype(jnp.int32)
    label_y, label_z = (whole // CZ).astype(F32), (whole % CZ).astype(F32)
    for k in range(SLOTS):
        here = chosen(deep == jnp.broadcast_to(label_z[k : k + 1], (CZ, 128)).astype(BF16))
        row = jnp.broadcast_to(label_y[k : k + 1], (CZ, 128)).astype(BF16)
        for y in range(CY):
            t_ref[y * CZ : (y + 1) * CZ, k * 128 : (k + 1) * 128] = jnp.where(
                row == y, here, jnp.zeros((CZ, 128), BF16)
            )
    for tile in range(3):
        for k in range(SLOTS):
            high, low = split(wire_ref[pl.ds(tile * SLOTS + k, PEERS, stride=WIRE), :])
            r_ref[tile, k * 128 : (k + 1) * 128, 0:128] = high
            r_ref[tile, k * 128 : (k + 1) * 128, 128:256] = low
        moved = half_sum(jnp.dot(t_ref[...], r_ref[tile], preferred_element_type=F32))
        for y in range(CY):
            main_ref[pl.ds(tile * 128 * CY + y, 128, stride=CY), :] = moved[y * CZ : (y + 1) * CZ].T
    [ext] = two_level([(rest[0 : 6 * SLOTS], labels)], left_ref, right_ref)
    ext_ref[...] = ext

    inverse = jnp.where(lane < K, pltpu.roll(work, 64, 1), 0.0)
    weights = jnp.broadcast_to(work[:, K : K + 1], (K, 128))
    inv_ref[...] = inverse
    start_ref[...] = weights
    beta = jnp.sqrt(load_sq - jnp.sum(raw * weights, axis=0, keepdims=True))
    beta_ref[...] = jnp.broadcast_to(beta, (8, 128))
    load = [ext[24 + a * CY : 24 + (a + 1) * CY, :] for a in range(3)]
    vector = [v / beta for v in minus_combined(load, main_ref, weights)]
    put_vector(vector, [jnp.where(lower, v[CY - 1 : CY], v[0:1]) for v in vector], v_ref)


def put_plane(pad_ref, dx, plane, line, side):
    for a in range(3):
        base = (dx * 3 + a) * 24
        edge = line[a : a + 1, :]
        pad_ref[base + 7 : base + 8, :] = jnp.where(side == 1, edge, 0.0)
        pad_ref[base + 8 : base + 16, :] = plane[a * CY : (a + 1) * CY, :]
        pad_ref[base + 16 : base + 17, :] = jnp.where(side == 0, edge, 0.0)


def stencil(main_ref, ext_ref, pad_ref):
    lane = lax.broadcasted_iota(jnp.int32, (CY, 128), 1)
    total = [jnp.zeros((CY, 128), F32) for _ in range(3)]
    for dx in range(3):
        for dy in range(3):
            for b in range(3):
                start = (dx * 3 + b) * 24 + 7 + dy
                here = pad_ref[start : start + CY, :]
                left = jnp.where(lane == 0, 0.0, pltpu.roll(here, 1, 1))
                right = jnp.where(lane == 127, 0.0, pltpu.roll(here, 127, 1))
                for dz, moved in enumerate((left, here, right)):
                    for a in range(3):
                        q = ((dx * 9 + dy * 3 + dz) * 3 + a) * 3 + b
                        if q < 240:
                            row = (3 * K + q) * CY
                            total[a] = total[a] + main_ref[row : row + CY, :] * moved
                        else:
                            row = (q - 240) * CY
                            total[a] = total[a] + ext_ref[row : row + CY, :] * moved
    return total


def image_kernel(count, place_ref, main_ref, ext_ref, first_ref, second_ref, *refs):
    vectors, (image_ref, send_ref, *edges, pad_ref, part_ref) = refs[:count], refs[count:]
    side = place_ref[0:1, :]
    even = place_ref[1:2, :] == 0
    first, second = first_ref[...], second_ref[...]
    up, down = jnp.where(even, second, first), jnp.where(even, first, second)
    put_plane(pad_ref, 0, up[0:24], up[24:32], side)
    put_plane(pad_ref, 1, vectors[-1][0:24, :], vectors[-1][24:32, :], side)
    put_plane(pad_ref, 2, down[0:24], down[24:32], side)
    image = stencil(main_ref, ext_ref, pad_ref)
    for a in range(3):
        image_ref[a * CY : (a + 1) * CY, :] = image[a]
    for edge_ref in edges:
        last = main_ref[pl.ds(CY - 1, 3 * K, stride=CY), :]
        edge_ref[0 : 3 * K, :] = jnp.where(side == 0, last, main_ref[pl.ds(0, 3 * K, stride=CY), :])
        edge_ref[3 * K :, :] = jnp.zeros((8, 128), F32)
        for a in range(3):
            row = 3 * K + a
            edge_ref[row : row + 1, :] = jnp.where(side == 0, image[a][CY - 1 : CY], image[a][0:1])
    for m in range(K):
        rows = [(a * K + m) * CY for a in range(3)]
        part_ref[m * CY : (m + 1) * CY, :] = sum(
            main_ref[row : row + CY, :] * image[a] for a, row in enumerate(rows)
        )
    others = [image] + [[ref[a * CY : (a + 1) * CY, :] for a in range(3)] for ref in vectors]
    for i in range(8):
        m = K + i
        if i < len(others):
            part_ref[m * CY : (m + 1) * CY, :] = sum(o * w for o, w in zip(others[i], image))
        else:
            part_ref[m * CY : (m + 1) * CY, :] = jnp.zeros((CY, 128), F32)
    part = sum(part_ref[pl.ds(y, K + 8, stride=CY), :] for y in range(CY))
    part = jnp.concatenate([part, jnp.zeros((128 - K - 8, 128), F32)], axis=0)
    send_ref[...] = exact_dot(jnp.ones((PEERS, 128), F32), part, NT)


def totals(got_ref):
    return exact_dot(got_ref[...], jnp.ones((PEERS, 128), F32), TN)


def next_kernel(got_ref, main_ref, image_ref, one_ref, other_ref, inv_ref, v_ref, weights_ref, h_ref):
    sums = totals(got_ref)
    weights = exact_dot(inv_ref[...], sums)
    h11 = sums[K + 1 : K + 2, :]
    along = jnp.sum(sums[0:K] * weights, axis=0, keepdims=True)
    h21 = jnp.sqrt(sums[K : K + 1, :] - along - h11 * h11)
    begin = [
        image_ref[a * CY : (a + 1) * CY, :] - h11 * one_ref[a * CY : (a + 1) * CY, :] for a in range(3)
    ]
    vector = [v / h21 for v in minus_combined(begin, main_ref, weights)]
    lines = []
    for a in range(3):
        along_line = jnp.sum(other_ref[a * K : (a + 1) * K, :] * weights, axis=0, keepdims=True)
        line = other_ref[3 * K + a : 3 * K + a + 1, :] - along_line - h11 * one_ref[24 + a : 25 + a, :]
        lines.append(line / h21)
    put_vector(vector, lines, v_ref)
    weights_ref[...] = weights
    h_ref[...] = jnp.zeros((8, 128), F32)
    h_ref[0:1, :] = h11
    h_ref[1:2, :] = h21


def send_kernel(got_ref, inv_ref, start_ref, first_ref, h_ref, beta_ref, u_ref, info_ref, wire_ref, y_ref):
    sums = totals(got_ref)
    weights = exact_dot(inv_ref[...], sums)
    h11, h21 = h_ref[0:1, :], h_ref[1:2, :]
    h12, h22 = sums[K + 1 : K + 2, :], sums[K + 2 : K + 3, :]
    along = jnp.sum(sums[0:K] * weights, axis=0, keepdims=True)
    h32 = jnp.sqrt(sums[K : K + 1, :] - along - h12 * h12 - h22 * h22)
    beta = beta_ref[0:1, :]
    m11 = h11 * h11 + h21 * h21
    m12 = h11 * h12 + h21 * h22
    m22 = h12 * h12 + h22 * h22 + h32 * h32
    g_one = beta * h11
    g_two = beta * h12
    determ = m11 * m22 - m12 * m12
    y_one = (m22 * g_one - m12 * g_two) / determ
    y_two = (m11 * g_two - m12 * g_one) / determ
    y_ref[...] = jnp.zeros((8, 128), F32)
    y_ref[0:1, :] = y_one
    y_ref[1:2, :] = y_two
    weights = start_ref[...] - y_one * first_ref[...] - y_two * weights
    wide = jnp.concatenate([weights] * (ROWS // 128), axis=1)
    target, rank, local = (info_ref[i : i + 1, :] for i in range(3))
    at_rank = lax.broadcasted_iota(jnp.int32, (SLOTS, ROWS), 0) == rank
    rows = [jnp.sum(u_ref[a * K : (a + 1) * K, :] * wide, axis=0, keepdims=True) for a in range(3)]
    rows = jnp.concatenate([jnp.where(at_rank, r, 0.0) for r in rows + [local.astype(F32)]], axis=0)
    rows = jnp.concatenate(split(rows), axis=0)
    onehot = lax.broadcasted_iota(jnp.int32, (PEERS, ROWS), 0) == target
    onehot = jnp.where(onehot, 1.0, 0.0).astype(BF16)
    mine = lax.dot_general(onehot, rows, NT, preferred_element_type=F32)
    mine = mine + pltpu.roll(mine, 64, 1)
    peer = lax.broadcasted_iota(jnp.int32, (PEERS, 128), 0)
    lane = lax.broadcasted_iota(jnp.int32, (PEERS, 128), 1)
    other = jnp.where(peer % 2 == 0, pltpu.roll(mine, PEERS - 1, 0), pltpu.roll(mine, 1, 0))
    pair = jnp.where(lane < 64, mine, other)
    wire_ref[pl.ds(0, PEERS, stride=3), :] = jnp.where(peer < 2, 0.0, pltpu.roll(pair, 2, 0))
    wire_ref[pl.ds(1, PEERS, stride=3), :] = pair
    wire_ref[pl.ds(2, PEERS, stride=3), :] = jnp.where(peer >= PEERS - 2, 0.0, pltpu.roll(pair, PEERS - 2, 0))


def last_kernel(
    place_ref, got_ref, main_ref, ext_ref, y_ref, one_ref, two_ref, im_one_ref, im_two_ref,
    sol_ref, res_ref, left_ref, right_ref, pad_ref,
):
    side = place_ref[0:1, :]
    for dx in range(3):
        got = got_ref[pl.ds(dx, PEERS, stride=3), :].T
        own, other = two_level(
            [(got[base : base + 48], got[base + 48 : base + 64]) for base in (0, 64)],
            left_ref.at[dx],
            right_ref.at[dx],
        )
        lines = [
            jnp.where(side == 0, other[a * CY : a * CY + 1, :], other[a * CY + 7 : a * CY + 8, :]) for a in range(3)
        ]
        put_plane(pad_ref, dx, own, jnp.concatenate(lines, axis=0), side)
        if dx == 1:
            term = own
    image = stencil(main_ref, ext_ref, pad_ref)
    y_one, y_two = y_ref[0:1, :], y_ref[1:2, :]
    solution = term + y_one * one_ref[0:24, :] + y_two * two_ref[0:24, :]
    for a in range(3):
        rows = slice(a * CY, (a + 1) * CY)
        residual = ext_ref[24 + a * CY : 24 + (a + 1) * CY, :] - image[a]
        residual = residual - y_one * im_one_ref[rows, :] - y_two * im_two_ref[rows, :]
        for y in range(CY):
            cols = slice(y * CZ, (y + 1) * CZ)
            sol_ref[a : a + 1, cols] = solution[a * CY + y : a * CY + y + 1, :]
            res_ref[a : a + 1, cols] = residual[y : y + 1, :]


def shape(*dims, dtype=F32):
    return jax.ShapeDtypeStruct(dims, dtype)


def specs(*spaces):
    return tuple(pl.BlockSpec(memory_space=space) for space in spaces)


def call(kernel, outs, scratch=(), inputs=0, in_specs=None, out_specs=None, limit=40):
    vmem = pltpu.VMEM
    return pl.pallas_call(
        kernel,
        out_shape=outs,
        in_specs=in_specs or specs(*[vmem] * inputs),
        out_specs=out_specs or specs(*[vmem] * len(outs)),
        scratch_shapes=list(scratch),
        compiler_params=pltpu.CompilerParams(vmem_limit_bytes=limit * 2**20),
    )


def exchange(rows):
    count = rows.shape[0] // PEERS
    shaped = rows.reshape(PEERS, count, 1, 128)
    got = lax.all_to_all(shaped, GX_GY, split_axis=0, concat_axis=0, tiled=True)
    return got.reshape(PEERS * count, 128)


def swap(plane, first):
    pairs = [(i, i + 1) for i in range(first, N_GX - 1, 2)]
    return lax.ppermute(plane, GX, pairs + [(j, i) for i, j in pairs])


def other_core(x):
    return lax.ppermute(x, "gy", [(0, 1), (1, 0)])


def body(operator, basis_u, basis_c, right_side, new_rows):
    row = lax.broadcasted_iota(jnp.int32, (8, 128), 0)
    place = jnp.where(row == 0, lax.axis_index("gy"), lax.axis_index(GX) % 2).astype(jnp.int32)
    vmem, hbm = pltpu.VMEM, pltpu.HBM
    wire, info = call(
        pack_kernel,
        (shape(PEERS * WIRE, 128), shape(8, ROWS, dtype=jnp.int32)),
        [
            vmem((243, ROWS), F32),
            vmem((144, ROWS), F32),
            vmem((3, ROWS), F32),
            vmem((1, ROWS), jnp.int32),
            vmem((ROWS, 2 * MAIN), BF16),
            vmem((3, 64, ROWS), F32),
            vmem((56, 128), F32),
            vmem((PEERS * WIRE, 128), F32),
            pltpu.SemaphoreType.DMA((6,)),
            pltpu.SemaphoreType.DMA((CHUNKS,)),
        ],
        in_specs=specs(hbm, hbm, hbm, hbm),
        out_specs=specs(hbm, vmem),
        limit=56,
    )(operator, basis_c, right_side, new_rows.reshape(1, ROWS))
    got = exchange(wire)
    mine = jnp.sum(got.reshape(PEERS, WIRE, 128)[:, 49:], axis=0)
    plane = shape(32, 128)
    main, ext, one, inverse, start, beta = call(
        unpack_kernel,
        (shape(MAIN * CY, 128), shape(48, 128), plane, shape(K, 128), shape(K, 128), shape(8, 128)),
        [
            vmem((ROWS, SLOTS * PEERS), BF16),
            vmem((3, SLOTS * PEERS, 256), BF16),
            vmem((48, SLOTS * PEERS), F32),
            vmem((128, SLOTS * PEERS), BF16),
            vmem((56, 128), F32),
        ],
        inputs=4,
    )(place, got, mine, other_core(mine))
    pad = vmem((9 * 24, 128), F32)
    image_scratch = [pad, vmem(((K + 8) * CY, 128), F32)]
    image_outs = (shape(3 * CY, 128), shape(PEERS, 128))
    one = lax.dynamic_update_slice(one, other_core(one[24:32]), (24, 0))
    image_one, send, edge = call(
        functools.partial(image_kernel, 1), (*image_outs, shape(3 * K + 8, 128)), image_scratch, inputs=6
    )(place, main, ext, swap(one, 0), swap(one, 1), one)
    other = other_core(edge)
    sums = exchange(send)
    two, weights, h_one = call(next_kernel, (plane, shape(K, 128), shape(8, 128)), inputs=6)(
        sums, main, image_one, one, other, inverse
    )
    image_two, send = call(functools.partial(image_kernel, 2), image_outs, image_scratch, inputs=7)(
        place, main, ext, swap(two, 0), swap(two, 1), one, two
    )
    sums = exchange(send)
    wire, y = call(send_kernel, (shape(PEERS * 3, 128), shape(8, 128)), inputs=8)(
        sums, inverse, start, weights, h_one, beta, basis_u, info
    )
    got = exchange(wire)
    return call(
        last_kernel,
        (shape(3, ROWS), shape(3, ROWS)),
        [vmem((3, 48, SLOTS * PEERS), F32), vmem((3, 256, SLOTS * PEERS), BF16), pad],
        inputs=9,
    )(place, got, main, ext, y, one, two, image_one, image_two)


def solution(mesh):
    torus = Mesh(mesh.devices.reshape(4, 4, 4, mesh.shape["gy"]), ("gx_0", "gx_1", "gx_2", "gy"))
    placed = (P(None, GX_GY), P(None, GX_GY), P(None, GX_GY), P(None, GX_GY), P(GX_GY))
    return jax.shard_map(
        body,
        mesh=torus,
        in_specs=placed,
        out_specs=(P(None, GX_GY), P(None, GX_GY)),
        check_vma=False,
    )
```

```python
import functools

import jax
import jax.numpy as jnp
from jax import lax
from jax.experimental import pallas as pl
from jax.experimental.pallas import tpu as pltpu
from jax.sharding import Mesh
from jax.sharding import PartitionSpec as P

CY = 8
CZ = 128
K = 48
SLOTS = 16
PEERS = 128
ROWS = 1024
N_GX = 64
GX_GY = ("gx_0", "gx_1", "gx_2", "gy")
GX = ("gx_0", "gx_1", "gx_2")
F32 = jnp.float32
BF16 = jnp.bfloat16
HIGHEST = lax.Precision.HIGHEST
SIDE = K + 1
BANDS = 25
GRAM = 10
HALF = GRAM // 2
WIRE = 49 + HALF
CHUNKS = 8
NT = (((1,), (1,)), ((), ()))
TN = (((0,), (0,)), ((), ()))
MAIN = 3 * 128


def split(x):
    high = x.astype(BF16)
    return high, (x - high.astype(F32)).astype(BF16)


def exact_dot(x, y, dims=(((1,), (0,)), ((), ()))):
    return lax.dot_general(x, y, dims, precision=HIGHEST, preferred_element_type=F32)


def chosen(mask):
    return jnp.where(mask, jnp.ones(mask.shape, BF16), jnp.zeros(mask.shape, BF16))


def half_sum(x):
    return x[:, :128] + x[:, 128:]


def squared(x):
    x = jnp.concatenate([x, jnp.zeros((64, 64), F32)], axis=1)
    return jnp.concatenate([x, jnp.zeros((64, 128), F32)], axis=0)


def folded(rows, start_ref):
    twice = rows + pltpu.roll(rows, SIDE, 1)
    sub = lax.broadcasted_iota(jnp.int32, (8, 128), 0)
    for tile in range(7):
        here = twice[tile * 8 : (tile + 1) * 8]
        total = jnp.zeros((8, 128), F32)
        for r in range(8):
            i = tile * 8 + r
            if i < SIDE:
                moved = pltpu.roll(here, (128 - i + BANDS * (i // GRAM)) % 128, 1)
                total = jnp.where(sub == r, moved, total)
        start_ref[tile * 8 : (tile + 1) * 8, :] = total
    lane = lax.broadcasted_iota(jnp.int32, (GRAM, 128), 1)
    return sum(
        jnp.where(lane // BANDS == g, start_ref[g * GRAM : (g + 1) * GRAM, :], 0.0) for g in range(5)
    )


def unfolded(bands, start_ref):
    sub = lax.broadcasted_iota(jnp.int32, (8, 128), 0)
    lane = lax.broadcasted_iota(jnp.int32, (GRAM, 128), 1)
    start_ref[48:56, :] = jnp.zeros((8, 128), F32)
    for g in range(5):
        start_ref[g * GRAM : (g + 1) * GRAM, :] = jnp.where(lane // BANDS == g, bands, 0.0)
    tiles = []
    for tile in range(7):
        here = start_ref[tile * 8 : (tile + 1) * 8, :]
        total = jnp.zeros((8, 128), F32)
        for r in range(8):
            i = tile * 8 + r
            if i < SIDE:
                moved = pltpu.roll(here, (128 + i - BANDS * (i // GRAM)) % 128, 1)
                total = jnp.where(sub == r, moved, total)
        tiles.append(total)
    half = jnp.concatenate(tiles + [jnp.zeros((72, 128), F32)], axis=0)
    row = lax.broadcasted_iota(jnp.int32, (128, 128), 0)
    lane = lax.broadcasted_iota(jnp.int32, (128, 128), 1)
    half = jnp.where(lane < SIDE, half + pltpu.roll(half, 128 - SIDE, 1), 0.0)
    return half + jnp.where(row == lane, 0.0, half.T)


def pieces(source, target, size):
    count = source.shape[0]
    parts = [pl.ds(i, min(size, count - i)) for i in range(0, count, size)]
    return [(source.at[part], target.at[part]) for part in parts]


def pack_kernel(
    op_hbm, c_hbm, b_hbm, rows_hbm, wire_hbm, info_ref,
    op_ref, c_ref, b_ref, rows_ref, p_ref, a_ref, fold_ref, wire_ref, in_sem, out_sem,
):
    copies = [
        pltpu.make_async_copy(source, target, in_sem.at[i])
        for i, (source, target) in enumerate(
            [(rows_hbm, rows_ref), (b_hbm, b_ref), *pieces(c_hbm, c_ref, 72), *pieces(op_hbm, op_ref, 128)]
        )
    ]
    for copy in copies:
        copy.start()
    copies[0].wait()
    new_rows = rows_ref[...]
    target = new_rows // ROWS
    local = new_rows % ROWS
    onehot = lax.broadcasted_iota(jnp.int32, (PEERS, ROWS), 0) == target
    onehot_f = jnp.where(onehot, 1.0, 0.0).astype(F32)
    onehot_b = onehot_f.astype(BF16)
    before = lax.broadcasted_iota(jnp.int32, (128, 128), 0) < lax.broadcasted_iota(jnp.int32, (128, 128), 1)
    before = jnp.where(before, 1.0, 0.0).astype(BF16)
    ones = jnp.ones((128, 128), BF16)
    seen = jnp.zeros((PEERS, 128), F32)
    ranks = []
    for block in range(ROWS // 128):
        part = onehot_b[:, block * 128 : (block + 1) * 128]
        count = jnp.dot(part, before, preferred_element_type=F32) + seen
        ranks.append(jnp.sum(onehot_f[:, block * 128 : (block + 1) * 128] * count, axis=0, keepdims=True))
        seen = seen + jnp.dot(part, ones, preferred_element_type=F32)
    rank = jnp.concatenate(ranks, axis=1)
    rank_at = jnp.where(onehot, rank, -1.0).astype(BF16)
    info_ref[0:1, :] = target
    info_ref[1:2, :] = rank.astype(jnp.int32)
    info_ref[2:3, :] = local
    info_ref[3:8, :] = jnp.zeros((5, ROWS), jnp.int32)
    for copy in copies[1:]:
        copy.wait()

    def put(tile, x):
        p_ref[:, tile * 256 : tile * 256 + 128], p_ref[:, tile * 256 + 128 : (tile + 1) * 256] = split(x.T)

    put(0, c_ref[0:128, :])
    put(1, jnp.concatenate([c_ref[128:144, :], op_ref[0:112, :]], axis=0))
    put(2, op_ref[112:240, :])
    sums, low = jnp.zeros((192, 64), F32), jnp.zeros((64, 64), F32)
    for a in range(3):
        a_ref[a, 48:64, :] = jnp.zeros((16, ROWS), F32)
        a_ref[a, 0:48, :] = c_ref[a * K : (a + 1) * K, :]
        a_ref[a, 48:49, :] = b_ref[a : a + 1, :]
        one, two = split(a_ref[a])
        three = (a_ref[a] - one.astype(F32) - two.astype(F32)).astype(BF16)
        terms = jnp.concatenate([one, two, three], axis=0)
        sums = sums + lax.dot_general(terms, one, NT, preferred_element_type=F32)
        low = low + lax.dot_general(two, two, NT, preferred_element_type=F32)
    cross = squared(sums[64:128] + sums[128:192])
    gram = squared(sums[0:64] + low) + cross + cross.T
    bands = folded(gram[0:64], fold_ref)
    second = lax.broadcasted_iota(jnp.int32, (PEERS, 128), 0) % 2 == 1
    for i in range(HALF):
        wire_ref[pl.ds(49 + i, PEERS, stride=WIRE), :] = jnp.where(
            second, bands[HALF + i : HALF + i + 1, :], bands[i : i + 1, :]
        )
    at_rank = lax.broadcasted_iota(jnp.int32, (SLOTS, ROWS), 0).astype(F32) == rank
    rest = [op_ref[240 + i : 241 + i, :] for i in range(3)] + [b_ref[i : i + 1, :] for i in range(3)]
    rest = [jnp.where(at_rank, row, 0.0) for row in rest + [local.astype(F32)]]
    rest = jnp.concatenate(rest + [jnp.zeros((SLOTS, ROWS), F32)], axis=0)
    rest = jnp.concatenate(split(rest), axis=0)
    wire_ref[pl.ds(48, PEERS, stride=WIRE), :] = half_sum(
        lax.dot_general(onehot_b, rest, NT, preferred_element_type=F32)
    )
    sent = []
    count = PEERS // CHUNKS
    for chunk in range(CHUNKS):
        mine = rank_at[chunk * count : (chunk + 1) * count]
        choice = [chosen(mine == k) for k in range(SLOTS)]
        moved = jnp.dot(jnp.concatenate(choice, axis=0), p_ref[...], preferred_element_type=F32)
        for tile in range(3):
            both = half_sum(moved[:, tile * 256 : (tile + 1) * 256])
            for k in range(SLOTS):
                wire_ref[pl.ds(chunk * count * WIRE + tile * SLOTS + k, count, stride=WIRE), :] = both[
                    k * count : (k + 1) * count
                ]
        rows = pl.ds(chunk * count * WIRE, count * WIRE)
        sent.append(pltpu.make_async_copy(wire_ref.at[rows], wire_hbm.at[rows], out_sem.at[chunk]))
        sent[-1].start()
    for copy in sent:
        copy.wait()


def two_level(groups, left_ref, right_ref):
    eight = lax.broadcasted_iota(jnp.int32, (CY, 128), 0)
    deep = lax.broadcasted_iota(jnp.int32, (128, 128), 0).astype(F32).astype(BF16)
    count = groups[0][0].shape[0] // SLOTS
    for g, (values, labels) in enumerate(groups):
        labels = labels.astype(jnp.int32)
        y, z = labels // CZ, (labels % CZ).astype(F32)
        for k in range(SLOTS):
            cols = slice(k * 128, (k + 1) * 128)
            row = jnp.broadcast_to(z[k : k + 1], (128, 128)).astype(BF16)
            right_ref[g * 128 : (g + 1) * 128, cols] = chosen(deep == row)
            here = eight == y[k : k + 1]
            for c in range(count):
                row = (g * count + c) * CY
                value = values[c * SLOTS + k : c * SLOTS + k + 1]
                left_ref[row : row + CY, cols] = jnp.where(here, value, 0.0)
    rows = len(groups) * count * CY
    left = jnp.concatenate(split(left_ref[...]), axis=0)
    moved = lax.dot_general(left, right_ref[...], NT, preferred_element_type=F32)
    moved = moved[0:rows] + moved[rows:]
    size = count * CY
    return [moved[g * size : (g + 1) * size, g * 128 : (g + 1) * 128] for g in range(len(groups))]


def minus_combined(start, main_ref, weights):
    result = []
    for a in range(3):
        total = start[a]
        for m in range(K):
            row = (a * K + m) * CY
            total = total - main_ref[row : row + CY, :] * weights[m : m + 1, :]
        result.append(total)
    return result


def put_vector(vector, lines, v_ref):
    v_ref[24:32, :] = jnp.zeros((8, 128), F32)
    for a in range(3):
        v_ref[a * CY : (a + 1) * CY, :] = vector[a]
        v_ref[24 + a : 25 + a, :] = lines[a]


def swept(work, begin, count):
    row_id = lax.broadcasted_iota(jnp.int32, (K, 128), 0)
    columns = [jnp.broadcast_to(work[:, j : j + 1], (K, 128)) for j in range(begin, begin + count)]
    for s in range(count):
        j = begin + s
        column = columns[s]
        inverse = 1.0 / column[j : j + 1, :]
        here = row_id == j

        def step(x):
            pivot = x[j : j + 1, :] * inverse
            return jnp.where(here, pivot, x - column * pivot)

        work = step(work)
        columns = columns[: s + 1] + [step(c) for c in columns[s + 1 :]]
    return work


def unpack_kernel(
    place_ref, wire_ref, mine_ref, other_ref, main_ref, ext_ref, v_ref, inv_ref, start_ref, beta_ref,
    t_ref, r_ref, left_ref, right_ref, fold_ref,
):
    deep = lax.broadcasted_iota(jnp.int32, (CZ, 128), 0).astype(F32).astype(BF16)
    lower = place_ref[0:1, :] == 0
    mine, other = mine_ref[0:HALF, :], other_ref[0:HALF, :]
    bands = jnp.concatenate([jnp.where(lower, mine, other), jnp.where(lower, other, mine)], axis=0)
    gram = unfolded(bands, fold_ref)
    load_sq = jnp.broadcast_to(gram[48:49, 48:49], (1, 128))
    row_id = lax.broadcasted_iota(jnp.int32, (K, 128), 0)
    lane = lax.broadcasted_iota(jnp.int32, (K, 128), 1)
    raw = jnp.broadcast_to(gram[0:K, K : K + 1], (K, 128))
    work = jnp.where(lane < K + 1, gram[0:K], jnp.where(lane - 64 == row_id, 1.0, 0.0))
    for begin in range(0, K, 4):
        work = swept(work, begin, 4)
    rest = wire_ref[48].T
    labels = rest[6 * SLOTS : 7 * SLOTS]
    whole = labels.astype(jnp.int32)
    label_y, label_z = (whole // CZ).astype(F32), (whole % CZ).astype(F32)
    for k in range(SLOTS):
        here = chosen(deep == jnp.broadcast_to(label_z[k : k + 1], (CZ, 128)).astype(BF16))
        row = jnp.broadcast_to(label_y[k : k + 1], (CZ, 128)).astype(BF16)
        for y in range(CY):
            t_ref[y * CZ : (y + 1) * CZ, k * 128 : (k + 1) * 128] = jnp.where(
                row == y, here, jnp.zeros((CZ, 128), BF16)
            )
    for tile in range(3):
        for k in range(SLOTS):
            high, low = split(wire_ref[tile * SLOTS + k])
            r_ref[tile, k * 128 : (k + 1) * 128, 0:128] = high
            r_ref[tile, k * 128 : (k + 1) * 128, 128:256] = low
        moved = half_sum(jnp.dot(t_ref[...], r_ref[tile], preferred_element_type=F32))
        for y in range(CY):
            main_ref[pl.ds(tile * 128 * CY + y, 128, stride=CY), :] = moved[y * CZ : (y + 1) * CZ].T
    [ext] = two_level([(rest[0 : 6 * SLOTS], labels)], left_ref, right_ref)
    ext_ref[...] = ext

    inverse = jnp.where(lane < K, pltpu.roll(work, 64, 1), 0.0)
    weights = jnp.broadcast_to(work[:, K : K + 1], (K, 128))
    inv_ref[...] = inverse
    start_ref[...] = weights
    beta = jnp.sqrt(load_sq - jnp.sum(raw * weights, axis=0, keepdims=True))
    beta_ref[...] = jnp.broadcast_to(beta, (8, 128))
    load = [ext[24 + a * CY : 24 + (a + 1) * CY, :] for a in range(3)]
    vector = [v / beta for v in minus_combined(load, main_ref, weights)]
    put_vector(vector, [jnp.where(lower, v[CY - 1 : CY], v[0:1]) for v in vector], v_ref)


def put_plane(pad_ref, dx, plane, line, side):
    for a in range(3):
        base = (dx * 3 + a) * 24
        edge = line[a : a + 1, :]
        pad_ref[base + 7 : base + 8, :] = jnp.where(side == 1, edge, 0.0)
        pad_ref[base + 8 : base + 16, :] = plane[a * CY : (a + 1) * CY, :]
        pad_ref[base + 16 : base + 17, :] = jnp.where(side == 0, edge, 0.0)


def stencil(main_ref, ext_ref, pad_ref):
    lane = lax.broadcasted_iota(jnp.int32, (CY, 128), 1)
    total = [jnp.zeros((CY, 128), F32) for _ in range(3)]
    for dx in range(3):
        for dy in range(3):
            for b in range(3):
                start = (dx * 3 + b) * 24 + 7 + dy
                here = pad_ref[start : start + CY, :]
                left = jnp.where(lane == 0, 0.0, pltpu.roll(here, 1, 1))
                right = jnp.where(lane == 127, 0.0, pltpu.roll(here, 127, 1))
                for dz, moved in enumerate((left, here, right)):
                    for a in range(3):
                        q = ((dx * 9 + dy * 3 + dz) * 3 + a) * 3 + b
                        if q < 240:
                            row = (3 * K + q) * CY
                            total[a] = total[a] + main_ref[row : row + CY, :] * moved
                        else:
                            row = (q - 240) * CY
                            total[a] = total[a] + ext_ref[row : row + CY, :] * moved
    return total


def image_kernel(count, place_ref, main_ref, ext_ref, first_ref, second_ref, *refs):
    vectors, (image_ref, send_ref, *edges, pad_ref, part_ref) = refs[:count], refs[count:]
    side = place_ref[0:1, :]
    even = place_ref[1:2, :] == 0
    first, second = first_ref[...], second_ref[...]
    up, down = jnp.where(even, second, first), jnp.where(even, first, second)
    put_plane(pad_ref, 0, up[0:24], up[24:32], side)
    put_plane(pad_ref, 1, vectors[-1][0:24, :], vectors[-1][24:32, :], side)
    put_plane(pad_ref, 2, down[0:24], down[24:32], side)
    image = stencil(main_ref, ext_ref, pad_ref)
    for a in range(3):
        image_ref[a * CY : (a + 1) * CY, :] = image[a]
    for edge_ref in edges:
        last = main_ref[pl.ds(CY - 1, 3 * K, stride=CY), :]
        edge_ref[0 : 3 * K, :] = jnp.where(side == 0, last, main_ref[pl.ds(0, 3 * K, stride=CY), :])
        edge_ref[3 * K :, :] = jnp.zeros((8, 128), F32)
        for a in range(3):
            row = 3 * K + a
            edge_ref[row : row + 1, :] = jnp.where(side == 0, image[a][CY - 1 : CY], image[a][0:1])
    for m in range(K):
        rows = [(a * K + m) * CY for a in range(3)]
        part_ref[m * CY : (m + 1) * CY, :] = sum(
            main_ref[row : row + CY, :] * image[a] for a, row in enumerate(rows)
        )
    others = [image] + [[ref[a * CY : (a + 1) * CY, :] for a in range(3)] for ref in vectors]
    for i in range(8):
        m = K + i
        if i < len(others):
            part_ref[m * CY : (m + 1) * CY, :] = sum(o * w for o, w in zip(others[i], image))
        else:
            part_ref[m * CY : (m + 1) * CY, :] = jnp.zeros((CY, 128), F32)
    part = sum(part_ref[pl.ds(y, K + 8, stride=CY), :] for y in range(CY))
    part = jnp.concatenate([part, jnp.zeros((128 - K - 8, 128), F32)], axis=0)
    send_ref[...] = exact_dot(jnp.ones((PEERS, 128), F32), part, NT)


def totals(got_ref):
    return exact_dot(got_ref[...], jnp.ones((PEERS, 128), F32), TN)


def next_kernel(got_ref, main_ref, image_ref, one_ref, other_ref, inv_ref, v_ref, weights_ref, h_ref):
    sums = totals(got_ref)
    weights = exact_dot(inv_ref[...], sums)
    h11 = sums[K + 1 : K + 2, :]
    along = jnp.sum(sums[0:K] * weights, axis=0, keepdims=True)
    h21 = jnp.sqrt(sums[K : K + 1, :] - along - h11 * h11)
    begin = [
        image_ref[a * CY : (a + 1) * CY, :] - h11 * one_ref[a * CY : (a + 1) * CY, :] for a in range(3)
    ]
    vector = [v / h21 for v in minus_combined(begin, main_ref, weights)]
    lines = []
    for a in range(3):
        along_line = jnp.sum(other_ref[a * K : (a + 1) * K, :] * weights, axis=0, keepdims=True)
        line = other_ref[3 * K + a : 3 * K + a + 1, :] - along_line - h11 * one_ref[24 + a : 25 + a, :]
        lines.append(line / h21)
    put_vector(vector, lines, v_ref)
    weights_ref[...] = weights
    h_ref[...] = jnp.zeros((8, 128), F32)
    h_ref[0:1, :] = h11
    h_ref[1:2, :] = h21


def send_kernel(got_ref, inv_ref, start_ref, first_ref, h_ref, beta_ref, u_ref, info_ref, wire_ref, y_ref):
    sums = totals(got_ref)
    weights = exact_dot(inv_ref[...], sums)
    h11, h21 = h_ref[0:1, :], h_ref[1:2, :]
    h12, h22 = sums[K + 1 : K + 2, :], sums[K + 2 : K + 3, :]
    along = jnp.sum(sums[0:K] * weights, axis=0, keepdims=True)
    h32 = jnp.sqrt(sums[K : K + 1, :] - along - h12 * h12 - h22 * h22)
    beta = beta_ref[0:1, :]
    m11 = h11 * h11 + h21 * h21
    m12 = h11 * h12 + h21 * h22
    m22 = h12 * h12 + h22 * h22 + h32 * h32
    g_one = beta * h11
    g_two = beta * h12
    determ = m11 * m22 - m12 * m12
    y_one = (m22 * g_one - m12 * g_two) / determ
    y_two = (m11 * g_two - m12 * g_one) / determ
    y_ref[...] = jnp.zeros((8, 128), F32)
    y_ref[0:1, :] = y_one
    y_ref[1:2, :] = y_two
    weights = start_ref[...] - y_one * first_ref[...] - y_two * weights
    wide = jnp.concatenate([weights] * (ROWS // 128), axis=1)
    target, rank, local = (info_ref[i : i + 1, :] for i in range(3))
    at_rank = lax.broadcasted_iota(jnp.int32, (SLOTS, ROWS), 0) == rank
    rows = [jnp.sum(u_ref[a * K : (a + 1) * K, :] * wide, axis=0, keepdims=True) for a in range(3)]
    rows = jnp.concatenate([jnp.where(at_rank, r, 0.0) for r in rows + [local.astype(F32)]], axis=0)
    rows = jnp.concatenate(split(rows), axis=0)
    onehot = lax.broadcasted_iota(jnp.int32, (PEERS, ROWS), 0) == target
    onehot = jnp.where(onehot, 1.0, 0.0).astype(BF16)
    mine = lax.dot_general(onehot, rows, NT, preferred_element_type=F32)
    mine = mine + pltpu.roll(mine, 64, 1)
    peer = lax.broadcasted_iota(jnp.int32, (PEERS, 128), 0)
    lane = lax.broadcasted_iota(jnp.int32, (PEERS, 128), 1)
    other = jnp.where(peer % 2 == 0, pltpu.roll(mine, PEERS - 1, 0), pltpu.roll(mine, 1, 0))
    pair = jnp.where(lane < 64, mine, other)
    wire_ref[pl.ds(0, PEERS, stride=3), :] = jnp.where(peer < 2, 0.0, pltpu.roll(pair, 2, 0))
    wire_ref[pl.ds(1, PEERS, stride=3), :] = pair
    wire_ref[pl.ds(2, PEERS, stride=3), :] = jnp.where(peer >= PEERS - 2, 0.0, pltpu.roll(pair, PEERS - 2, 0))


def last_kernel(
    place_ref, got_ref, main_ref, ext_ref, y_ref, one_ref, two_ref, im_one_ref, im_two_ref,
    sol_ref, res_ref, left_ref, right_ref, pad_ref,
):
    side = place_ref[0:1, :]
    for dx in range(3):
        got = got_ref[pl.ds(dx, PEERS, stride=3), :].T
        own, other = two_level(
            [(got[base : base + 48], got[base + 48 : base + 64]) for base in (0, 64)],
            left_ref.at[dx],
            right_ref.at[dx],
        )
        lines = [
            jnp.where(side == 0, other[a * CY : a * CY + 1, :], other[a * CY + 7 : a * CY + 8, :]) for a in range(3)
        ]
        put_plane(pad_ref, dx, own, jnp.concatenate(lines, axis=0), side)
        if dx == 1:
            term = own
    image = stencil(main_ref, ext_ref, pad_ref)
    y_one, y_two = y_ref[0:1, :], y_ref[1:2, :]
    solution = term + y_one * one_ref[0:24, :] + y_two * two_ref[0:24, :]
    for a in range(3):
        rows = slice(a * CY, (a + 1) * CY)
        residual = ext_ref[24 + a * CY : 24 + (a + 1) * CY, :] - image[a]
        residual = residual - y_one * im_one_ref[rows, :] - y_two * im_two_ref[rows, :]
        for y in range(CY):
            cols = slice(y * CZ, (y + 1) * CZ)
            sol_ref[a : a + 1, cols] = solution[a * CY + y : a * CY + y + 1, :]
            res_ref[a : a + 1, cols] = residual[y : y + 1, :]


def shape(*dims, dtype=F32):
    return jax.ShapeDtypeStruct(dims, dtype)


def specs(*spaces):
    return tuple(pl.BlockSpec(memory_space=space) for space in spaces)


def call(kernel, outs, scratch=(), inputs=0, in_specs=None, out_specs=None, limit=40):
    vmem = pltpu.VMEM
    return pl.pallas_call(
        kernel,
        out_shape=outs,
        in_specs=in_specs or specs(*[vmem] * inputs),
        out_specs=out_specs or specs(*[vmem] * len(outs)),
        scratch_shapes=list(scratch),
        compiler_params=pltpu.CompilerParams(vmem_limit_bytes=limit * 2**20),
    )


def exchange(rows):
    count = rows.shape[0] // PEERS
    shaped = rows.reshape(PEERS, count, 1, 128)
    got = lax.all_to_all(shaped, GX_GY, split_axis=0, concat_axis=0, tiled=True)
    return got.reshape(PEERS * count, 128)


def swap(plane, first):
    pairs = [(i, i + 1) for i in range(first, N_GX - 1, 2)]
    return lax.ppermute(plane, GX, pairs + [(j, i) for i, j in pairs])


def other_core(x):
    return lax.ppermute(x, "gy", [(0, 1), (1, 0)])


def body(operator, basis_u, basis_c, right_side, new_rows):
    row = lax.broadcasted_iota(jnp.int32, (8, 128), 0)
    place = jnp.where(row == 0, lax.axis_index("gy"), lax.axis_index(GX) % 2).astype(jnp.int32)
    vmem, hbm = pltpu.VMEM, pltpu.HBM
    wire, info = call(
        pack_kernel,
        (shape(PEERS * WIRE, 128), shape(8, ROWS, dtype=jnp.int32)),
        [
            vmem((243, ROWS), F32),
            vmem((144, ROWS), F32),
            vmem((3, ROWS), F32),
            vmem((1, ROWS), jnp.int32),
            vmem((ROWS, 2 * MAIN), BF16),
            vmem((3, 64, ROWS), F32),
            vmem((56, 128), F32),
            vmem((PEERS * WIRE, 128), F32),
            pltpu.SemaphoreType.DMA((6,)),
            pltpu.SemaphoreType.DMA((CHUNKS,)),
        ],
        in_specs=specs(hbm, hbm, hbm, hbm),
        out_specs=specs(hbm, vmem),
        limit=56,
    )(operator, basis_c, right_side, new_rows.reshape(1, ROWS))
    got = exchange(wire)
    got = got.reshape(PEERS, WIRE, 128).transpose(1, 0, 2)
    mine = jnp.sum(got[49:], axis=1)
    plane = shape(32, 128)
    main, ext, one, inverse, start, beta = call(
        unpack_kernel,
        (shape(MAIN * CY, 128), shape(48, 128), plane, shape(K, 128), shape(K, 128), shape(8, 128)),
        [
            vmem((ROWS, SLOTS * PEERS), BF16),
            vmem((3, SLOTS * PEERS, 256), BF16),
            vmem((48, SLOTS * PEERS), F32),
            vmem((128, SLOTS * PEERS), BF16),
            vmem((56, 128), F32),
        ],
        inputs=4,
    )(place, got, mine, other_core(mine))
    pad = vmem((9 * 24, 128), F32)
    image_scratch = [pad, vmem(((K + 8) * CY, 128), F32)]
    image_outs = (shape(3 * CY, 128), shape(PEERS, 128))
    one = lax.dynamic_update_slice(one, other_core(one[24:32]), (24, 0))
    image_one, send, edge = call(
        functools.partial(image_kernel, 1), (*image_outs, shape(3 * K + 8, 128)), image_scratch, inputs=6
    )(place, main, ext, swap(one, 0), swap(one, 1), one)
    other = other_core(edge)
    sums = exchange(send)
    two, weights, h_one = call(next_kernel, (plane, shape(K, 128), shape(8, 128)), inputs=6)(
        sums, main, image_one, one, other, inverse
    )
    image_two, send = call(functools.partial(image_kernel, 2), image_outs, image_scratch, inputs=7)(
        place, main, ext, swap(two, 0), swap(two, 1), one, two
    )
    sums = exchange(send)
    wire, y = call(send_kernel, (shape(PEERS * 3, 128), shape(8, 128)), inputs=8)(
        sums, inverse, start, weights, h_one, beta, basis_u, info
    )
    got = exchange(wire)
    return call(
        last_kernel,
        (shape(3, ROWS), shape(3, ROWS)),
        [vmem((3, 48, SLOTS * PEERS), F32), vmem((3, 256, SLOTS * PEERS), BF16), pad],
        inputs=9,
    )(place, got, main, ext, y, one, two, image_one, image_two)


def solution(mesh):
    torus = Mesh(mesh.devices.reshape(4, 4, 4, mesh.shape["gy"]), ("gx_0", "gx_1", "gx_2", "gy"))
    placed = (P(None, GX_GY), P(None, GX_GY), P(None, GX_GY), P(None, GX_GY), P(GX_GY))
    return jax.shard_map(
        body,
        mesh=torus,
        in_specs=placed,
        out_specs=(P(None, GX_GY), P(None, GX_GY)),
        check_vma=False,
    )
```

```python
import functools

import jax
import jax.numpy as jnp
from jax import lax
from jax.experimental import pallas as pl
from jax.experimental.pallas import tpu as pltpu
from jax.sharding import Mesh
from jax.sharding import PartitionSpec as P

CY = 8
CZ = 128
K = 48
SLOTS = 16
PEERS = 128
ROWS = 1024
N_GX = 64
GX_GY = ("gx_0", "gx_1", "gx_2", "gy")
GX = ("gx_0", "gx_1", "gx_2")
F32 = jnp.float32
BF16 = jnp.bfloat16
HIGHEST = lax.Precision.HIGHEST
SIDE = K + 1
BANDS = 25
GRAM = 10
HALF = GRAM // 2
WIRE = 49 + HALF
CHUNKS = 8
NT = (((1,), (1,)), ((), ()))
TN = (((0,), (0,)), ((), ()))
MAIN = 3 * 128
EARLY = 2 * 128 - 3 * K


def split(x):
    high = x.astype(BF16)
    return high, (x - high.astype(F32)).astype(BF16)


def exact_dot(x, y, dims=(((1,), (0,)), ((), ()))):
    return lax.dot_general(x, y, dims, precision=HIGHEST, preferred_element_type=F32)


def chosen(mask):
    return jnp.where(mask, jnp.ones(mask.shape, BF16), jnp.zeros(mask.shape, BF16))


def half_sum(x):
    return x[:, :128] + x[:, 128:]


def squared(x):
    x = jnp.concatenate([x, jnp.zeros((64, 64), F32)], axis=1)
    return jnp.concatenate([x, jnp.zeros((64, 128), F32)], axis=0)


def folded(rows, start_ref):
    twice = rows + pltpu.roll(rows, SIDE, 1)
    sub = lax.broadcasted_iota(jnp.int32, (8, 128), 0)
    for tile in range(7):
        here = twice[tile * 8 : (tile + 1) * 8]
        total = jnp.zeros((8, 128), F32)
        for r in range(8):
            i = tile * 8 + r
            if i < SIDE:
                moved = pltpu.roll(here, (128 - i + BANDS * (i // GRAM)) % 128, 1)
                total = jnp.where(sub == r, moved, total)
        start_ref[tile * 8 : (tile + 1) * 8, :] = total
    lane = lax.broadcasted_iota(jnp.int32, (GRAM, 128), 1)
    return sum(
        jnp.where(lane // BANDS == g, start_ref[g * GRAM : (g + 1) * GRAM, :], 0.0) for g in range(5)
    )


def unfolded(bands, start_ref):
    sub = lax.broadcasted_iota(jnp.int32, (8, 128), 0)
    lane = lax.broadcasted_iota(jnp.int32, (GRAM, 128), 1)
    start_ref[48:56, :] = jnp.zeros((8, 128), F32)
    for g in range(5):
        start_ref[g * GRAM : (g + 1) * GRAM, :] = jnp.where(lane // BANDS == g, bands, 0.0)
    tiles = []
    for tile in range(7):
        here = start_ref[tile * 8 : (tile + 1) * 8, :]
        total = jnp.zeros((8, 128), F32)
        for r in range(8):
            i = tile * 8 + r
            if i < SIDE:
                moved = pltpu.roll(here, (128 + i - BANDS * (i // GRAM)) % 128, 1)
                total = jnp.where(sub == r, moved, total)
        tiles.append(total)
    half = jnp.concatenate(tiles + [jnp.zeros((72, 128), F32)], axis=0)
    row = lax.broadcasted_iota(jnp.int32, (128, 128), 0)
    lane = lax.broadcasted_iota(jnp.int32, (128, 128), 1)
    half = jnp.where(lane < SIDE, half + pltpu.roll(half, 128 - SIDE, 1), 0.0)
    return half + jnp.where(row == lane, 0.0, half.T)


def pieces(source, target, size):
    count = source.shape[0]
    parts = [pl.ds(i, min(size, count - i)) for i in range(0, count, size)]
    return [(source.at[part], target.at[part]) for part in parts]


def pack_kernel(
    op_hbm, c_hbm, b_hbm, rows_hbm, wire_hbm, info_ref,
    op_ref, c_ref, b_ref, rows_ref, p_ref, a_ref, fold_ref, wire_ref, in_sem, out_sem,
):
    copies = [
        pltpu.make_async_copy(source, target, in_sem.at[i])
        for i, (source, target) in enumerate(
            [(rows_hbm, rows_ref), (b_hbm, b_ref), *pieces(c_hbm, c_ref, 72), *pieces(op_hbm, op_ref, 128)]
        )
    ]
    for copy in copies:
        copy.start()
    copies[0].wait()
    new_rows = rows_ref[...]
    target = new_rows // ROWS
    local = new_rows % ROWS
    onehot = lax.broadcasted_iota(jnp.int32, (PEERS, ROWS), 0) == target
    onehot_f = jnp.where(onehot, 1.0, 0.0).astype(F32)
    onehot_b = onehot_f.astype(BF16)
    before = lax.broadcasted_iota(jnp.int32, (128, 128), 0) < lax.broadcasted_iota(jnp.int32, (128, 128), 1)
    before = jnp.where(before, 1.0, 0.0).astype(BF16)
    ones = jnp.ones((128, 128), BF16)
    seen = jnp.zeros((PEERS, 128), F32)
    ranks = []
    for block in range(ROWS // 128):
        part = onehot_b[:, block * 128 : (block + 1) * 128]
        count = jnp.dot(part, before, preferred_element_type=F32) + seen
        ranks.append(jnp.sum(onehot_f[:, block * 128 : (block + 1) * 128] * count, axis=0, keepdims=True))
        seen = seen + jnp.dot(part, ones, preferred_element_type=F32)
    rank = jnp.concatenate(ranks, axis=1)
    rank_at = jnp.where(onehot, rank, -1.0).astype(BF16)
    info_ref[0:1, :] = target
    info_ref[1:2, :] = rank.astype(jnp.int32)
    info_ref[2:3, :] = local
    info_ref[3:8, :] = jnp.zeros((5, ROWS), jnp.int32)
    for copy in copies[1:]:
        copy.wait()

    def put(tile, x):
        p_ref[:, tile * 256 : tile * 256 + 128], p_ref[:, tile * 256 + 128 : (tile + 1) * 256] = split(x.T)

    put(0, c_ref[0:128, :])
    put(1, jnp.concatenate([c_ref[128:144, :], op_ref[0:112, :]], axis=0))
    put(2, op_ref[112:240, :])
    sums, low = jnp.zeros((192, 64), F32), jnp.zeros((64, 64), F32)
    for a in range(3):
        a_ref[a, 48:64, :] = jnp.zeros((16, ROWS), F32)
        a_ref[a, 0:48, :] = c_ref[a * K : (a + 1) * K, :]
        a_ref[a, 48:49, :] = b_ref[a : a + 1, :]
        one, two = split(a_ref[a])
        three = (a_ref[a] - one.astype(F32) - two.astype(F32)).astype(BF16)
        terms = jnp.concatenate([one, two, three], axis=0)
        sums = sums + lax.dot_general(terms, one, NT, preferred_element_type=F32)
        low = low + lax.dot_general(two, two, NT, preferred_element_type=F32)
    cross = squared(sums[64:128] + sums[128:192])
    gram = squared(sums[0:64] + low) + cross + cross.T
    bands = folded(gram[0:64], fold_ref)
    second = lax.broadcasted_iota(jnp.int32, (PEERS, 128), 0) % 2 == 1
    for i in range(HALF):
        wire_ref[pl.ds(49 + i, PEERS, stride=WIRE), :] = jnp.where(
            second, bands[HALF + i : HALF + i + 1, :], bands[i : i + 1, :]
        )
    at_rank = lax.broadcasted_iota(jnp.int32, (SLOTS, ROWS), 0).astype(F32) == rank
    rest = [op_ref[240 + i : 241 + i, :] for i in range(3)] + [b_ref[i : i + 1, :] for i in range(3)]
    rest = [jnp.where(at_rank, row, 0.0) for row in rest + [local.astype(F32)]]
    rest = jnp.concatenate(rest + [jnp.zeros((SLOTS, ROWS), F32)], axis=0)
    rest = jnp.concatenate(split(rest), axis=0)
    wire_ref[pl.ds(48, PEERS, stride=WIRE), :] = half_sum(
        lax.dot_general(onehot_b, rest, NT, preferred_element_type=F32)
    )
    sent = []
    count = PEERS // CHUNKS
    for chunk in range(CHUNKS):
        mine = rank_at[chunk * count : (chunk + 1) * count]
        choice = [chosen(mine == k) for k in range(SLOTS)]
        moved = jnp.dot(jnp.concatenate(choice, axis=0), p_ref[...], preferred_element_type=F32)
        for tile in range(3):
            both = half_sum(moved[:, tile * 256 : (tile + 1) * 256])
            for k in range(SLOTS):
                wire_ref[pl.ds(chunk * count * WIRE + tile * SLOTS + k, count, stride=WIRE), :] = both[
                    k * count : (k + 1) * count
                ]
        rows = pl.ds(chunk * count * WIRE, count * WIRE)
        sent.append(pltpu.make_async_copy(wire_ref.at[rows], wire_hbm.at[rows], out_sem.at[chunk]))
        sent[-1].start()
    for copy in sent:
        copy.wait()


def two_level(groups, left_ref, right_ref):
    eight = lax.broadcasted_iota(jnp.int32, (CY, 128), 0)
    deep = lax.broadcasted_iota(jnp.int32, (128, 128), 0).astype(F32).astype(BF16)
    count = groups[0][0].shape[0] // SLOTS
    for g, (values, labels) in enumerate(groups):
        labels = labels.astype(jnp.int32)
        y, z = labels // CZ, (labels % CZ).astype(F32)
        for k in range(SLOTS):
            cols = slice(k * 128, (k + 1) * 128)
            row = jnp.broadcast_to(z[k : k + 1], (128, 128)).astype(BF16)
            right_ref[g * 128 : (g + 1) * 128, cols] = chosen(deep == row)
            here = eight == y[k : k + 1]
            for c in range(count):
                row = (g * count + c) * CY
                value = values[c * SLOTS + k : c * SLOTS + k + 1]
                left_ref[row : row + CY, cols] = jnp.where(here, value, 0.0)
    rows = len(groups) * count * CY
    left = jnp.concatenate(split(left_ref[...]), axis=0)
    moved = lax.dot_general(left, right_ref[...], NT, preferred_element_type=F32)
    moved = moved[0:rows] + moved[rows:]
    size = count * CY
    return [moved[g * size : (g + 1) * size, g * 128 : (g + 1) * 128] for g in range(len(groups))]


def minus_combined(start, main_ref, weights):
    result = []
    for a in range(3):
        total = start[a]
        for m in range(K):
            row = (a * K + m) * CY
            total = total - main_ref[row : row + CY, :] * weights[m : m + 1, :]
        result.append(total)
    return result


def put_vector(vector, lines, v_ref):
    v_ref[24:32, :] = jnp.zeros((8, 128), F32)
    for a in range(3):
        v_ref[a * CY : (a + 1) * CY, :] = vector[a]
        v_ref[24 + a : 25 + a, :] = lines[a]


def swept(work, begin, count):
    row_id = lax.broadcasted_iota(jnp.int32, (K, 128), 0)
    columns = [jnp.broadcast_to(work[:, j : j + 1], (K, 128)) for j in range(begin, begin + count)]
    for s in range(count):
        j = begin + s
        column = columns[s]
        inverse = 1.0 / column[j : j + 1, :]
        here = row_id == j

        def step(x):
            pivot = x[j : j + 1, :] * inverse
            return jnp.where(here, pivot, x - column * pivot)

        work = step(work)
        columns = columns[: s + 1] + [step(c) for c in columns[s + 1 :]]
    return work


def put_table(labels, t_ref):
    deep = lax.broadcasted_iota(jnp.int32, (CZ, 128), 0).astype(F32).astype(BF16)
    whole = labels.astype(jnp.int32)
    label_y, label_z = (whole // CZ).astype(F32), (whole % CZ).astype(F32)
    for k in range(SLOTS):
        here = chosen(deep == jnp.broadcast_to(label_z[k : k + 1], (CZ, 128)).astype(BF16))
        row = jnp.broadcast_to(label_y[k : k + 1], (CZ, 128)).astype(BF16)
        for y in range(CY):
            t_ref[y * CZ : (y + 1) * CZ, k * 128 : (k + 1) * 128] = jnp.where(
                row == y, here, jnp.zeros((CZ, 128), BF16)
            )


def put_tile(wire_ref, tile, t_ref, r_ref, out_ref, first):
    for k in range(SLOTS):
        high, low = split(wire_ref[tile * SLOTS + k])
        r_ref[k * 128 : (k + 1) * 128, 0:128] = high
        r_ref[k * 128 : (k + 1) * 128, 128:256] = low
    moved = half_sum(jnp.dot(t_ref[...], r_ref[...], preferred_element_type=F32))
    for y in range(CY):
        out_ref[pl.ds(first * CY + y, 128, stride=CY), :] = moved[y * CZ : (y + 1) * CZ].T


def late_kernel(wire_ref, late_ref, t_ref, r_ref):
    put_table(wire_ref[48].T[6 * SLOTS : 7 * SLOTS], t_ref)
    put_tile(wire_ref, 2, t_ref, r_ref, late_ref, 0)


def unpack_kernel(
    place_ref, wire_ref, mine_ref, other_ref, main_ref, ext_ref, v_ref, inv_ref, start_ref, beta_ref,
    t_ref, r_ref, left_ref, right_ref, fold_ref,
):
    lower = place_ref[0:1, :] == 0
    mine, other = mine_ref[0:HALF, :], other_ref[0:HALF, :]
    bands = jnp.concatenate([jnp.where(lower, mine, other), jnp.where(lower, other, mine)], axis=0)
    gram = unfolded(bands, fold_ref)
    load_sq = jnp.broadcast_to(gram[48:49, 48:49], (1, 128))
    row_id = lax.broadcasted_iota(jnp.int32, (K, 128), 0)
    lane = lax.broadcasted_iota(jnp.int32, (K, 128), 1)
    raw = jnp.broadcast_to(gram[0:K, K : K + 1], (K, 128))
    work = jnp.where(lane < K + 1, gram[0:K], jnp.where(lane - 64 == row_id, 1.0, 0.0))
    for begin in range(0, K, 4):
        work = swept(work, begin, 4)
    rest = wire_ref[48].T
    labels = rest[6 * SLOTS : 7 * SLOTS]
    put_table(labels, t_ref)
    for tile in range(2):
        put_tile(wire_ref, tile, t_ref, r_ref.at[tile], main_ref, tile * 128)
    [ext] = two_level([(rest[0 : 6 * SLOTS], labels)], left_ref, right_ref)
    ext_ref[...] = ext

    inverse = jnp.where(lane < K, pltpu.roll(work, 64, 1), 0.0)
    weights = jnp.broadcast_to(work[:, K : K + 1], (K, 128))
    inv_ref[...] = inverse
    start_ref[...] = weights
    beta = jnp.sqrt(load_sq - jnp.sum(raw * weights, axis=0, keepdims=True))
    beta_ref[...] = jnp.broadcast_to(beta, (8, 128))
    load = [ext[24 + a * CY : 24 + (a + 1) * CY, :] for a in range(3)]
    vector = [v / beta for v in minus_combined(load, main_ref, weights)]
    put_vector(vector, [jnp.where(lower, v[CY - 1 : CY], v[0:1]) for v in vector], v_ref)


def put_plane(pad_ref, dx, plane, line, side):
    for a in range(3):
        base = (dx * 3 + a) * 24
        edge = line[a : a + 1, :]
        pad_ref[base + 7 : base + 8, :] = jnp.where(side == 1, edge, 0.0)
        pad_ref[base + 8 : base + 16, :] = plane[a * CY : (a + 1) * CY, :]
        pad_ref[base + 16 : base + 17, :] = jnp.where(side == 0, edge, 0.0)


def stencil(main_ref, late_ref, ext_ref, pad_ref):
    lane = lax.broadcasted_iota(jnp.int32, (CY, 128), 1)
    total = [jnp.zeros((CY, 128), F32) for _ in range(3)]
    for dx in range(3):
        for dy in range(3):
            for b in range(3):
                start = (dx * 3 + b) * 24 + 7 + dy
                here = pad_ref[start : start + CY, :]
                left = jnp.where(lane == 0, 0.0, pltpu.roll(here, 1, 1))
                right = jnp.where(lane == 127, 0.0, pltpu.roll(here, 127, 1))
                for dz, moved in enumerate((left, here, right)):
                    for a in range(3):
                        q = ((dx * 9 + dy * 3 + dz) * 3 + a) * 3 + b
                        if q < EARLY:
                            source, row = main_ref, (3 * K + q) * CY
                        elif q < 240:
                            source, row = late_ref, (q - EARLY) * CY
                        else:
                            source, row = ext_ref, (q - 240) * CY
                        total[a] = total[a] + source[row : row + CY, :] * moved
    return total


def image_kernel(count, place_ref, main_ref, late_ref, ext_ref, first_ref, second_ref, *refs):
    vectors, (image_ref, send_ref, *edges, pad_ref, part_ref) = refs[:count], refs[count:]
    side = place_ref[0:1, :]
    even = place_ref[1:2, :] == 0
    first, second = first_ref[...], second_ref[...]
    up, down = jnp.where(even, second, first), jnp.where(even, first, second)
    put_plane(pad_ref, 0, up[0:24], up[24:32], side)
    put_plane(pad_ref, 1, vectors[-1][0:24, :], vectors[-1][24:32, :], side)
    put_plane(pad_ref, 2, down[0:24], down[24:32], side)
    image = stencil(main_ref, late_ref, ext_ref, pad_ref)
    for a in range(3):
        image_ref[a * CY : (a + 1) * CY, :] = image[a]
    for edge_ref in edges:
        last = main_ref[pl.ds(CY - 1, 3 * K, stride=CY), :]
        edge_ref[0 : 3 * K, :] = jnp.where(side == 0, last, main_ref[pl.ds(0, 3 * K, stride=CY), :])
        edge_ref[3 * K :, :] = jnp.zeros((8, 128), F32)
        for a in range(3):
            row = 3 * K + a
            edge_ref[row : row + 1, :] = jnp.where(side == 0, image[a][CY - 1 : CY], image[a][0:1])
    for m in range(K):
        rows = [(a * K + m) * CY for a in range(3)]
        part_ref[m * CY : (m + 1) * CY, :] = sum(
            main_ref[row : row + CY, :] * image[a] for a, row in enumerate(rows)
        )
    others = [image] + [[ref[a * CY : (a + 1) * CY, :] for a in range(3)] for ref in vectors]
    for i in range(8):
        m = K + i
        if i < len(others):
            part_ref[m * CY : (m + 1) * CY, :] = sum(o * w for o, w in zip(others[i], image))
        else:
            part_ref[m * CY : (m + 1) * CY, :] = jnp.zeros((CY, 128), F32)
    part = sum(part_ref[pl.ds(y, K + 8, stride=CY), :] for y in range(CY))
    part = jnp.concatenate([part, jnp.zeros((128 - K - 8, 128), F32)], axis=0)
    send_ref[...] = exact_dot(jnp.ones((PEERS, 128), F32), part, NT)


def totals(got_ref):
    return exact_dot(got_ref[...], jnp.ones((PEERS, 128), F32), TN)


def next_kernel(got_ref, main_ref, image_ref, one_ref, other_ref, inv_ref, v_ref, weights_ref, h_ref):
    sums = totals(got_ref)
    weights = exact_dot(inv_ref[...], sums)
    h11 = sums[K + 1 : K + 2, :]
    along = jnp.sum(sums[0:K] * weights, axis=0, keepdims=True)
    h21 = jnp.sqrt(sums[K : K + 1, :] - along - h11 * h11)
    begin = [
        image_ref[a * CY : (a + 1) * CY, :] - h11 * one_ref[a * CY : (a + 1) * CY, :] for a in range(3)
    ]
    vector = [v / h21 for v in minus_combined(begin, main_ref, weights)]
    lines = []
    for a in range(3):
        along_line = jnp.sum(other_ref[a * K : (a + 1) * K, :] * weights, axis=0, keepdims=True)
        line = other_ref[3 * K + a : 3 * K + a + 1, :] - along_line - h11 * one_ref[24 + a : 25 + a, :]
        lines.append(line / h21)
    put_vector(vector, lines, v_ref)
    weights_ref[...] = weights
    h_ref[...] = jnp.zeros((8, 128), F32)
    h_ref[0:1, :] = h11
    h_ref[1:2, :] = h21


def send_kernel(got_ref, inv_ref, start_ref, first_ref, h_ref, beta_ref, u_ref, info_ref, wire_ref, y_ref):
    sums = totals(got_ref)
    weights = exact_dot(inv_ref[...], sums)
    h11, h21 = h_ref[0:1, :], h_ref[1:2, :]
    h12, h22 = sums[K + 1 : K + 2, :], sums[K + 2 : K + 3, :]
    along = jnp.sum(sums[0:K] * weights, axis=0, keepdims=True)
    h32 = jnp.sqrt(sums[K : K + 1, :] - along - h12 * h12 - h22 * h22)
    beta = beta_ref[0:1, :]
    m11 = h11 * h11 + h21 * h21
    m12 = h11 * h12 + h21 * h22
    m22 = h12 * h12 + h22 * h22 + h32 * h32
    g_one = beta * h11
    g_two = beta * h12
    determ = m11 * m22 - m12 * m12
    y_one = (m22 * g_one - m12 * g_two) / determ
    y_two = (m11 * g_two - m12 * g_one) / determ
    y_ref[...] = jnp.zeros((8, 128), F32)
    y_ref[0:1, :] = y_one
    y_ref[1:2, :] = y_two
    weights = start_ref[...] - y_one * first_ref[...] - y_two * weights
    wide = jnp.concatenate([weights] * (ROWS // 128), axis=1)
    target, rank, local = (info_ref[i : i + 1, :] for i in range(3))
    at_rank = lax.broadcasted_iota(jnp.int32, (SLOTS, ROWS), 0) == rank
    rows = [jnp.sum(u_ref[a * K : (a + 1) * K, :] * wide, axis=0, keepdims=True) for a in range(3)]
    rows = jnp.concatenate([jnp.where(at_rank, r, 0.0) for r in rows + [local.astype(F32)]], axis=0)
    rows = jnp.concatenate(split(rows), axis=0)
    onehot = lax.broadcasted_iota(jnp.int32, (PEERS, ROWS), 0) == target
    onehot = jnp.where(onehot, 1.0, 0.0).astype(BF16)
    mine = lax.dot_general(onehot, rows, NT, preferred_element_type=F32)
    mine = mine + pltpu.roll(mine, 64, 1)
    peer = lax.broadcasted_iota(jnp.int32, (PEERS, 128), 0)
    lane = lax.broadcasted_iota(jnp.int32, (PEERS, 128), 1)
    other = jnp.where(peer % 2 == 0, pltpu.roll(mine, PEERS - 1, 0), pltpu.roll(mine, 1, 0))
    pair = jnp.where(lane < 64, mine, other)
    wire_ref[pl.ds(0, PEERS, stride=3), :] = jnp.where(peer < 2, 0.0, pltpu.roll(pair, 2, 0))
    wire_ref[pl.ds(1, PEERS, stride=3), :] = pair
    wire_ref[pl.ds(2, PEERS, stride=3), :] = jnp.where(peer >= PEERS - 2, 0.0, pltpu.roll(pair, PEERS - 2, 0))


def last_kernel(
    place_ref, got_ref, main_ref, late_ref, ext_ref, y_ref, one_ref, two_ref, im_one_ref, im_two_ref,
    sol_ref, res_ref, left_ref, right_ref, pad_ref,
):
    side = place_ref[0:1, :]
    for dx in range(3):
        got = got_ref[pl.ds(dx, PEERS, stride=3), :].T
        own, other = two_level(
            [(got[base : base + 48], got[base + 48 : base + 64]) for base in (0, 64)],
            left_ref.at[dx],
            right_ref.at[dx],
        )
        lines = [
            jnp.where(side == 0, other[a * CY : a * CY + 1, :], other[a * CY + 7 : a * CY + 8, :]) for a in range(3)
        ]
        put_plane(pad_ref, dx, own, jnp.concatenate(lines, axis=0), side)
        if dx == 1:
            term = own
    image = stencil(main_ref, late_ref, ext_ref, pad_ref)
    y_one, y_two = y_ref[0:1, :], y_ref[1:2, :]
    solution = term + y_one * one_ref[0:24, :] + y_two * two_ref[0:24, :]
    for a in range(3):
        rows = slice(a * CY, (a + 1) * CY)
        residual = ext_ref[24 + a * CY : 24 + (a + 1) * CY, :] - image[a]
        residual = residual - y_one * im_one_ref[rows, :] - y_two * im_two_ref[rows, :]
        for y in range(CY):
            cols = slice(y * CZ, (y + 1) * CZ)
            sol_ref[a : a + 1, cols] = solution[a * CY + y : a * CY + y + 1, :]
            res_ref[a : a + 1, cols] = residual[y : y + 1, :]


def shape(*dims, dtype=F32):
    return jax.ShapeDtypeStruct(dims, dtype)


def specs(*spaces):
    return tuple(pl.BlockSpec(memory_space=space) for space in spaces)


def call(kernel, outs, scratch=(), inputs=0, in_specs=None, out_specs=None, limit=40, cost=None):
    vmem = pltpu.VMEM
    return pl.pallas_call(
        kernel,
        out_shape=outs,
        in_specs=in_specs or specs(*[vmem] * inputs),
        out_specs=out_specs or specs(*[vmem] * len(outs)),
        scratch_shapes=list(scratch),
        compiler_params=pltpu.CompilerParams(vmem_limit_bytes=limit * 2**20),
        cost_estimate=cost,
    )


def exchange(rows):
    count = rows.shape[0] // PEERS
    shaped = rows.reshape(PEERS, count, 1, 128)
    got = lax.all_to_all(shaped, GX_GY, split_axis=0, concat_axis=0, tiled=True)
    return got.reshape(PEERS * count, 128)


def swap(plane, first):
    pairs = [(i, i + 1) for i in range(first, N_GX - 1, 2)]
    return lax.ppermute(plane, GX, pairs + [(j, i) for i, j in pairs])


def other_core(x):
    return lax.ppermute(x, "gy", [(0, 1), (1, 0)])


def body(operator, basis_u, basis_c, right_side, new_rows):
    row = lax.broadcasted_iota(jnp.int32, (8, 128), 0)
    place = jnp.where(row == 0, lax.axis_index("gy"), lax.axis_index(GX) % 2).astype(jnp.int32)
    vmem, hbm = pltpu.VMEM, pltpu.HBM
    wire, info = call(
        pack_kernel,
        (shape(PEERS * WIRE, 128), shape(8, ROWS, dtype=jnp.int32)),
        [
            vmem((243, ROWS), F32),
            vmem((144, ROWS), F32),
            vmem((3, ROWS), F32),
            vmem((1, ROWS), jnp.int32),
            vmem((ROWS, 2 * MAIN), BF16),
            vmem((3, 64, ROWS), F32),
            vmem((56, 128), F32),
            vmem((PEERS * WIRE, 128), F32),
            pltpu.SemaphoreType.DMA((6,)),
            pltpu.SemaphoreType.DMA((CHUNKS,)),
        ],
        in_specs=specs(hbm, hbm, hbm, hbm),
        out_specs=specs(hbm, vmem),
        limit=56,
    )(operator, basis_c, right_side, new_rows.reshape(1, ROWS))
    got = exchange(wire)
    got = got.reshape(PEERS, WIRE, 128).transpose(1, 0, 2)
    mine = jnp.sum(got[49:], axis=1)
    plane = shape(32, 128)
    main, ext, one, inverse, start, beta = call(
        unpack_kernel,
        (shape(2 * 128 * CY, 128), shape(48, 128), plane, shape(K, 128), shape(K, 128), shape(8, 128)),
        [
            vmem((ROWS, SLOTS * PEERS), BF16),
            vmem((2, SLOTS * PEERS, 256), BF16),
            vmem((48, SLOTS * PEERS), F32),
            vmem((128, SLOTS * PEERS), BF16),
            vmem((56, 128), F32),
        ],
        inputs=4,
    )(place, got, mine, other_core(mine))
    [late] = call(
        late_kernel,
        (shape(128 * CY, 128),),
        [vmem((ROWS, SLOTS * PEERS), BF16), vmem((SLOTS * PEERS, 256), BF16)],
        inputs=1,
        cost=pl.CostEstimate(flops=2 * ROWS * SLOTS * PEERS * 256, bytes_accessed=5 * 10**6, transcendentals=0),
    )(got)
    pad = vmem((9 * 24, 128), F32)
    image_scratch = [pad, vmem(((K + 8) * CY, 128), F32)]
    image_outs = (shape(3 * CY, 128), shape(PEERS, 128))
    one = lax.dynamic_update_slice(one, other_core(one[24:32]), (24, 0))
    image_one, send, edge = call(
        functools.partial(image_kernel, 1), (*image_outs, shape(3 * K + 8, 128)), image_scratch, inputs=7
    )(place, main, late, ext, swap(one, 0), swap(one, 1), one)
    other = other_core(edge)
    sums = exchange(send)
    two, weights, h_one = call(next_kernel, (plane, shape(K, 128), shape(8, 128)), inputs=6)(
        sums, main, image_one, one, other, inverse
    )
    image_two, send = call(functools.partial(image_kernel, 2), image_outs, image_scratch, inputs=8)(
        place, main, late, ext, swap(two, 0), swap(two, 1), one, two
    )
    sums = exchange(send)
    wire, y = call(send_kernel, (shape(PEERS * 3, 128), shape(8, 128)), inputs=8)(
        sums, inverse, start, weights, h_one, beta, basis_u, info
    )
    got = exchange(wire)
    return call(
        last_kernel,
        (shape(3, ROWS), shape(3, ROWS)),
        [vmem((3, 48, SLOTS * PEERS), F32), vmem((3, 256, SLOTS * PEERS), BF16), pad],
        inputs=10,
    )(place, got, main, late, ext, y, one, two, image_one, image_two)


def solution(mesh):
    torus = Mesh(mesh.devices.reshape(4, 4, 4, mesh.shape["gy"]), ("gx_0", "gx_1", "gx_2", "gy"))
    placed = (P(None, GX_GY), P(None, GX_GY), P(None, GX_GY), P(None, GX_GY), P(GX_GY))
    return jax.shard_map(
        body,
        mesh=torus,
        in_specs=placed,
        out_specs=(P(None, GX_GY), P(None, GX_GY)),
        check_vma=False,
    )
```

```python
import functools

import jax
import jax.numpy as jnp
from jax import lax
from jax.experimental import pallas as pl
from jax.experimental.pallas import tpu as pltpu
from jax.sharding import Mesh
from jax.sharding import PartitionSpec as P

CY = 8
CZ = 128
K = 48
SLOTS = 16
PEERS = 128
ROWS = 1024
N_GX = 64
GX_GY = ("gx_0", "gx_1", "gx_2", "gy")
GX = ("gx_0", "gx_1", "gx_2")
F32 = jnp.float32
BF16 = jnp.bfloat16
HIGHEST = lax.Precision.HIGHEST
SIDE = K + 1
BANDS = 25
GRAM = 10
HALF = GRAM // 2
WIRE = 49 + HALF
CHUNKS = 8
NT = (((1,), (1,)), ((), ()))
TN = (((0,), (0,)), ((), ()))
MAIN = 3 * 128
EARLY = 2 * 128 - 3 * K


def split(x):
    high = x.astype(BF16)
    return high, (x - high.astype(F32)).astype(BF16)


def exact_dot(x, y, dims=(((1,), (0,)), ((), ()))):
    return lax.dot_general(x, y, dims, precision=HIGHEST, preferred_element_type=F32)


def chosen(mask):
    return jnp.where(mask, jnp.ones(mask.shape, BF16), jnp.zeros(mask.shape, BF16))


def half_sum(x):
    return x[:, :128] + x[:, 128:]


def squared(x):
    x = jnp.concatenate([x, jnp.zeros((64, 64), F32)], axis=1)
    return jnp.concatenate([x, jnp.zeros((64, 128), F32)], axis=0)


def folded(rows, start_ref):
    twice = rows + pltpu.roll(rows, SIDE, 1)
    sub = lax.broadcasted_iota(jnp.int32, (8, 128), 0)
    for tile in range(7):
        here = twice[tile * 8 : (tile + 1) * 8]
        total = jnp.zeros((8, 128), F32)
        for r in range(8):
            i = tile * 8 + r
            if i < SIDE:
                moved = pltpu.roll(here, (128 - i + BANDS * (i // GRAM)) % 128, 1)
                total = jnp.where(sub == r, moved, total)
        start_ref[tile * 8 : (tile + 1) * 8, :] = total
    lane = lax.broadcasted_iota(jnp.int32, (GRAM, 128), 1)
    return sum(
        jnp.where(lane // BANDS == g, start_ref[g * GRAM : (g + 1) * GRAM, :], 0.0) for g in range(5)
    )


def unfolded(bands, start_ref):
    sub = lax.broadcasted_iota(jnp.int32, (8, 128), 0)
    lane = lax.broadcasted_iota(jnp.int32, (GRAM, 128), 1)
    start_ref[48:56, :] = jnp.zeros((8, 128), F32)
    for g in range(5):
        start_ref[g * GRAM : (g + 1) * GRAM, :] = jnp.where(lane // BANDS == g, bands, 0.0)
    tiles = []
    for tile in range(7):
        here = start_ref[tile * 8 : (tile + 1) * 8, :]
        total = jnp.zeros((8, 128), F32)
        for r in range(8):
            i = tile * 8 + r
            if i < SIDE:
                moved = pltpu.roll(here, (128 + i - BANDS * (i // GRAM)) % 128, 1)
                total = jnp.where(sub == r, moved, total)
        tiles.append(total)
    half = jnp.concatenate(tiles + [jnp.zeros((72, 128), F32)], axis=0)
    row = lax.broadcasted_iota(jnp.int32, (128, 128), 0)
    lane = lax.broadcasted_iota(jnp.int32, (128, 128), 1)
    half = jnp.where(lane < SIDE, half + pltpu.roll(half, 128 - SIDE, 1), 0.0)
    return half + jnp.where(row == lane, 0.0, half.T)


def pieces(source, target, size):
    count = source.shape[0]
    parts = [pl.ds(i, min(size, count - i)) for i in range(0, count, size)]
    return [(source.at[part], target.at[part]) for part in parts]


def pack_kernel(
    op_hbm, c_hbm, b_hbm, rows_hbm, wire_hbm, info_hbm,
    op_ref, c_ref, b_ref, rows_ref, p_ref, a_ref, fold_ref, wire_ref, info_ref, in_sem, out_sem,
):
    copies = [
        pltpu.make_async_copy(source, target, in_sem.at[i])
        for i, (source, target) in enumerate(
            [(rows_hbm, rows_ref), (b_hbm, b_ref), *pieces(c_hbm, c_ref, 72), *pieces(op_hbm, op_ref, 128)]
        )
    ]
    for copy in copies:
        copy.start()
    copies[0].wait()
    new_rows = rows_ref[...]
    target = new_rows // ROWS
    local = new_rows % ROWS
    onehot = lax.broadcasted_iota(jnp.int32, (PEERS, ROWS), 0) == target
    onehot_f = jnp.where(onehot, 1.0, 0.0).astype(F32)
    onehot_b = onehot_f.astype(BF16)
    before = lax.broadcasted_iota(jnp.int32, (128, 128), 0) < lax.broadcasted_iota(jnp.int32, (128, 128), 1)
    before = jnp.where(before, 1.0, 0.0).astype(BF16)
    ones = jnp.ones((128, 128), BF16)
    seen = jnp.zeros((PEERS, 128), F32)
    ranks = []
    for block in range(ROWS // 128):
        part = onehot_b[:, block * 128 : (block + 1) * 128]
        count = jnp.dot(part, before, preferred_element_type=F32) + seen
        ranks.append(jnp.sum(onehot_f[:, block * 128 : (block + 1) * 128] * count, axis=0, keepdims=True))
        seen = seen + jnp.dot(part, ones, preferred_element_type=F32)
    rank = jnp.concatenate(ranks, axis=1)
    rank_at = jnp.where(onehot, rank, -1.0).astype(BF16)
    info_ref[0:1, :] = target
    info_ref[1:2, :] = rank.astype(jnp.int32)
    info_ref[2:3, :] = local
    info_ref[3:8, :] = jnp.zeros((5, ROWS), jnp.int32)
    sent = [pltpu.make_async_copy(info_ref, info_hbm, out_sem.at[CHUNKS])]
    sent[0].start()
    for copy in copies[1:]:
        copy.wait()

    def put(tile, x):
        p_ref[:, tile * 256 : tile * 256 + 128], p_ref[:, tile * 256 + 128 : (tile + 1) * 256] = split(x.T)

    put(0, c_ref[0:128, :])
    put(1, jnp.concatenate([c_ref[128:144, :], op_ref[0:112, :]], axis=0))
    put(2, op_ref[112:240, :])
    sums, low = jnp.zeros((192, 64), F32), jnp.zeros((64, 64), F32)
    for a in range(3):
        a_ref[a, 48:64, :] = jnp.zeros((16, ROWS), F32)
        a_ref[a, 0:48, :] = c_ref[a * K : (a + 1) * K, :]
        a_ref[a, 48:49, :] = b_ref[a : a + 1, :]
        one, two = split(a_ref[a])
        three = (a_ref[a] - one.astype(F32) - two.astype(F32)).astype(BF16)
        terms = jnp.concatenate([one, two, three], axis=0)
        sums = sums + lax.dot_general(terms, one, NT, preferred_element_type=F32)
        low = low + lax.dot_general(two, two, NT, preferred_element_type=F32)
    cross = squared(sums[64:128] + sums[128:192])
    gram = squared(sums[0:64] + low) + cross + cross.T
    bands = folded(gram[0:64], fold_ref)
    second = lax.broadcasted_iota(jnp.int32, (PEERS, 128), 0) % 2 == 1
    for i in range(HALF):
        wire_ref[pl.ds(49 + i, PEERS, stride=WIRE), :] = jnp.where(
            second, bands[HALF + i : HALF + i + 1, :], bands[i : i + 1, :]
        )
    at_rank = lax.broadcasted_iota(jnp.int32, (SLOTS, ROWS), 0).astype(F32) == rank
    rest = [op_ref[240 + i : 241 + i, :] for i in range(3)] + [b_ref[i : i + 1, :] for i in range(3)]
    rest = [jnp.where(at_rank, row, 0.0) for row in rest + [local.astype(F32)]]
    rest = jnp.concatenate(rest + [jnp.zeros((SLOTS, ROWS), F32)], axis=0)
    rest = jnp.concatenate(split(rest), axis=0)
    wire_ref[pl.ds(48, PEERS, stride=WIRE), :] = half_sum(
        lax.dot_general(onehot_b, rest, NT, preferred_element_type=F32)
    )
    count = PEERS // CHUNKS
    for chunk in range(CHUNKS):
        mine = rank_at[chunk * count : (chunk + 1) * count]
        choice = [chosen(mine == k) for k in range(SLOTS)]
        moved = jnp.dot(jnp.concatenate(choice, axis=0), p_ref[...], preferred_element_type=F32)
        for tile in range(3):
            both = half_sum(moved[:, tile * 256 : (tile + 1) * 256])
            for k in range(SLOTS):
                wire_ref[pl.ds(chunk * count * WIRE + tile * SLOTS + k, count, stride=WIRE), :] = both[
                    k * count : (k + 1) * count
                ]
        rows = pl.ds(chunk * count * WIRE, count * WIRE)
        sent.append(pltpu.make_async_copy(wire_ref.at[rows], wire_hbm.at[rows], out_sem.at[chunk]))
        sent[-1].start()
    for copy in sent:
        copy.wait()


def two_level(groups, left_ref, right_ref):
    eight = lax.broadcasted_iota(jnp.int32, (CY, 128), 0)
    deep = lax.broadcasted_iota(jnp.int32, (128, 128), 0).astype(F32).astype(BF16)
    count = groups[0][0].shape[0] // SLOTS
    for g, (values, labels) in enumerate(groups):
        labels = labels.astype(jnp.int32)
        y, z = labels // CZ, (labels % CZ).astype(F32)
        for k in range(SLOTS):
            cols = slice(k * 128, (k + 1) * 128)
            row = jnp.broadcast_to(z[k : k + 1], (128, 128)).astype(BF16)
            right_ref[g * 128 : (g + 1) * 128, cols] = chosen(deep == row)
            here = eight == y[k : k + 1]
            for c in range(count):
                row = (g * count + c) * CY
                value = values[c * SLOTS + k : c * SLOTS + k + 1]
                left_ref[row : row + CY, cols] = jnp.where(here, value, 0.0)
    rows = len(groups) * count * CY
    left = jnp.concatenate(split(left_ref[...]), axis=0)
    moved = lax.dot_general(left, right_ref[...], NT, preferred_element_type=F32)
    moved = moved[0:rows] + moved[rows:]
    size = count * CY
    return [moved[g * size : (g + 1) * size, g * 128 : (g + 1) * 128] for g in range(len(groups))]


def minus_combined(start, main_ref, weights):
    result = []
    for a in range(3):
        total = start[a]
        for m in range(K):
            row = (a * K + m) * CY
            total = total - main_ref[row : row + CY, :] * weights[m : m + 1, :]
        result.append(total)
    return result


def put_vector(vector, lines, v_ref):
    v_ref[24:32, :] = jnp.zeros((8, 128), F32)
    for a in range(3):
        v_ref[a * CY : (a + 1) * CY, :] = vector[a]
        v_ref[24 + a : 25 + a, :] = lines[a]


def swept(work, begin, count):
    row_id = lax.broadcasted_iota(jnp.int32, (K, 128), 0)
    columns = [jnp.broadcast_to(work[:, j : j + 1], (K, 128)) for j in range(begin, begin + count)]
    for s in range(count):
        j = begin + s
        column = columns[s]
        inverse = 1.0 / column[j : j + 1, :]
        here = row_id == j

        def step(x):
            pivot = x[j : j + 1, :] * inverse
            return jnp.where(here, pivot, x - column * pivot)

        work = step(work)
        columns = columns[: s + 1] + [step(c) for c in columns[s + 1 :]]
    return work


def put_table(labels, t_ref):
    deep = lax.broadcasted_iota(jnp.int32, (CZ, 128), 0).astype(F32).astype(BF16)
    whole = labels.astype(jnp.int32)
    label_y, label_z = (whole // CZ).astype(F32), (whole % CZ).astype(F32)
    for k in range(SLOTS):
        here = chosen(deep == jnp.broadcast_to(label_z[k : k + 1], (CZ, 128)).astype(BF16))
        row = jnp.broadcast_to(label_y[k : k + 1], (CZ, 128)).astype(BF16)
        for y in range(CY):
            t_ref[y * CZ : (y + 1) * CZ, k * 128 : (k + 1) * 128] = jnp.where(
                row == y, here, jnp.zeros((CZ, 128), BF16)
            )


def put_tile(wire_ref, tile, t_ref, r_ref, out_ref, first):
    for k in range(SLOTS):
        high, low = split(wire_ref[tile * SLOTS + k])
        r_ref[k * 128 : (k + 1) * 128, 0:128] = high
        r_ref[k * 128 : (k + 1) * 128, 128:256] = low
    moved = half_sum(jnp.dot(t_ref[...], r_ref[...], preferred_element_type=F32))
    for y in range(CY):
        out_ref[pl.ds(first * CY + y, 128, stride=CY), :] = moved[y * CZ : (y + 1) * CZ].T


def late_kernel(wire_ref, late_ref, t_ref, r_ref):
    put_table(wire_ref[48].T[6 * SLOTS : 7 * SLOTS], t_ref)
    put_tile(wire_ref, 2, t_ref, r_ref, late_ref, 0)


def unpack_kernel(
    place_ref, wire_ref, mine_ref, other_ref, main_ref, ext_ref, v_ref, inv_ref, start_ref, beta_ref,
    t_ref, r_ref, left_ref, right_ref, fold_ref,
):
    lower = place_ref[0:1, :] == 0
    mine, other = mine_ref[0:HALF, :], other_ref[0:HALF, :]
    bands = jnp.concatenate([jnp.where(lower, mine, other), jnp.where(lower, other, mine)], axis=0)
    gram = unfolded(bands, fold_ref)
    load_sq = jnp.broadcast_to(gram[48:49, 48:49], (1, 128))
    row_id = lax.broadcasted_iota(jnp.int32, (K, 128), 0)
    lane = lax.broadcasted_iota(jnp.int32, (K, 128), 1)
    raw = jnp.broadcast_to(gram[0:K, K : K + 1], (K, 128))
    work = jnp.where(lane < K + 1, gram[0:K], jnp.where(lane - 64 == row_id, 1.0, 0.0))
    for begin in range(0, K, 4):
        work = swept(work, begin, 4)
    rest = wire_ref[48].T
    labels = rest[6 * SLOTS : 7 * SLOTS]
    put_table(labels, t_ref)
    for tile in range(2):
        put_tile(wire_ref, tile, t_ref, r_ref.at[tile], main_ref, tile * 128)
    [ext] = two_level([(rest[0 : 6 * SLOTS], labels)], left_ref, right_ref)
    ext_ref[...] = ext

    inverse = jnp.where(lane < K, pltpu.roll(work, 64, 1), 0.0)
    weights = jnp.broadcast_to(work[:, K : K + 1], (K, 128))
    inv_ref[...] = inverse
    start_ref[...] = weights
    beta = jnp.sqrt(load_sq - jnp.sum(raw * weights, axis=0, keepdims=True))
    beta_ref[...] = jnp.broadcast_to(beta, (8, 128))
    load = [ext[24 + a * CY : 24 + (a + 1) * CY, :] for a in range(3)]
    vector = [v / beta for v in minus_combined(load, main_ref, weights)]
    put_vector(vector, [jnp.where(lower, v[CY - 1 : CY], v[0:1]) for v in vector], v_ref)


def put_plane(pad_ref, dx, plane, line, side):
    for a in range(3):
        base = (dx * 3 + a) * 24
        edge = line[a : a + 1, :]
        pad_ref[base + 7 : base + 8, :] = jnp.where(side == 1, edge, 0.0)
        pad_ref[base + 8 : base + 16, :] = plane[a * CY : (a + 1) * CY, :]
        pad_ref[base + 16 : base + 17, :] = jnp.where(side == 0, edge, 0.0)


def stencil(main_ref, late_ref, ext_ref, pad_ref):
    lane = lax.broadcasted_iota(jnp.int32, (CY, 128), 1)
    total = [jnp.zeros((CY, 128), F32) for _ in range(3)]
    for dx in range(3):
        for dy in range(3):
            for b in range(3):
                start = (dx * 3 + b) * 24 + 7 + dy
                here = pad_ref[start : start + CY, :]
                left = jnp.where(lane == 0, 0.0, pltpu.roll(here, 1, 1))
                right = jnp.where(lane == 127, 0.0, pltpu.roll(here, 127, 1))
                for dz, moved in enumerate((left, here, right)):
                    for a in range(3):
                        q = ((dx * 9 + dy * 3 + dz) * 3 + a) * 3 + b
                        if q < EARLY:
                            source, row = main_ref, (3 * K + q) * CY
                        elif q < 240:
                            source, row = late_ref, (q - EARLY) * CY
                        else:
                            source, row = ext_ref, (q - 240) * CY
                        total[a] = total[a] + source[row : row + CY, :] * moved
    return total


def image_kernel(count, place_ref, main_ref, late_ref, ext_ref, first_ref, second_ref, *refs):
    vectors, (image_ref, send_ref, *edges, pad_ref, part_ref) = refs[:count], refs[count:]
    side = place_ref[0:1, :]
    even = place_ref[1:2, :] == 0
    first, second = first_ref[...], second_ref[...]
    up, down = jnp.where(even, second, first), jnp.where(even, first, second)
    put_plane(pad_ref, 0, up[0:24], up[24:32], side)
    put_plane(pad_ref, 1, vectors[-1][0:24, :], vectors[-1][24:32, :], side)
    put_plane(pad_ref, 2, down[0:24], down[24:32], side)
    image = stencil(main_ref, late_ref, ext_ref, pad_ref)
    for a in range(3):
        image_ref[a * CY : (a + 1) * CY, :] = image[a]
    for edge_ref in edges:
        last = main_ref[pl.ds(CY - 1, 3 * K, stride=CY), :]
        edge_ref[0 : 3 * K, :] = jnp.where(side == 0, last, main_ref[pl.ds(0, 3 * K, stride=CY), :])
        edge_ref[3 * K :, :] = jnp.zeros((8, 128), F32)
        for a in range(3):
            row = 3 * K + a
            edge_ref[row : row + 1, :] = jnp.where(side == 0, image[a][CY - 1 : CY], image[a][0:1])
    for m in range(K):
        rows = [(a * K + m) * CY for a in range(3)]
        part_ref[m * CY : (m + 1) * CY, :] = sum(
            main_ref[row : row + CY, :] * image[a] for a, row in enumerate(rows)
        )
    others = [image] + [[ref[a * CY : (a + 1) * CY, :] for a in range(3)] for ref in vectors]
    for i in range(8):
        m = K + i
        if i < len(others):
            part_ref[m * CY : (m + 1) * CY, :] = sum(o * w for o, w in zip(others[i], image))
        else:
            part_ref[m * CY : (m + 1) * CY, :] = jnp.zeros((CY, 128), F32)
    part = sum(part_ref[pl.ds(y, K + 8, stride=CY), :] for y in range(CY))
    part = jnp.concatenate([part, jnp.zeros((128 - K - 8, 128), F32)], axis=0)
    send_ref[...] = exact_dot(jnp.ones((PEERS, 128), F32), part, NT)


def totals(got_ref):
    return exact_dot(got_ref[...], jnp.ones((PEERS, 128), F32), TN)


def next_kernel(got_ref, main_ref, image_ref, one_ref, other_ref, inv_ref, v_ref, weights_ref, h_ref):
    sums = totals(got_ref)
    weights = exact_dot(inv_ref[...], sums)
    h11 = sums[K + 1 : K + 2, :]
    along = jnp.sum(sums[0:K] * weights, axis=0, keepdims=True)
    h21 = jnp.sqrt(sums[K : K + 1, :] - along - h11 * h11)
    begin = [
        image_ref[a * CY : (a + 1) * CY, :] - h11 * one_ref[a * CY : (a + 1) * CY, :] for a in range(3)
    ]
    vector = [v / h21 for v in minus_combined(begin, main_ref, weights)]
    lines = []
    for a in range(3):
        along_line = jnp.sum(other_ref[a * K : (a + 1) * K, :] * weights, axis=0, keepdims=True)
        line = other_ref[3 * K + a : 3 * K + a + 1, :] - along_line - h11 * one_ref[24 + a : 25 + a, :]
        lines.append(line / h21)
    put_vector(vector, lines, v_ref)
    weights_ref[...] = weights
    h_ref[...] = jnp.zeros((8, 128), F32)
    h_ref[0:1, :] = h11
    h_ref[1:2, :] = h21


def send_kernel(got_ref, inv_ref, start_ref, first_ref, h_ref, beta_ref, u_ref, info_ref, wire_ref, y_ref):
    sums = totals(got_ref)
    weights = exact_dot(inv_ref[...], sums)
    h11, h21 = h_ref[0:1, :], h_ref[1:2, :]
    h12, h22 = sums[K + 1 : K + 2, :], sums[K + 2 : K + 3, :]
    along = jnp.sum(sums[0:K] * weights, axis=0, keepdims=True)
    h32 = jnp.sqrt(sums[K : K + 1, :] - along - h12 * h12 - h22 * h22)
    beta = beta_ref[0:1, :]
    m11 = h11 * h11 + h21 * h21
    m12 = h11 * h12 + h21 * h22
    m22 = h12 * h12 + h22 * h22 + h32 * h32
    g_one = beta * h11
    g_two = beta * h12
    determ = m11 * m22 - m12 * m12
    y_one = (m22 * g_one - m12 * g_two) / determ
    y_two = (m11 * g_two - m12 * g_one) / determ
    y_ref[...] = jnp.zeros((8, 128), F32)
    y_ref[0:1, :] = y_one
    y_ref[1:2, :] = y_two
    weights = start_ref[...] - y_one * first_ref[...] - y_two * weights
    wide = jnp.concatenate([weights] * (ROWS // 128), axis=1)
    target, rank, local = (info_ref[i : i + 1, :] for i in range(3))
    at_rank = lax.broadcasted_iota(jnp.int32, (SLOTS, ROWS), 0) == rank
    rows = [jnp.sum(u_ref[a * K : (a + 1) * K, :] * wide, axis=0, keepdims=True) for a in range(3)]
    rows = jnp.concatenate([jnp.where(at_rank, r, 0.0) for r in rows + [local.astype(F32)]], axis=0)
    rows = jnp.concatenate(split(rows), axis=0)
    onehot = lax.broadcasted_iota(jnp.int32, (PEERS, ROWS), 0) == target
    onehot = jnp.where(onehot, 1.0, 0.0).astype(BF16)
    mine = lax.dot_general(onehot, rows, NT, preferred_element_type=F32)
    mine = mine + pltpu.roll(mine, 64, 1)
    peer = lax.broadcasted_iota(jnp.int32, (PEERS, 128), 0)
    lane = lax.broadcasted_iota(jnp.int32, (PEERS, 128), 1)
    other = jnp.where(peer % 2 == 0, pltpu.roll(mine, PEERS - 1, 0), pltpu.roll(mine, 1, 0))
    pair = jnp.where(lane < 64, mine, other)
    wire_ref[pl.ds(0, PEERS, stride=3), :] = jnp.where(peer < 2, 0.0, pltpu.roll(pair, 2, 0))
    wire_ref[pl.ds(1, PEERS, stride=3), :] = pair
    wire_ref[pl.ds(2, PEERS, stride=3), :] = jnp.where(peer >= PEERS - 2, 0.0, pltpu.roll(pair, PEERS - 2, 0))


def last_kernel(
    place_ref, got_ref, main_ref, late_ref, ext_ref, y_ref, one_ref, two_ref, im_one_ref, im_two_ref,
    sol_ref, res_ref, left_ref, right_ref, pad_ref,
):
    side = place_ref[0:1, :]
    for dx in range(3):
        got = got_ref[pl.ds(dx, PEERS, stride=3), :].T
        own, other = two_level(
            [(got[base : base + 48], got[base + 48 : base + 64]) for base in (0, 64)],
            left_ref.at[dx],
            right_ref.at[dx],
        )
        lines = [
            jnp.where(side == 0, other[a * CY : a * CY + 1, :], other[a * CY + 7 : a * CY + 8, :]) for a in range(3)
        ]
        put_plane(pad_ref, dx, own, jnp.concatenate(lines, axis=0), side)
        if dx == 1:
            term = own
    image = stencil(main_ref, late_ref, ext_ref, pad_ref)
    y_one, y_two = y_ref[0:1, :], y_ref[1:2, :]
    solution = term + y_one * one_ref[0:24, :] + y_two * two_ref[0:24, :]
    for a in range(3):
        rows = slice(a * CY, (a + 1) * CY)
        residual = ext_ref[24 + a * CY : 24 + (a + 1) * CY, :] - image[a]
        residual = residual - y_one * im_one_ref[rows, :] - y_two * im_two_ref[rows, :]
        for y in range(CY):
            cols = slice(y * CZ, (y + 1) * CZ)
            sol_ref[a : a + 1, cols] = solution[a * CY + y : a * CY + y + 1, :]
            res_ref[a : a + 1, cols] = residual[y : y + 1, :]


def shape(*dims, dtype=F32):
    return jax.ShapeDtypeStruct(dims, dtype)


def specs(*spaces):
    return tuple(pl.BlockSpec(memory_space=space) for space in spaces)


def call(kernel, outs, scratch=(), inputs=0, in_specs=None, out_specs=None, limit=40, cost=None):
    vmem = pltpu.VMEM
    return pl.pallas_call(
        kernel,
        out_shape=outs,
        in_specs=in_specs or specs(*[vmem] * inputs),
        out_specs=out_specs or specs(*[vmem] * len(outs)),
        scratch_shapes=list(scratch),
        compiler_params=pltpu.CompilerParams(vmem_limit_bytes=limit * 2**20),
        cost_estimate=cost,
    )


def exchange(rows):
    count = rows.shape[0] // PEERS
    shaped = rows.reshape(PEERS, count, 1, 128)
    got = lax.all_to_all(shaped, GX_GY, split_axis=0, concat_axis=0, tiled=True)
    return got.reshape(PEERS * count, 128)


def swap(plane, first):
    pairs = [(i, i + 1) for i in range(first, N_GX - 1, 2)]
    return lax.ppermute(plane, GX, pairs + [(j, i) for i, j in pairs])


def other_core(x):
    return lax.ppermute(x, "gy", [(0, 1), (1, 0)])


def body(operator, basis_u, basis_c, right_side, new_rows):
    row = lax.broadcasted_iota(jnp.int32, (8, 128), 0)
    place = jnp.where(row == 0, lax.axis_index("gy"), lax.axis_index(GX) % 2).astype(jnp.int32)
    vmem, hbm = pltpu.VMEM, pltpu.HBM
    wire, info = call(
        pack_kernel,
        (shape(PEERS * WIRE, 128), shape(8, ROWS, dtype=jnp.int32)),
        [
            vmem((243, ROWS), F32),
            vmem((144, ROWS), F32),
            vmem((3, ROWS), F32),
            vmem((1, ROWS), jnp.int32),
            vmem((ROWS, 2 * MAIN), BF16),
            vmem((3, 64, ROWS), F32),
            vmem((56, 128), F32),
            vmem((PEERS * WIRE, 128), F32),
            vmem((8, ROWS), jnp.int32),
            pltpu.SemaphoreType.DMA((6,)),
            pltpu.SemaphoreType.DMA((CHUNKS + 1,)),
        ],
        in_specs=specs(hbm, hbm, hbm, hbm),
        out_specs=specs(hbm, hbm),
        limit=56,
    )(operator, basis_c, right_side, new_rows.reshape(1, ROWS))
    got = exchange(wire)
    got = got.reshape(PEERS, WIRE, 128).transpose(1, 0, 2)
    mine = jnp.sum(got[49:], axis=1)
    plane = shape(32, 128)
    main, ext, one, inverse, start, beta = call(
        unpack_kernel,
        (shape(2 * 128 * CY, 128), shape(48, 128), plane, shape(K, 128), shape(K, 128), shape(8, 128)),
        [
            vmem((ROWS, SLOTS * PEERS), BF16),
            vmem((2, SLOTS * PEERS, 256), BF16),
            vmem((48, SLOTS * PEERS), F32),
            vmem((128, SLOTS * PEERS), BF16),
            vmem((56, 128), F32),
        ],
        inputs=4,
    )(place, got, mine, other_core(mine))
    [late] = call(
        late_kernel,
        (shape(128 * CY, 128),),
        [vmem((ROWS, SLOTS * PEERS), BF16), vmem((SLOTS * PEERS, 256), BF16)],
        inputs=1,
        cost=pl.CostEstimate(flops=2 * ROWS * SLOTS * PEERS * 256, bytes_accessed=5 * 10**6, transcendentals=0),
    )(got)
    pad = vmem((9 * 24, 128), F32)
    image_scratch = [pad, vmem(((K + 8) * CY, 128), F32)]
    image_outs = (shape(3 * CY, 128), shape(PEERS, 128))
    one = lax.dynamic_update_slice(one, other_core(one[24:32]), (24, 0))
    image_one, send, edge = call(
        functools.partial(image_kernel, 1), (*image_outs, shape(3 * K + 8, 128)), image_scratch, inputs=7
    )(place, main, late, ext, swap(one, 0), swap(one, 1), one)
    other = other_core(edge)
    sums = exchange(send)
    two, weights, h_one = call(next_kernel, (plane, shape(K, 128), shape(8, 128)), inputs=6)(
        sums, main, image_one, one, other, inverse
    )
    image_two, send = call(functools.partial(image_kernel, 2), image_outs, image_scratch, inputs=8)(
        place, main, late, ext, swap(two, 0), swap(two, 1), one, two
    )
    sums = exchange(send)
    wire, y = call(send_kernel, (shape(PEERS * 3, 128), shape(8, 128)), inputs=8)(
        sums, inverse, start, weights, h_one, beta, basis_u, info
    )
    got = exchange(wire)
    return call(
        last_kernel,
        (shape(3, ROWS), shape(3, ROWS)),
        [vmem((3, 48, SLOTS * PEERS), F32), vmem((3, 256, SLOTS * PEERS), BF16), pad],
        inputs=10,
    )(place, got, main, late, ext, y, one, two, image_one, image_two)


def solution(mesh):
    torus = Mesh(mesh.devices.reshape(4, 4, 4, mesh.shape["gy"]), ("gx_0", "gx_1", "gx_2", "gy"))
    placed = (P(None, GX_GY), P(None, GX_GY), P(None, GX_GY), P(None, GX_GY), P(GX_GY))
    return jax.shard_map(
        body,
        mesh=torus,
        in_specs=placed,
        out_specs=(P(None, GX_GY), P(None, GX_GY)),
        check_vma=False,
    )
```

```python
import functools

import jax
import jax.numpy as jnp
from jax import lax
from jax.experimental import pallas as pl
from jax.experimental.pallas import tpu as pltpu
from jax.sharding import Mesh
from jax.sharding import PartitionSpec as P

CY = 8
CZ = 128
K = 48
SLOTS = 16
PEERS = 128
ROWS = 1024
N_GX = 64
GX_GY = ("gx_0", "gx_1", "gx_2", "gy")
GX = ("gx_0", "gx_1", "gx_2")
F32 = jnp.float32
BF16 = jnp.bfloat16
HIGHEST = lax.Precision.HIGHEST
SIDE = K + 1
BANDS = 25
GRAM = 10
HALF = GRAM // 2
WIRE = 49 + HALF
CHUNKS = 8
NT = (((1,), (1,)), ((), ()))
TN = (((0,), (0,)), ((), ()))
MAIN = 3 * 128
EARLY = 2 * 128 - 3 * K


def split(x):
    high = x.astype(BF16)
    return high, (x - high.astype(F32)).astype(BF16)


def exact_dot(x, y, dims=(((1,), (0,)), ((), ()))):
    return lax.dot_general(x, y, dims, precision=HIGHEST, preferred_element_type=F32)


def chosen(mask):
    return jnp.where(mask, jnp.ones(mask.shape, BF16), jnp.zeros(mask.shape, BF16))


def half_sum(x):
    return x[:, :128] + x[:, 128:]


def squared(x):
    x = jnp.concatenate([x, jnp.zeros((64, 64), F32)], axis=1)
    return jnp.concatenate([x, jnp.zeros((64, 128), F32)], axis=0)


def folded(rows, start_ref):
    twice = rows + pltpu.roll(rows, SIDE, 1)
    sub = lax.broadcasted_iota(jnp.int32, (8, 128), 0)
    for tile in range(7):
        here = twice[tile * 8 : (tile + 1) * 8]
        total = jnp.zeros((8, 128), F32)
        for r in range(8):
            i = tile * 8 + r
            if i < SIDE:
                moved = pltpu.roll(here, (128 - i + BANDS * (i // GRAM)) % 128, 1)
                total = jnp.where(sub == r, moved, total)
        start_ref[tile * 8 : (tile + 1) * 8, :] = total
    lane = lax.broadcasted_iota(jnp.int32, (GRAM, 128), 1)
    return sum(
        jnp.where(lane // BANDS == g, start_ref[g * GRAM : (g + 1) * GRAM, :], 0.0) for g in range(5)
    )


def unfolded(bands, start_ref):
    sub = lax.broadcasted_iota(jnp.int32, (8, 128), 0)
    lane = lax.broadcasted_iota(jnp.int32, (GRAM, 128), 1)
    start_ref[48:56, :] = jnp.zeros((8, 128), F32)
    for g in range(5):
        start_ref[g * GRAM : (g + 1) * GRAM, :] = jnp.where(lane // BANDS == g, bands, 0.0)
    tiles = []
    for tile in range(7):
        here = start_ref[tile * 8 : (tile + 1) * 8, :]
        total = jnp.zeros((8, 128), F32)
        for r in range(8):
            i = tile * 8 + r
            if i < SIDE:
                moved = pltpu.roll(here, (128 + i - BANDS * (i // GRAM)) % 128, 1)
                total = jnp.where(sub == r, moved, total)
        tiles.append(total)
    half = jnp.concatenate(tiles + [jnp.zeros((72, 128), F32)], axis=0)
    row = lax.broadcasted_iota(jnp.int32, (128, 128), 0)
    lane = lax.broadcasted_iota(jnp.int32, (128, 128), 1)
    half = jnp.where(lane < SIDE, half + pltpu.roll(half, 128 - SIDE, 1), 0.0)
    return half + jnp.where(row == lane, 0.0, half.T)


def pieces(source, target, size):
    count = source.shape[0]
    parts = [pl.ds(i, min(size, count - i)) for i in range(0, count, size)]
    return [(source.at[part], target.at[part]) for part in parts]


def pack_kernel(
    op_hbm, c_hbm, b_hbm, rows_hbm, wire_hbm, info_hbm,
    op_ref, c_ref, b_ref, rows_ref, p_ref, a_ref, fold_ref, wire_ref, info_ref, in_sem, out_sem,
):
    copies = [
        pltpu.make_async_copy(source, target, in_sem.at[i])
        for i, (source, target) in enumerate(
            [(rows_hbm, rows_ref), (b_hbm, b_ref), *pieces(c_hbm, c_ref, 72), *pieces(op_hbm, op_ref, 128)]
        )
    ]
    for copy in copies:
        copy.start()
    copies[0].wait()
    new_rows = rows_ref[...]
    target = new_rows // ROWS
    local = new_rows % ROWS
    onehot = lax.broadcasted_iota(jnp.int32, (PEERS, ROWS), 0) == target
    onehot_f = jnp.where(onehot, 1.0, 0.0).astype(F32)
    onehot_b = onehot_f.astype(BF16)
    before = lax.broadcasted_iota(jnp.int32, (128, 128), 0) < lax.broadcasted_iota(jnp.int32, (128, 128), 1)
    before = jnp.where(before, 1.0, 0.0).astype(BF16)
    ones = jnp.ones((128, 128), BF16)
    seen = jnp.zeros((PEERS, 128), F32)
    ranks = []
    for block in range(ROWS // 128):
        part = onehot_b[:, block * 128 : (block + 1) * 128]
        count = jnp.dot(part, before, preferred_element_type=F32) + seen
        ranks.append(jnp.sum(onehot_f[:, block * 128 : (block + 1) * 128] * count, axis=0, keepdims=True))
        seen = seen + jnp.dot(part, ones, preferred_element_type=F32)
    rank = jnp.concatenate(ranks, axis=1)
    rank_at = jnp.where(onehot, rank, -1.0).astype(BF16)
    info_ref[0:1, :] = target
    info_ref[1:2, :] = rank.astype(jnp.int32)
    info_ref[2:3, :] = local
    info_ref[3:8, :] = jnp.zeros((5, ROWS), jnp.int32)
    sent = [pltpu.make_async_copy(info_ref, info_hbm, out_sem.at[CHUNKS])]
    sent[0].start()
    for copy in copies[1:]:
        copy.wait()

    def put(tile, x):
        p_ref[:, tile * 256 : tile * 256 + 128], p_ref[:, tile * 256 + 128 : (tile + 1) * 256] = split(x.T)

    put(0, c_ref[0:128, :])
    put(1, jnp.concatenate([c_ref[128:144, :], op_ref[0:112, :]], axis=0))
    put(2, op_ref[112:240, :])
    sums, low = jnp.zeros((192, 64), F32), jnp.zeros((64, 64), F32)
    for a in range(3):
        a_ref[a, 48:64, :] = jnp.zeros((16, ROWS), F32)
        a_ref[a, 0:48, :] = c_ref[a * K : (a + 1) * K, :]
        a_ref[a, 48:49, :] = b_ref[a : a + 1, :]
        one, two = split(a_ref[a])
        three = (a_ref[a] - one.astype(F32) - two.astype(F32)).astype(BF16)
        terms = jnp.concatenate([one, two, three], axis=0)
        sums = sums + lax.dot_general(terms, one, NT, preferred_element_type=F32)
        low = low + lax.dot_general(two, two, NT, preferred_element_type=F32)
    cross = squared(sums[64:128] + sums[128:192])
    gram = squared(sums[0:64] + low) + cross + cross.T
    bands = folded(gram[0:64], fold_ref)
    second = lax.broadcasted_iota(jnp.int32, (PEERS, 128), 0) % 2 == 1
    for i in range(HALF):
        wire_ref[pl.ds(49 + i, PEERS, stride=WIRE), :] = jnp.where(
            second, bands[HALF + i : HALF + i + 1, :], bands[i : i + 1, :]
        )
    at_rank = lax.broadcasted_iota(jnp.int32, (SLOTS, ROWS), 0).astype(F32) == rank
    rest = [op_ref[240 + i : 241 + i, :] for i in range(3)] + [b_ref[i : i + 1, :] for i in range(3)]
    rest = [jnp.where(at_rank, row, 0.0) for row in rest + [local.astype(F32)]]
    rest = jnp.concatenate(rest + [jnp.zeros((SLOTS, ROWS), F32)], axis=0)
    rest = jnp.concatenate(split(rest), axis=0)
    wire_ref[pl.ds(48, PEERS, stride=WIRE), :] = half_sum(
        lax.dot_general(onehot_b, rest, NT, preferred_element_type=F32)
    )
    count = PEERS // CHUNKS
    for chunk in range(CHUNKS):
        mine = rank_at[chunk * count : (chunk + 1) * count]
        choice = [chosen(mine == k) for k in range(SLOTS)]
        moved = jnp.dot(jnp.concatenate(choice, axis=0), p_ref[...], preferred_element_type=F32)
        for tile in range(3):
            both = half_sum(moved[:, tile * 256 : (tile + 1) * 256])
            for k in range(SLOTS):
                wire_ref[pl.ds(chunk * count * WIRE + tile * SLOTS + k, count, stride=WIRE), :] = both[
                    k * count : (k + 1) * count
                ]
        rows = pl.ds(chunk * count * WIRE, count * WIRE)
        sent.append(pltpu.make_async_copy(wire_ref.at[rows], wire_hbm.at[rows], out_sem.at[chunk]))
        sent[-1].start()
    for copy in sent:
        copy.wait()


def two_level(groups, left_ref, right_ref):
    eight = lax.broadcasted_iota(jnp.int32, (CY, 128), 0)
    deep = lax.broadcasted_iota(jnp.int32, (128, 128), 0).astype(F32).astype(BF16)
    count = groups[0][0].shape[0] // SLOTS
    for g, (values, labels) in enumerate(groups):
        labels = labels.astype(jnp.int32)
        y, z = labels // CZ, (labels % CZ).astype(F32)
        for k in range(SLOTS):
            cols = slice(k * 128, (k + 1) * 128)
            row = jnp.broadcast_to(z[k : k + 1], (128, 128)).astype(BF16)
            right_ref[g * 128 : (g + 1) * 128, cols] = chosen(deep == row)
            here = eight == y[k : k + 1]
            for c in range(count):
                row = (g * count + c) * CY
                value = values[c * SLOTS + k : c * SLOTS + k + 1]
                left_ref[row : row + CY, cols] = jnp.where(here, value, 0.0)
    rows = len(groups) * count * CY
    left = jnp.concatenate(split(left_ref[...]), axis=0)
    moved = lax.dot_general(left, right_ref[...], NT, preferred_element_type=F32)
    moved = moved[0:rows] + moved[rows:]
    size = count * CY
    return [moved[g * size : (g + 1) * size, g * 128 : (g + 1) * 128] for g in range(len(groups))]


def minus_combined(start, main_ref, weights):
    result = []
    for a in range(3):
        total = start[a]
        for m in range(K):
            row = (a * K + m) * CY
            total = total - main_ref[row : row + CY, :] * weights[m : m + 1, :]
        result.append(total)
    return result


def put_vector(vector, lines, v_ref):
    v_ref[24:32, :] = jnp.zeros((8, 128), F32)
    for a in range(3):
        v_ref[a * CY : (a + 1) * CY, :] = vector[a]
        v_ref[24 + a : 25 + a, :] = lines[a]


def swept(work, begin, count):
    row_id = lax.broadcasted_iota(jnp.int32, (K, 128), 0)
    columns = [jnp.broadcast_to(work[:, j : j + 1], (K, 128)) for j in range(begin, begin + count)]
    for s in range(count):
        j = begin + s
        column = columns[s]
        inverse = 1.0 / column[j : j + 1, :]
        here = row_id == j

        def step(x):
            pivot = x[j : j + 1, :] * inverse
            return jnp.where(here, pivot, x - column * pivot)

        work = step(work)
        columns = columns[: s + 1] + [step(c) for c in columns[s + 1 :]]
    return work


def put_table(labels, t_ref):
    deep = lax.broadcasted_iota(jnp.int32, (CZ, 128), 0).astype(F32).astype(BF16)
    whole = labels.astype(jnp.int32)
    label_y, label_z = (whole // CZ).astype(F32), (whole % CZ).astype(F32)
    for k in range(SLOTS):
        here = chosen(deep == jnp.broadcast_to(label_z[k : k + 1], (CZ, 128)).astype(BF16))
        row = jnp.broadcast_to(label_y[k : k + 1], (CZ, 128)).astype(BF16)
        for y in range(CY):
            t_ref[y * CZ : (y + 1) * CZ, k * 128 : (k + 1) * 128] = jnp.where(
                row == y, here, jnp.zeros((CZ, 128), BF16)
            )


def put_tile(wire_ref, tile, t_ref, r_ref, out_ref, first):
    for k in range(SLOTS):
        high, low = split(wire_ref[tile * SLOTS + k])
        r_ref[k * 128 : (k + 1) * 128, 0:128] = high
        r_ref[k * 128 : (k + 1) * 128, 128:256] = low
    moved = half_sum(jnp.dot(t_ref[...], r_ref[...], preferred_element_type=F32))
    for y in range(CY):
        out_ref[pl.ds(first * CY + y, 128, stride=CY), :] = moved[y * CZ : (y + 1) * CZ].T


def late_kernel(wire_ref, late_ref, t_ref, r_ref):
    put_table(wire_ref[48].T[6 * SLOTS : 7 * SLOTS], t_ref)
    put_tile(wire_ref, 2, t_ref, r_ref, late_ref, 0)


def unpack_kernel(
    place_ref, wire_ref, mine_ref, other_ref, main_ref, ext_ref, v_ref, inv_ref, start_ref, beta_ref,
    t_ref, r_ref, left_ref, right_ref, fold_ref,
):
    lower = place_ref[0:1, :] == 0
    mine, other = mine_ref[0:HALF, :], other_ref[0:HALF, :]
    bands = jnp.concatenate([jnp.where(lower, mine, other), jnp.where(lower, other, mine)], axis=0)
    gram = unfolded(bands, fold_ref)
    load_sq = jnp.broadcast_to(gram[48:49, 48:49], (1, 128))
    row_id = lax.broadcasted_iota(jnp.int32, (K, 128), 0)
    lane = lax.broadcasted_iota(jnp.int32, (K, 128), 1)
    raw = jnp.broadcast_to(gram[0:K, K : K + 1], (K, 128))
    work = jnp.where(lane < K + 1, gram[0:K], jnp.where(lane - 64 == row_id, 1.0, 0.0))
    for begin in range(0, K, 4):
        work = swept(work, begin, 4)
    rest = wire_ref[48].T
    labels = rest[6 * SLOTS : 7 * SLOTS]
    put_table(labels, t_ref)
    for tile in range(2):
        put_tile(wire_ref, tile, t_ref, r_ref.at[tile], main_ref, tile * 128)
    [ext] = two_level([(rest[0 : 6 * SLOTS], labels)], left_ref, right_ref)
    ext_ref[...] = ext

    inverse = jnp.where(lane < K, pltpu.roll(work, 64, 1), 0.0)
    weights = jnp.broadcast_to(work[:, K : K + 1], (K, 128))
    inv_ref[...] = inverse
    start_ref[...] = weights
    beta = jnp.sqrt(load_sq - jnp.sum(raw * weights, axis=0, keepdims=True))
    beta_ref[...] = jnp.broadcast_to(beta, (8, 128))
    load = [ext[24 + a * CY : 24 + (a + 1) * CY, :] for a in range(3)]
    vector = [v / beta for v in minus_combined(load, main_ref, weights)]
    put_vector(vector, [jnp.where(lower, v[CY - 1 : CY], v[0:1]) for v in vector], v_ref)


def put_plane(pad_ref, dx, plane, line, side):
    for a in range(3):
        base = (dx * 3 + a) * 24
        edge = line[a : a + 1, :]
        pad_ref[base + 7 : base + 8, :] = jnp.where(side == 1, edge, 0.0)
        pad_ref[base + 8 : base + 16, :] = plane[a * CY : (a + 1) * CY, :]
        pad_ref[base + 16 : base + 17, :] = jnp.where(side == 0, edge, 0.0)


def stencil(main_ref, late_ref, ext_ref, pad_ref):
    lane = lax.broadcasted_iota(jnp.int32, (CY, 128), 1)
    total = [jnp.zeros((CY, 128), F32) for _ in range(3)]
    for dx in range(3):
        for dy in range(3):
            for b in range(3):
                start = (dx * 3 + b) * 24 + 7 + dy
                here = pad_ref[start : start + CY, :]
                left = jnp.where(lane == 0, 0.0, pltpu.roll(here, 1, 1))
                right = jnp.where(lane == 127, 0.0, pltpu.roll(here, 127, 1))
                for dz, moved in enumerate((left, here, right)):
                    for a in range(3):
                        q = ((dx * 9 + dy * 3 + dz) * 3 + a) * 3 + b
                        if q < EARLY:
                            source, row = main_ref, (3 * K + q) * CY
                        elif q < 240:
                            source, row = late_ref, (q - EARLY) * CY
                        else:
                            source, row = ext_ref, (q - 240) * CY
                        total[a] = total[a] + source[row : row + CY, :] * moved
    return total


def image_kernel(count, place_ref, main_ref, late_ref, ext_ref, first_ref, second_ref, *refs):
    vectors, (image_ref, send_ref, *edges, pad_ref, part_ref) = refs[:count], refs[count:]
    side = place_ref[0:1, :]
    even = place_ref[1:2, :] == 0
    first, second = first_ref[...], second_ref[...]
    up, down = jnp.where(even, second, first), jnp.where(even, first, second)
    put_plane(pad_ref, 0, up[0:24], up[24:32], side)
    put_plane(pad_ref, 1, vectors[-1][0:24, :], vectors[-1][24:32, :], side)
    put_plane(pad_ref, 2, down[0:24], down[24:32], side)
    image = stencil(main_ref, late_ref, ext_ref, pad_ref)
    for a in range(3):
        image_ref[a * CY : (a + 1) * CY, :] = image[a]
    for edge_ref in edges:
        last = main_ref[pl.ds(CY - 1, 3 * K, stride=CY), :]
        edge_ref[0 : 3 * K, :] = jnp.where(side == 0, last, main_ref[pl.ds(0, 3 * K, stride=CY), :])
        edge_ref[3 * K :, :] = jnp.zeros((8, 128), F32)
        for a in range(3):
            row = 3 * K + a
            edge_ref[row : row + 1, :] = jnp.where(side == 0, image[a][CY - 1 : CY], image[a][0:1])
    for m in range(K):
        rows = [(a * K + m) * CY for a in range(3)]
        part_ref[m * CY : (m + 1) * CY, :] = sum(
            main_ref[row : row + CY, :] * image[a] for a, row in enumerate(rows)
        )
    others = [image] + [[ref[a * CY : (a + 1) * CY, :] for a in range(3)] for ref in vectors]
    for i in range(8):
        m = K + i
        if i < len(others):
            part_ref[m * CY : (m + 1) * CY, :] = sum(o * w for o, w in zip(others[i], image))
        else:
            part_ref[m * CY : (m + 1) * CY, :] = jnp.zeros((CY, 128), F32)
    part = sum(part_ref[pl.ds(y, K + 8, stride=CY), :] for y in range(CY))
    part = jnp.concatenate([part, jnp.zeros((128 - K - 8, 128), F32)], axis=0)
    send_ref[...] = exact_dot(jnp.ones((PEERS, 128), F32), part, NT)


def totals(got_ref):
    return exact_dot(got_ref[...], jnp.ones((PEERS, 128), F32), TN)


def next_kernel(got_ref, main_ref, image_ref, one_ref, other_ref, inv_ref, v_ref, weights_ref, h_ref):
    sums = totals(got_ref)
    weights = exact_dot(inv_ref[...], sums)
    h11 = sums[K + 1 : K + 2, :]
    along = jnp.sum(sums[0:K] * weights, axis=0, keepdims=True)
    h21 = jnp.sqrt(sums[K : K + 1, :] - along - h11 * h11)
    begin = [
        image_ref[a * CY : (a + 1) * CY, :] - h11 * one_ref[a * CY : (a + 1) * CY, :] for a in range(3)
    ]
    vector = [v / h21 for v in minus_combined(begin, main_ref, weights)]
    lines = []
    for a in range(3):
        along_line = jnp.sum(other_ref[a * K : (a + 1) * K, :] * weights, axis=0, keepdims=True)
        line = other_ref[3 * K + a : 3 * K + a + 1, :] - along_line - h11 * one_ref[24 + a : 25 + a, :]
        lines.append(line / h21)
    put_vector(vector, lines, v_ref)
    weights_ref[...] = weights
    h_ref[...] = jnp.zeros((8, 128), F32)
    h_ref[0:1, :] = h11
    h_ref[1:2, :] = h21


def send_kernel(got_ref, inv_ref, start_ref, first_ref, h_ref, beta_ref, u_ref, info_ref, wire_ref, y_ref):
    sums = totals(got_ref)
    weights = exact_dot(inv_ref[...], sums)
    h11, h21 = h_ref[0:1, :], h_ref[1:2, :]
    h12, h22 = sums[K + 1 : K + 2, :], sums[K + 2 : K + 3, :]
    along = jnp.sum(sums[0:K] * weights, axis=0, keepdims=True)
    h32 = jnp.sqrt(sums[K : K + 1, :] - along - h12 * h12 - h22 * h22)
    beta = beta_ref[0:1, :]
    m11 = h11 * h11 + h21 * h21
    m12 = h11 * h12 + h21 * h22
    m22 = h12 * h12 + h22 * h22 + h32 * h32
    g_one = beta * h11
    g_two = beta * h12
    determ = m11 * m22 - m12 * m12
    y_one = (m22 * g_one - m12 * g_two) / determ
    y_two = (m11 * g_two - m12 * g_one) / determ
    y_ref[...] = jnp.zeros((8, 128), F32)
    y_ref[0:1, :] = y_one
    y_ref[1:2, :] = y_two
    weights = start_ref[...] - y_one * first_ref[...] - y_two * weights
    wide = jnp.concatenate([weights] * (ROWS // 128), axis=1)
    target, rank, local = (info_ref[i : i + 1, :] for i in range(3))
    at_rank = lax.broadcasted_iota(jnp.int32, (SLOTS, ROWS), 0) == rank
    rows = [jnp.sum(u_ref[a * K : (a + 1) * K, :] * wide, axis=0, keepdims=True) for a in range(3)]
    rows = jnp.concatenate([jnp.where(at_rank, r, 0.0) for r in rows + [local.astype(F32)]], axis=0)
    rows = jnp.concatenate(split(rows), axis=0)
    onehot = lax.broadcasted_iota(jnp.int32, (PEERS, ROWS), 0) == target
    onehot = jnp.where(onehot, 1.0, 0.0).astype(BF16)
    mine = lax.dot_general(onehot, rows, NT, preferred_element_type=F32)
    mine = mine + pltpu.roll(mine, 64, 1)
    peer = lax.broadcasted_iota(jnp.int32, (PEERS, 128), 0)
    lane = lax.broadcasted_iota(jnp.int32, (PEERS, 128), 1)
    other = jnp.where(peer % 2 == 0, pltpu.roll(mine, PEERS - 1, 0), pltpu.roll(mine, 1, 0))
    pair = jnp.where(lane < 64, mine, other)
    wire_ref[pl.ds(0, PEERS, stride=3), :] = jnp.where(peer < 2, 0.0, pltpu.roll(pair, 2, 0))
    wire_ref[pl.ds(1, PEERS, stride=3), :] = pair
    wire_ref[pl.ds(2, PEERS, stride=3), :] = jnp.where(peer >= PEERS - 2, 0.0, pltpu.roll(pair, PEERS - 2, 0))


def last_kernel(
    place_ref, got_ref, main_ref, late_ref, ext_ref, y_ref, one_ref, two_ref, im_one_ref, im_two_ref,
    sol_hbm, res_hbm, left_ref, right_ref, pad_ref, sol_ref, res_ref, sem,
):
    side = place_ref[0:1, :]
    for dx in range(3):
        got = got_ref[pl.ds(dx, PEERS, stride=3), :].T
        own, other = two_level(
            [(got[base : base + 48], got[base + 48 : base + 64]) for base in (0, 64)],
            left_ref.at[dx],
            right_ref.at[dx],
        )
        lines = [
            jnp.where(side == 0, other[a * CY : a * CY + 1, :], other[a * CY + 7 : a * CY + 8, :]) for a in range(3)
        ]
        put_plane(pad_ref, dx, own, jnp.concatenate(lines, axis=0), side)
        if dx == 1:
            term = own
    y_one, y_two = y_ref[0:1, :], y_ref[1:2, :]
    solution = term + y_one * one_ref[0:24, :] + y_two * two_ref[0:24, :]
    for a in range(3):
        for y in range(CY):
            sol_ref[a : a + 1, y * CZ : (y + 1) * CZ] = solution[a * CY + y : a * CY + y + 1, :]
    first = pltpu.make_async_copy(sol_ref, sol_hbm, sem.at[0])
    first.start()
    image = stencil(main_ref, late_ref, ext_ref, pad_ref)
    for a in range(3):
        rows = slice(a * CY, (a + 1) * CY)
        residual = ext_ref[24 + a * CY : 24 + (a + 1) * CY, :] - image[a]
        residual = residual - y_one * im_one_ref[rows, :] - y_two * im_two_ref[rows, :]
        for y in range(CY):
            res_ref[a : a + 1, y * CZ : (y + 1) * CZ] = residual[y : y + 1, :]
    second = pltpu.make_async_copy(res_ref, res_hbm, sem.at[1])
    second.start()
    first.wait()
    second.wait()


def shape(*dims, dtype=F32):
    return jax.ShapeDtypeStruct(dims, dtype)


def specs(*spaces):
    return tuple(pl.BlockSpec(memory_space=space) for space in spaces)


def call(kernel, outs, scratch=(), inputs=0, in_specs=None, out_specs=None, limit=40, cost=None):
    vmem = pltpu.VMEM
    return pl.pallas_call(
        kernel,
        out_shape=outs,
        in_specs=in_specs or specs(*[vmem] * inputs),
        out_specs=out_specs or specs(*[vmem] * len(outs)),
        scratch_shapes=list(scratch),
        compiler_params=pltpu.CompilerParams(vmem_limit_bytes=limit * 2**20),
        cost_estimate=cost,
    )


def exchange(rows):
    count = rows.shape[0] // PEERS
    shaped = rows.reshape(PEERS, count, 1, 128)
    got = lax.all_to_all(shaped, GX_GY, split_axis=0, concat_axis=0, tiled=True)
    return got.reshape(PEERS * count, 128)


def swap(plane, first):
    pairs = [(i, i + 1) for i in range(first, N_GX - 1, 2)]
    return lax.ppermute(plane, GX, pairs + [(j, i) for i, j in pairs])


def other_core(x):
    return lax.ppermute(x, "gy", [(0, 1), (1, 0)])


def body(operator, basis_u, basis_c, right_side, new_rows):
    row = lax.broadcasted_iota(jnp.int32, (8, 128), 0)
    place = jnp.where(row == 0, lax.axis_index("gy"), lax.axis_index(GX) % 2).astype(jnp.int32)
    vmem, hbm = pltpu.VMEM, pltpu.HBM
    wire, info = call(
        pack_kernel,
        (shape(PEERS * WIRE, 128), shape(8, ROWS, dtype=jnp.int32)),
        [
            vmem((243, ROWS), F32),
            vmem((144, ROWS), F32),
            vmem((3, ROWS), F32),
            vmem((1, ROWS), jnp.int32),
            vmem((ROWS, 2 * MAIN), BF16),
            vmem((3, 64, ROWS), F32),
            vmem((56, 128), F32),
            vmem((PEERS * WIRE, 128), F32),
            vmem((8, ROWS), jnp.int32),
            pltpu.SemaphoreType.DMA((6,)),
            pltpu.SemaphoreType.DMA((CHUNKS + 1,)),
        ],
        in_specs=specs(hbm, hbm, hbm, hbm),
        out_specs=specs(hbm, hbm),
        limit=56,
    )(operator, basis_c, right_side, new_rows.reshape(1, ROWS))
    got = exchange(wire)
    got = got.reshape(PEERS, WIRE, 128).transpose(1, 0, 2)
    mine = jnp.sum(got[49:], axis=1)
    plane = shape(32, 128)
    main, ext, one, inverse, start, beta = call(
        unpack_kernel,
        (shape(2 * 128 * CY, 128), shape(48, 128), plane, shape(K, 128), shape(K, 128), shape(8, 128)),
        [
            vmem((ROWS, SLOTS * PEERS), BF16),
            vmem((2, SLOTS * PEERS, 256), BF16),
            vmem((48, SLOTS * PEERS), F32),
            vmem((128, SLOTS * PEERS), BF16),
            vmem((56, 128), F32),
        ],
        inputs=4,
    )(place, got, mine, other_core(mine))
    [late] = call(
        late_kernel,
        (shape(128 * CY, 128),),
        [vmem((ROWS, SLOTS * PEERS), BF16), vmem((SLOTS * PEERS, 256), BF16)],
        inputs=1,
        cost=pl.CostEstimate(flops=2 * ROWS * SLOTS * PEERS * 256, bytes_accessed=5 * 10**6, transcendentals=0),
    )(got)
    pad = vmem((9 * 24, 128), F32)
    image_scratch = [pad, vmem(((K + 8) * CY, 128), F32)]
    image_outs = (shape(3 * CY, 128), shape(PEERS, 128))
    one = lax.dynamic_update_slice(one, other_core(one[24:32]), (24, 0))
    image_one, send, edge = call(
        functools.partial(image_kernel, 1), (*image_outs, shape(3 * K + 8, 128)), image_scratch, inputs=7
    )(place, main, late, ext, swap(one, 0), swap(one, 1), one)
    other = other_core(edge)
    sums = exchange(send)
    two, weights, h_one = call(next_kernel, (plane, shape(K, 128), shape(8, 128)), inputs=6)(
        sums, main, image_one, one, other, inverse
    )
    image_two, send = call(functools.partial(image_kernel, 2), image_outs, image_scratch, inputs=8)(
        place, main, late, ext, swap(two, 0), swap(two, 1), one, two
    )
    sums = exchange(send)
    wire, y = call(send_kernel, (shape(PEERS * 3, 128), shape(8, 128)), inputs=8)(
        sums, inverse, start, weights, h_one, beta, basis_u, info
    )
    got = exchange(wire)
    return call(
        last_kernel,
        (shape(3, ROWS), shape(3, ROWS)),
        [
            vmem((3, 48, SLOTS * PEERS), F32),
            vmem((3, 256, SLOTS * PEERS), BF16),
            pad,
            vmem((3, ROWS), F32),
            vmem((3, ROWS), F32),
            pltpu.SemaphoreType.DMA((2,)),
        ],
        inputs=10,
        out_specs=specs(hbm, hbm),
    )(place, got, main, late, ext, y, one, two, image_one, image_two)


def solution(mesh):
    torus = Mesh(mesh.devices.reshape(4, 4, 4, mesh.shape["gy"]), ("gx_0", "gx_1", "gx_2", "gy"))
    placed = (P(None, GX_GY), P(None, GX_GY), P(None, GX_GY), P(None, GX_GY), P(GX_GY))
    return jax.shard_map(
        body,
        mesh=torus,
        in_specs=placed,
        out_specs=(P(None, GX_GY), P(None, GX_GY)),
        check_vma=False,
    )
```
